32 devices in a mesh: dp: 8 (over y, x, core), mp: 4 (over z).
Axes of the slice: x: 2, y: 2, z: 4, core: 2. Of those that a mesh axis runs over, the one named last changes fastest.
Arguments:
- hidden_in: bfloat16 [6144, 768], P(('dp', 'mp')), may hold values from -6 to 6
- text_lens: int32 [8], P('dp'), may hold values from 1 to 512, as said below
- key_mask: int32 [6144], P('dp'), may hold values 0 or 1
- bucket_x: int32 [8, 768, 768], P('dp'), may hold values from 0 to 63
- bucket_y: int32 [8, 768, 768], P('dp'), may hold values from 0 to 63
- w_qkv: bfloat16 [3, 768, 768], P(None, None, 'mp'), may hold values from -0.21875 to 0.21875
- b_q: bfloat16 [768], P('mp'), may hold values from -1.75 to 1.75
- b_v: bfloat16 [768], P('mp'), may hold values from -1.75 to 1.75
- w_out: bfloat16 [768, 768], P('mp'), may hold values from -0.875 to 0.875
- b_out: bfloat16 [768], replicated, may hold values from -1.75 to 1.75
- g_attn: float32 [768], replicated, may hold values from 0.5 to 1.5
- n_attn: float32 [768], replicated, may hold values from -1.75 to 1.75
- w_up: bfloat16 [768, 3072], P(None, 'mp'), may hold values from -0.21875 to 0.21875
- b_up: bfloat16 [3072], P('mp'), may hold values from -1.75 to 1.75
- w_down: bfloat16 [3072, 768], P('mp'), may hold values from -0.109375 to 0.109375
- b_down: bfloat16 [768], replicated, may hold values from -1.75 to 1.75
- g_ffn: float32 [768], replicated, may hold values from 0.5 to 1.5
- n_ffn: float32 [768], replicated, may hold values from -1.75 to 1.75
- t_pos: bfloat16 [12, 32], P('mp'), may hold values from -48 to 48
- t_x: bfloat16 [12, 64], P('mp'), may hold values from -48 to 48
- t_y: bfloat16 [12, 64], P('mp'), may hold values from -48 to 48
- cotangent: bfloat16 [6144, 768], P(('dp', 'mp')), may hold values from -6 to 6
Outputs:
- layer_out: bfloat16 [6144, 768], P(('dp', 'mp'))
- input_grad: bfloat16 [6144, 768], P(('dp', 'mp'))
- grad_w_qkv: float32 [3, 768, 768], P(None, None, 'mp')
- grad_b_q: float32 [768], P('mp')
- grad_b_v: float32 [768], P('mp')
- grad_w_out: float32 [768, 768], P('mp')
- grad_b_out: float32 [768], replicated
- grad_g_attn: float32 [768], replicated
- grad_n_attn: float32 [768], replicated
- grad_w_up: float32 [768, 3072], P(None, 'mp')
- grad_b_up: float32 [3072], P('mp')
- grad_w_down: float32 [3072, 768], P('mp')
- grad_b_down: float32 [768], replicated
- grad_g_ffn: float32 [768], replicated
- grad_n_ffn: float32 [768], replicated
- grad_t_pos: float32 [12, 32], P('mp')
- grad_t_x: float32 [12, 64], P('mp')
- grad_t_y: float32 [12, 64], P('mp')
The draws below stay inside these ranges and needn't reach their ends.
Inputs may be any that keep to these rules, and one draw needn't show every extreme that they name: `text_lens`: some document has exactly 512 text tokens.
All inputs are finite; a program needn't handle non-finite values. No bound on the sum of `key_mask` on one device may be relied on, other than what follows from the above.
Results may differ from the reference program's by a relative error of at most 0.015.
Values may be sent and summed in bfloat16 or wider, within the bound.
A program may use at most 128 MiB of HBM per device.

```python
import jax
import jax.numpy as jnp
from jax import lax

D = 768
HEADS = 12
HEAD_DIM = 64
FF = 3072
BINS_1D = 32
BINS_2D = 64
PATCHES = 196
TEXT_MAX = 512
SLOT = 768
DOCS = 8
TOKENS = 6144


def draw_text_lens(key, part):
    key_shift, key_raw, key_pick = jax.random.split(jax.random.fold_in(key, 11), 3)
    halving = jax.random.randint(key_shift, (DOCS,), 0, 2)
    ceiling = TEXT_MAX // (1 + halving)
    raw_lens = 1 + jax.random.randint(key_raw, (DOCS,), 0, ceiling)
    chosen = jax.random.randint(key_pick, (), 0, DOCS)
    return jnp.where(jnp.arange(DOCS) == chosen, TEXT_MAX, raw_lens).astype(jnp.int32)


def plant(values, stream_key, smallest, largest):
    longest = values.shape.index(max(values.shape))
    spots = []
    for shift in (0, 1):
        where = [jax.random.randint(jax.random.fold_in(stream_key, axis), (), 0, length) for axis, length in enumerate(values.shape)]
        where[longest] = (where[longest] + shift) % values.shape[longest]
        spots.append(tuple(where))
    return values.at[spots[0]].set(smallest).at[spots[1]].set(largest)


def shard_levels(stream_key, dims, pieces, low, top_value):
    loudness, own = 1.0, jax.random.fold_in(stream_key, 6)
    for axis_at, shards_of in pieces:
        draws = jnp.exp(jax.random.uniform(jax.random.fold_in(own, axis_at), (shards_of,), jnp.float32, low / len(pieces), top_value / len(pieces)))
        loudness = loudness * jnp.repeat(draws, dims[axis_at] // shards_of).reshape([-1 if axis == axis_at else 1 for axis in range(len(dims))])
    return loudness


def centred(key, extent, scale, most, pieces=(), kind=jnp.bfloat16):
    array = scale * jax.random.normal(key, extent, jnp.float32)
    if pieces:
        array = array * shard_levels(key, extent, pieces, -0.22, 0.18)
    return jnp.clip(array, -most, most).astype(kind)


def setup_inputs(seed: int = 0) -> dict:
    key_of = jax.random.split(jax.random.key(seed), 23)
    return {
        "hidden_in": centred(key_of[0], (TOKENS, D), 1.0, 6.0, ((0, 32),)),
        "text_lens": draw_text_lens(jax.random.fold_in(key_of[22], 71), 0),
        "key_mask": plant((jax.random.randint(key_of[2], (TOKENS,), 0, 8) < 7).astype(jnp.int32), jax.random.fold_in(key_of[2], 1), 0, 1),
        "bucket_x": plant(jax.random.randint(key_of[3], (DOCS, SLOT, SLOT), 0, BINS_2D), jax.random.fold_in(key_of[3], 1), 0, BINS_2D - 1).astype(jnp.int32),
        "bucket_y": plant(jax.random.randint(key_of[4], (DOCS, SLOT, SLOT), 0, BINS_2D), jax.random.fold_in(key_of[4], 1), 0, BINS_2D - 1).astype(jnp.int32),
        "w_qkv": centred(key_of[5], (3, D, D), D ** -0.5, 0.21875, ((2, 4),)),
        "b_q": centred(key_of[6], (D,), 0.3, 1.75, ((0, 4),)),
        "b_v": centred(key_of[7], (D,), 0.3, 1.75, ((0, 4),)),
        "w_out": centred(key_of[8], (D, D), (D // 16) ** -0.5, 0.875, ((0, 4),)),
        "b_out": centred(key_of[9], (D,), 0.3, 1.75),
        "g_attn": jnp.clip(1.0 + 0.1 * jax.random.normal(key_of[10], (D,), jnp.float32), 0.5, 1.5),
        "n_attn": centred(key_of[11], (D,), 0.3, 1.75, (), jnp.float32),
        "w_up": centred(key_of[12], (D, FF), D ** -0.5, 0.21875, ((1, 4),)),
        "b_up": centred(key_of[13], (FF,), 0.3, 1.75, ((0, 4),)),
        "w_down": centred(key_of[14], (FF, D), FF ** -0.5, 0.109375, ((0, 4),)),
        "b_down": centred(key_of[15], (D,), 0.3, 1.75),
        "g_ffn": jnp.clip(1.0 + 0.1 * jax.random.normal(key_of[16], (D,), jnp.float32), 0.5, 1.5),
        "n_ffn": centred(key_of[17], (D,), 0.3, 1.75, (), jnp.float32),
        "t_pos": centred(key_of[18], (HEADS, BINS_1D), 8.0, 48.0, ((0, 4),)),
        "t_x": centred(key_of[19], (HEADS, BINS_2D), 8.0, 48.0, ((0, 4),)),
        "t_y": centred(key_of[20], (HEADS, BINS_2D), 8.0, 48.0, ((0, 4),)),
        "cotangent": centred(key_of[21], (TOKENS, D), 1.0, 6.0, ((0, 32),)),
    }


@jax.custom_vjp
def low(v):
    return lax.optimization_barrier(v.astype(jnp.bfloat16)).astype(jnp.float32)

@jax.custom_vjp
def low_back(v):
    return v

def low_keep(v):
    return (low(v), None)

def low_pass(kept, grad):
    return (grad,)

def back_keep(v):
    return (v, None)

def back_low(kept, grad):
    return (low(grad),)
low.defvjp(low_keep, low_pass)
low_back.defvjp(back_keep, back_low)
HIGHEST = lax.Precision.HIGHEST
THRESHOLDS = (12, 16, 23, 32, 46, 64, 91)

def relative_bucket(slot_len):
    places = jnp.arange(slot_len, dtype=jnp.int32)
    offset = places[None, :] - places[:, None]
    magnitude = jnp.abs(offset)
    far_part = jnp.full(offset.shape, 8, jnp.int32)
    for border in THRESHOLDS:
        far_part = far_part + (magnitude >= border).astype(jnp.int32)
    near_part = jnp.where(magnitude < 8, magnitude, far_part)
    return jnp.where(offset > 0, 16, 0).astype(jnp.int32) + near_part

def layer_norm(values, norm_gain, norm_shift):
    center = lax.optimization_barrier(jnp.mean(values, axis=-1, keepdims=True))
    spread = values - center
    varied = lax.optimization_barrier(jnp.mean(spread * spread, axis=-1, keepdims=True))
    return spread * lax.rsqrt(varied + 1e-05) * norm_gain + norm_shift

def doc_forward(params, inputs, plane_x, plane_y, key_valid, line_bucket):
    w_qkv, b_q, b_v, w_out, b_out, g_attn, n_attn, w_up, b_up, w_down, b_down, g_ffn, n_ffn, t_pos, t_x, t_y = params
    slot_len = inputs.shape[0]
    mixed = jnp.einsum('td,cde->cte', inputs, w_qkv, precision=HIGHEST)
    query = low(low_back(mixed[0] + b_q)).reshape(slot_len, HEADS, HEAD_DIM)
    keys_all = low(low_back(mixed[1])).reshape(slot_len, HEADS, HEAD_DIM)
    values_all = low(low_back(mixed[2] + b_v)).reshape(slot_len, HEADS, HEAD_DIM)
    score_scale = HEAD_DIM ** (-0.5)
    bias = (t_pos[:, line_bucket] + t_x[:, plane_x] + t_y[:, plane_y]) * score_scale
    scores = low_back(jnp.einsum('ihd,jhd->hij', query, keys_all, precision=HIGHEST) * score_scale + bias)
    masked = jnp.where(key_valid[None, None, :], scores, -1e+30)
    probs = jax.nn.softmax(masked, axis=-1)
    context = jnp.einsum('hij,jhd->ihd', low(probs), values_all, precision=HIGHEST)
    context = low(low_back(context)).reshape(slot_len, D)
    attn = low_back(jnp.dot(context, w_out, precision=HIGHEST)) + b_out
    normed = layer_norm(inputs + attn, g_attn, n_attn)
    pre_act = low_back(jnp.dot(low(normed), w_up, precision=HIGHEST) + b_up)
    act = low(jax.nn.gelu(pre_act, approximate=False))
    branch = low_back(jnp.dot(act, w_down, precision=HIGHEST)) + b_down
    return layer_norm(normed + branch, g_ffn, n_ffn)

def add_pair(first, second):
    return first + second

def reference(hidden_in, text_lens, key_mask, bucket_x, bucket_y, w_qkv, b_q, b_v, w_out, b_out, g_attn, n_attn, w_up, b_up, w_down, b_down, g_ffn, n_ffn, t_pos, t_x, t_y, cotangent):
    params = tuple((item.astype(jnp.float32) for item in (w_qkv, b_q, b_v, w_out, b_out, g_attn, n_attn, w_up, b_up, w_down, b_down, g_ffn, n_ffn, t_pos, t_x, t_y)))
    line_bucket = relative_bucket(SLOT)
    places = jnp.arange(SLOT, dtype=jnp.int32)
    doc_length = 1 + PATCHES + text_lens
    row_valid = places[None, :] < doc_length[:, None]
    key_valid = row_valid & ((key_mask.reshape(DOCS, SLOT) == 1) | (places[None, :] == 0))
    inputs = hidden_in.astype(jnp.float32).reshape(DOCS, SLOT, D)
    grads_in = cotangent.astype(jnp.float32).reshape(DOCS, SLOT, D) * row_valid[:, :, None].astype(jnp.float32)

    def one_doc(totals, item):
        doc_in, doc_grad, plane_x, plane_y, doc_keys = item

        def forward(param_set, doc_rows):
            return doc_forward(param_set, doc_rows, plane_x, plane_y, doc_keys, line_bucket)
        result, pull_back = jax.vjp(forward, params, doc_in)
        param_grads, input_part = pull_back(doc_grad)
        return (jax.tree.map(add_pair, totals, param_grads), (result, input_part))
    zeros_init = jax.tree.map(jnp.zeros_like, params)
    totals, (results, input_parts) = lax.scan(one_doc, zeros_init, (inputs, grads_in, bucket_x, bucket_y, key_valid))
    g_wqkv, g_bq, g_bv, g_wout, g_bout, g_gattn, g_nattn, g_wup, g_bup, g_wdown, g_bdown, g_gffn, g_nffn, g_tpos, g_tx, g_ty = totals
    return (results.reshape(TOKENS, D).astype(jnp.bfloat16), input_parts.reshape(TOKENS, D).astype(jnp.bfloat16), g_wqkv, g_bq, g_bv, g_wout, g_bout, g_gattn, g_nattn, g_wup, g_bup, g_wdown, g_bdown, g_gffn, g_nffn, g_tpos, g_tx, g_ty)
```

```python
import functools
import jax
import jax.numpy as jnp
from jax import lax
from jax.experimental import pallas as pl
from jax.experimental.pallas import tpu as pltpu
from jax.sharding import PartitionSpec as P

HEAD_DIM = 64
PATCHES = 196
THRESHOLDS = (12, 16, 23, 32, 46, 64, 91)
TILE = 128
F32, BF16 = jnp.float32, jnp.bfloat16
MESH = pl.DeviceIdType.MESH
VMEM = pl.BlockSpec(memory_space=pltpu.VMEM)
ANY = pl.BlockSpec(memory_space=pl.ANY)
BIG = 58 << 20


def line_bucket(off):
    mag = jnp.abs(off)
    far = jnp.full(off.shape, 8, jnp.int32)
    for border in THRESHOLDS:
        far = far + (mag >= border).astype(jnp.int32)
    return jnp.where(off > 0, 16, 0) + jnp.where(mag < 8, mag, far)


def dot(a, b, ca, cb):
    return lax.dot_general(a, b, (((ca,), (cb,)), ((), ())), preferred_element_type=F32)


def flip(index, bit):
    step = 2**bit
    return index + step * (1 - 2 * ((index // step) % 2))


def gather_plan(dp_size, reverse):
    bits = list(range(1, dp_size.bit_length() - 1))
    return (bits[::-1] if reverse else bits) + [0]


def plan_label(index, plan):
    label = 0
    for place, bit in enumerate(plan):
        label = label + ((index // 2**bit) % 2) * 2**place
    return label


def front_kernel(
    n_mp, n_dp, plans,
    x_ref, w_ref, bq_ref, bv_ref, bx_hbm, by_hbm, tx_ref, ty_ref, tp_ref, len_ref, km_ref, wo_src, wu_src, wd_src,
    xf_ref, q_ref, k_ref, v_ref, e_ref, inv_ref, cr_ref, wo_out, wu_out, wd_out,
    bx_ref, by_ref, bias_ref, line_ref, cs_ref,
    b_sem, x_send, x_recv, c_send, c_recv, own_sem, z_send, z_recv, p_send, p_recv,
):
    d = lax.axis_index("dp")
    z = lax.axis_index("mp")
    rows = x_ref.shape[0]
    slot = bx_ref.shape[0]
    width = w_ref.shape[2]
    heads = width // HEAD_DIM
    tiles = slot // TILE
    scale = HEAD_DIM**-0.5
    sources = (wo_src, wu_src, wd_src)
    gathered = (wo_out, wu_out, wd_out)

    loads = []
    for c in range(tiles):
        part = pl.ds(c * TILE, TILE)
        pair = (
            pltpu.make_async_copy(bx_hbm.at[part], bx_ref.at[part], b_sem.at[0, c]),
            pltpu.make_async_copy(by_hbm.at[part], by_ref.at[part], b_sem.at[1, c]),
        )
        for copy in pair:
            copy.start()
        loads.append(pair)

    barrier = pltpu.get_barrier_semaphore()
    peers = [(d, (z + k) % n_mp) for k in range(1, n_mp)] + [(flip(d, bit), z) for bit in plans[0]]
    for peer in peers:
        pl.semaphore_signal(barrier, inc=1, device_id=peer, device_id_type=MESH)
    xf_ref[z] = x_ref[...]
    pl.semaphore_wait(barrier, len(peers))

    def hop(block, to, sem):
        return pltpu.make_async_remote_copy(
            xf_ref.at[block], xf_ref.at[block], x_send.at[sem], x_recv.at[block], device_id=(d, to), device_id_type=MESH
        )

    def x_step(step, act):
        low, high = z - step, z + step
        if step == 0:
            @pl.when(z < n_mp - 1)
            def _():
                act(hop(z, z + 1, z))

            @pl.when(z > 0)
            def _():
                act(hop(z, z - 1, n_mp))

            return

        @pl.when(jnp.logical_and(low >= 0, z < n_mp - 1))
        def _():
            act(hop(low, z + 1, low))

        @pl.when(jnp.logical_and(high < n_mp, z > 0))
        def _():
            act(hop(high, z - 1, high))

    def x_arrived(step):
        low, high = z - step, z + step

        @pl.when(low >= 0)
        def _():
            hop(low, z, low).wait_recv()

        @pl.when(high < n_mp)
        def _():
            hop(high, z, high).wait_recv()

    x_step(0, lambda c: c.start())

    labels = [plan_label(d, plan) for plan in plans]

    def z_copy(w, to, shard):
        label = labels[w]
        return pltpu.make_async_remote_copy(
            sources[w].at[label], gathered[w].at[shard, label], z_send.at[w, to], z_recv.at[w, shard],
            device_id=(d, to), device_id_type=MESH,
        )

    def own_copy(w):
        return pltpu.make_async_copy(sources[w], gathered[w].at[z], own_sem.at[w])

    def plane_copy(w, place, shard, incoming):
        size = 2**place
        base = (labels[w] // size) * size
        if incoming:
            base = flip(base, place)
        part = gathered[w].at[shard, pl.ds(base, size)]
        return pltpu.make_async_remote_copy(
            part, part, p_send.at[w, place, shard], p_recv.at[w, place, shard],
            device_id=(flip(d, plans[w][place]), z), device_id_type=MESH,
        )

    others = [(z + k) % n_mp for k in range(1, n_mp)]
    depth = len(plans[0])
    for w in range(3):
        for to in others:
            z_copy(w, to, z).start()
    for w in range(3):
        own_copy(w).start()

    def plane_start(w, place):
        for shard in others:
            if place == 0:
                z_copy(w, shard, shard).wait_recv()
            else:
                plane_copy(w, place - 1, shard, True).wait_recv()
            plane_copy(w, place, shard, False).start()

    tab = [
        jnp.broadcast_to(
            jnp.concatenate([tx_ref[h : h + 1, :].astype(F32), ty_ref[h : h + 1, :].astype(F32)], axis=1) * scale, (8, TILE)
        )
        for h in range(heads)
    ]
    bins_x = tx_ref.shape[1]
    pad = jnp.zeros((1, TILE - tp_ref.shape[1]), F32)
    ltab = [
        jnp.broadcast_to(jnp.concatenate([tp_ref[h : h + 1, :].astype(F32) * scale, pad], axis=1), (8, TILE))
        for h in range(heads)
    ]
    ci = lax.broadcasted_iota(jnp.int32, (8, TILE), 1)
    ri = lax.broadcasted_iota(jnp.int32, (8, TILE), 0)

    @pl.loop(0, TILE // 8)
    def _(g):
        at = pl.ds(pl.multiple_of(g * 8, 8), 8)
        for off in range(5):
            idx = line_bucket(ci - ri - g * 8 + (off - 2) * TILE)
            for h in range(heads):
                line_ref[h, off, at, :] = jnp.take_along_axis(ltab[h], idx, axis=1)

    place_ids = lax.broadcasted_iota(jnp.int32, (1, slot), 1)
    live = place_ids < 1 + PATCHES + len_ref[0]
    seen = jnp.where(live & ((km_ref[...] == 1) | (place_ids == 0)), 0.0, -1e30)

    def bias_chunk(c):
        for copy in loads[c]:
            copy.wait()

        @pl.loop(0, TILE // 8)
        def _(g):
            at = pl.ds(pl.multiple_of(c * TILE + g * 8, 8), 8)
            near = pl.ds(pl.multiple_of(g * 8, 8), 8)
            for j in range(tiles):
                cols = slice(j * TILE, (j + 1) * TILE)
                ix = bx_ref[at, cols]
                iy = by_ref[at, cols] + bins_x
                hide = seen[:, cols]
                off = min(max(j - c + 2, 0), 4)
                for h in range(heads):
                    b = jnp.take_along_axis(tab[h], ix, axis=1) + jnp.take_along_axis(tab[h], iy, axis=1)
                    bias_ref[h, at, cols] = (b + line_ref[h, off, near, :]) + hide

    for c in range(tiles):
        if c == tiles - 2:
            x_arrived(1)
            x_step(1, lambda copy: copy.start())
        bias_chunk(c)
    x_arrived(2)
    x_step(2, lambda copy: copy.start())
    plane_start(0, 0)
    x_arrived(3)

    lane = lax.broadcasted_iota(jnp.int32, (1, width), 1)
    mine = [(lane >= h * HEAD_DIM) & (lane < (h + 1) * HEAD_DIM) for h in range(heads)]
    for b in range(n_mp):
        at = pl.ds(b * rows, rows)
        xb = xf_ref[b]
        q_ref[at, :] = ((dot(xb, w_ref[0], 1, 0) + bq_ref[...].astype(F32)).astype(BF16).astype(F32) * scale).astype(BF16)
        k_ref[at, :] = dot(xb, w_ref[1], 1, 0).astype(BF16)
        v_ref[at, :] = (dot(xb, w_ref[2], 1, 0) + bv_ref[...].astype(F32)).astype(BF16)

    def c_copy(turn, to, source):
        return pltpu.make_async_remote_copy(
            cs_ref.at[turn], cr_ref.at[source], c_send.at[turn], c_recv.at[source], device_id=(d, to), device_id_type=MESH
        )

    def attend(turn):
        to = (z + 1 + turn) % n_mp
        at = pl.ds(pl.multiple_of(to * rows, rows), rows)
        q = q_ref[at, :]
        out = jnp.zeros((rows, width), F32)
        for h in range(heads):
            s = dot(jnp.where(mine[h], q, jnp.zeros((), BF16)), k_ref[...], 1, 1) + bias_ref[h, at, :]
            top = jnp.max(s, axis=1, keepdims=True)
            e = jnp.exp(s - top).astype(BF16)
            e_ref[h, at, :] = e
            inv = 1.0 / jnp.sum(e.astype(F32), axis=1, keepdims=True)
            inv_ref[at, h : h + 1] = inv
            out = out + jnp.where(mine[h], dot(e, v_ref[...], 1, 0) * inv, 0.0)
        return to, out.astype(BF16)

    @pl.loop(0, n_mp - 1)
    def _(turn):
        to, out = attend(turn)
        cs_ref[turn] = out
        c_copy(turn, to, z).start()

    cr_ref[z] = attend(n_mp - 1)[1]

    plane_start(0, 1)
    for w in (1, 2):
        plane_start(w, 0)
    for place in range(2, depth):
        plane_start(0, place)
    for place in range(1, depth):
        for w in (1, 2):
            plane_start(w, place)
    for shard in others:
        for w in range(3):
            plane_copy(w, depth - 1, shard, True).wait_recv()

    for turn in range(n_mp - 1):
        c_copy(turn, z, others[turn]).wait_recv()
    for turn in range(n_mp - 1):
        c_copy(turn, z, z).wait_send()
    for step in range(n_mp - 1):
        x_step(step, lambda copy: copy.wait_send())
    for w in range(3):
        own_copy(w).wait()
        for to in others:
            z_copy(w, to, z).wait_send()
            for place in range(depth):
                plane_copy(w, place, to, False).wait_send()


def front(n_mp, n_dp, x, w_qkv, b_q, b_v, bx, by, t_x, t_y, t_pos, text_lens, key_mask, w_out, w_up, w_down):
    rows, wide = x.shape
    slot = bx.shape[0]
    width = w_qkv.shape[2]
    heads = width // HEAD_DIM
    plans = [gather_plan(n_dp, False), gather_plan(n_dp, False), gather_plan(n_dp, True)]
    depth = len(plans[0])
    slices = [w.reshape(n_dp, w.shape[0] // n_dp, w.shape[1]) for w in (w_out, w_up, w_down)]
    sds = jax.ShapeDtypeStruct
    dma = pltpu.SemaphoreType.DMA
    return pl.pallas_call(
        functools.partial(front_kernel, n_mp, n_dp, plans),
        out_shape=[
            sds((n_mp, rows, wide), BF16), sds((slot, width), BF16), sds((slot, width), BF16), sds((slot, width), BF16),
            sds((heads, slot, slot), BF16), sds((slot, heads), F32), sds((n_mp, rows, width), BF16),
        ] + [sds((n_mp,) + s.shape, BF16) for s in slices],
        in_specs=[VMEM, VMEM, VMEM, VMEM, ANY, ANY, VMEM, VMEM, VMEM, pl.BlockSpec(memory_space=pltpu.SMEM), VMEM, ANY, ANY, ANY],
        out_specs=[VMEM] * 7 + [ANY] * 3,
        scratch_shapes=[
            pltpu.VMEM((slot, slot), jnp.int32), pltpu.VMEM((slot, slot), jnp.int32), pltpu.VMEM((heads, slot, slot), F32),
            pltpu.VMEM((heads, 5, TILE, TILE), F32), pltpu.VMEM((n_mp - 1, rows, width), BF16),
            dma((2, slot // TILE)), dma((n_mp + 1,)), dma((n_mp,)), dma((n_mp - 1,)), dma((n_mp,)), dma((3,)),
            dma((3, n_mp)), dma((3, n_mp)), dma((3, depth, n_mp)), dma((3, depth, n_mp)),
        ],
        compiler_params=pltpu.CompilerParams(collective_id=0, has_side_effects=True, vmem_limit_bytes=BIG),
        name="front",
    )(x, w_qkv, b_q.reshape(1, -1), b_v.reshape(1, -1), bx, by, t_x, t_y, t_pos, text_lens, key_mask.reshape(1, -1), *slices)

HI, LO, GROUP, STEP = 4, 16, 16, 2


def back_kernel(
    n_mp,
    g_ref, q_ref, k_ref, v_ref, e_ref, inv_ref, w_ref, xf_ref, da_ref, bx_hbm, by_hbm,
    dx_ref, gw_ref, gb_ref, gt_ref, gl_ref,
    dc_ref, ds_ref, dt_ref, dn_ref, acc_ref, near_ref, part_ref, got_ref, bx_ref, by_ref,
    b_sem, d_send, d_recv, r_send, r_recv,
):
    d = lax.axis_index("dp")
    z = lax.axis_index("mp")
    heads, slot, _ = e_ref.shape
    width = k_ref.shape[1]
    rows = da_ref.shape[0]
    tiles = slot // TILE
    scale = HEAD_DIM**-0.5
    others = [(z + k) % n_mp for k in range(1, n_mp)]

    loads = [pltpu.make_async_copy(bx_hbm, bx_ref, b_sem.at[0]), pltpu.make_async_copy(by_hbm, by_ref, b_sem.at[1])]
    for copy in loads:
        copy.start()
    barrier = pltpu.get_barrier_semaphore()
    for to in others:
        pl.semaphore_signal(barrier, inc=1, device_id=(d, to), device_id_type=MESH)
    pl.semaphore_wait(barrier, n_mp - 1)

    def d_copy(to, source):
        return pltpu.make_async_remote_copy(
            g_ref.at[to], dc_ref.at[source], d_send.at[to], d_recv.at[source], device_id=(d, to), device_id_type=MESH
        )

    for to in others:
        d_copy(to, z).start()
    dc_ref[z] = g_ref[z]

    lane = lax.broadcasted_iota(jnp.int32, (1, width), 1)
    mine = [(lane >= h * HEAD_DIM) & (lane < (h + 1) * HEAD_DIM) for h in range(heads)]
    zero = jnp.zeros((), BF16)
    factor = jnp.zeros((slot, width), F32)
    for h in range(heads):
        factor = jnp.where(mine[h], inv_ref[:, h : h + 1], factor)
    qt = q_ref[...].astype(F32).T.astype(BF16)
    for source in others:
        d_copy(source, source).wait_recv()

    dctx = dc_ref[...].reshape(slot, width)
    gt = (dctx.astype(F32) * factor).T.astype(BF16)
    block = 384
    dq = [None] * (slot // block)
    for h in range(heads):
        hs = slice(h * HEAD_DIM, (h + 1) * HEAD_DIM)
        dk = dv = None
        for r in range(slot // block):
            rs = slice(r * block, (r + 1) * block)
            e = e_ref[h, rs, :]
            p = e.astype(F32) * inv_ref[rs, h : h + 1]
            dp = dot(jnp.where(mine[h], dctx[rs, :], zero), v_ref[...], 1, 1)
            ds = (p * (dp - jnp.sum(p * dp, axis=1, keepdims=True))).astype(BF16)
            ds_ref[h, rs, :] = ds
            a = jnp.where(mine[h], dot(ds, k_ref[...], 1, 0), 0.0)
            dq[r] = a if dq[r] is None else dq[r] + a
            b = dot(qt[hs, rs], ds, 1, 0)
            dk = b if dk is None else dk + b
            c = dot(gt[hs, rs], e, 1, 0)
            dv = c if dv is None else dv + c
        dt_ref[1, hs, :] = dk.astype(BF16)
        dt_ref[2, hs, :] = dv.astype(BF16)
    for r in range(slot // block):
        rs = slice(r * block, (r + 1) * block)
        low = (dq[r] * scale).astype(BF16)
        dn_ref[0, rs, :] = low
        dt_ref[0, :, rs] = low.astype(F32).T.astype(BF16)
    for c in (1, 2):
        dn_ref[c] = dt_ref[c].astype(F32).T.astype(BF16)

    def r_copy(turn, to, source):
        return pltpu.make_async_remote_copy(
            part_ref.at[turn], got_ref.at[source], r_send.at[turn], r_recv.at[source], device_id=(d, to), device_id_type=MESH
        )

    def dx_part(to):
        at = pl.ds(pl.multiple_of(to * rows, rows), rows)
        out = dot(dn_ref[0, at, :], w_ref[0], 1, 1)
        for c in (1, 2):
            out = out + dot(dn_ref[c, at, :], w_ref[c], 1, 1)
        return out

    for turn in range(n_mp - 1):
        part_ref[turn] = dx_part(others[turn]).astype(BF16)
        r_copy(turn, others[turn], z).start()
    da_ref_sum = da_ref[...] + dx_part(z)

    ones = jnp.ones((8, slot), BF16)
    xf = xf_ref[...].reshape(slot, xf_ref.shape[2])
    for c in range(3):
        gw_ref[c] = dot(dt_ref[c], xf, 1, 0)
        gb_ref[c] = dot(ones, dn_ref[c], 1, 0)

    for copy in loads:
        copy.wait()
    acc_ref[...] = jnp.zeros_like(acc_ref)
    one = jnp.ones((), BF16)

    @pl.loop(0, slot // (GROUP * STEP))
    def _(i):
        at = [pl.ds(pl.multiple_of(i * GROUP * STEP + g * GROUP, GROUP), GROUP) for g in range(STEP)]
        ds = [[ds_ref[h, at[g], :] for h in range(heads)] for g in range(STEP)]
        for t, b_ref in enumerate((bx_ref, by_ref)):
            tot = None
            for g in range(STEP):
                b = b_ref[at[g], :]
                hi = (b >> 4).astype(F32).astype(BF16)
                lo = (b & 15).astype(F32).astype(BF16)
                left = []
                for a in range(HI):
                    m = hi == jnp.asarray(a, BF16)
                    left += [jnp.where(m, ds[g][h], zero) for h in range(heads)]
                right = [jnp.where(lo == jnp.asarray(c, BF16), one, zero) for c in range(LO)]
                o = dot(jnp.concatenate(left, 0), jnp.concatenate(right, 0), 1, 1)
                tot = o if tot is None else tot + o
            acc_ref[t] += tot

    m, n = HI * heads * GROUP, LO * GROUP
    same = (lax.broadcasted_iota(jnp.int32, (m, n), 0) & (GROUP - 1)) == (lax.broadcasted_iota(jnp.int32, (m, n), 1) & (GROUP - 1))
    pick = (lax.broadcasted_iota(jnp.int32, (n, LO), 0) // GROUP == lax.broadcasted_iota(jnp.int32, (n, LO), 1)).astype(F32)
    for t in range(2):
        kept = jnp.sum(jnp.where(same, acc_ref[t], 0.0).reshape(m // GROUP, GROUP, n), axis=1)
        gt_ref[t] = lax.dot_general(
            kept, pick, (((1,), (0,)), ((), ())), precision=lax.Precision.HIGHEST, preferred_element_type=F32
        ) * scale

    for h in range(heads):
        for off in range(5):
            tot = jnp.zeros((TILE, TILE), F32)
            for i in range(tiles):
                for j in range(tiles):
                    if min(max(j - i, -2), 2) + 2 == off:
                        tot = tot + ds_ref[h, i * TILE : (i + 1) * TILE, j * TILE : (j + 1) * TILE].astype(F32)
            near_ref[h, off] = tot
    ci = lax.broadcasted_iota(jnp.int32, (TILE, TILE), 1)
    ri = lax.broadcasted_iota(jnp.int32, (TILE, TILE), 0)
    bins = gl_ref.shape[1]
    half = bins // 2
    ids = [line_bucket(ci - ri + (off - 2) * TILE) for off in range(5)]
    for h in range(heads):
        found = []
        for b in range(bins):
            tot = None
            for off in range(5):
                if off in (1, 2, 3) and (off == 2 or (b >= half) == (off == 3)):
                    piece = jnp.where(ids[off] == b, near_ref[h, off], 0.0)
                elif off == 0 and b == half - 1 or off == 4 and b == bins - 1:
                    piece = near_ref[h, off]
                else:
                    continue
                tot = piece if tot is None else tot + piece
            found.append(jnp.sum(tot, axis=0, keepdims=True))
        gl_ref[h] = jnp.sum(jnp.concatenate(found, 0), axis=1, keepdims=True) * scale

    for source in others:
        r_copy(0, z, source).wait_recv()
        da_ref_sum = da_ref_sum + got_ref[source].astype(F32)
    dx_ref[...] = da_ref_sum.astype(BF16)
    for turn in range(n_mp - 1):
        r_copy(turn, z, z).wait_send()
    for to in others:
        d_copy(to, z).wait_send()


def back(n_mp, dctx, q, k, v, e, inv, w_qkv, xf, d_a1, bx, by, bins):
    heads, slot, _ = e.shape
    width = k.shape[1]
    rows, wide = d_a1.shape
    sds = jax.ShapeDtypeStruct
    dma = pltpu.SemaphoreType.DMA
    vm = pltpu.VMEM
    return pl.pallas_call(
        functools.partial(back_kernel, n_mp),
        out_shape=[
            sds((rows, wide), BF16), sds((3, width, wide), F32), sds((3, 8, width), F32), sds((2, HI * heads, LO), F32),
            sds((heads, bins, 1), F32),
        ],
        in_specs=[VMEM] * 9 + [ANY] * 2,
        out_specs=[VMEM] * 5,
        scratch_shapes=[
            vm((n_mp, rows, width), BF16), vm((heads, slot, slot), BF16), vm((3, width, slot), BF16), vm((3, slot, width), BF16),
            vm((2, HI * heads * GROUP, LO * GROUP), F32), vm((heads, 5, TILE, TILE), F32), vm((n_mp - 1, rows, wide), BF16),
            vm((n_mp, rows, wide), BF16), vm((slot, slot), jnp.int32), vm((slot, slot), jnp.int32),
            dma((2,)), dma((n_mp,)), dma((n_mp,)), dma((n_mp - 1,)), dma((n_mp,)),
        ],
        compiler_params=pltpu.CompilerParams(collective_id=1, has_side_effects=True, vmem_limit_bytes=BIG),
        name="back",
    )(dctx, q, k, v, e, inv, w_qkv, xf, d_a1, bx, by)


def layer_norm(values, norm_gain, norm_shift):
    center = jnp.mean(values, axis=-1, keepdims=True)
    spread = values - center
    varied = jnp.mean(spread * spread, axis=-1, keepdims=True)
    return spread * lax.rsqrt(varied + 1e-05) * norm_gain + norm_shift


def exact_gelu(values):
    return jax.nn.gelu(values, approximate=False)


def layer(n_mp, n_dp):
    def on_device(
        hidden_in, text_lens, key_mask, bucket_x, bucket_y, w_qkv, b_q, b_v, w_out, b_out, g_attn, n_attn,
        w_up, b_up, w_down, b_down, g_ffn, n_ffn, t_pos, t_x, t_y, cotangent,
    ):
        rows, wide = hidden_in.shape
        slot = bucket_x.shape[1]
        width = w_qkv.shape[2]
        heads = width // HEAD_DIM
        bx, by = bucket_x[0], bucket_y[0]
        xf, q, k, v, e, inv, ctx, wo, wu, wd = front(
            n_mp, n_dp, hidden_in, w_qkv, b_q, b_v, bx, by, t_x, t_y, t_pos, text_lens, key_mask, w_out, w_up, w_down
        )
        wo = wo.reshape(n_mp, width, wide)
        wu = wu.reshape(n_mp, wide, -1)
        wd = wd.reshape(n_mp, -1, wide)
        b_up_all = lax.all_gather(b_up, "mp", axis=0)

        attn = jnp.einsum("sre,sed->rd", ctx, wo, preferred_element_type=F32)
        resid_one = hidden_in.astype(F32) + attn + b_out.astype(F32)
        normed, norm_back_one = jax.vjp(layer_norm, resid_one, g_attn, n_attn)
        normed_low = normed.astype(BF16)
        normed_full = lax.all_gather(normed_low, "mp", axis=0, tiled=True)
        pre = jnp.einsum("rd,sdf->srf", normed_low, wu, preferred_element_type=F32) + b_up_all.astype(F32)[:, None, :]
        act, gelu_back = jax.vjp(exact_gelu, pre)
        branch = jnp.einsum("srf,sfd->rd", act.astype(BF16), wd, preferred_element_type=F32)
        resid_two = normed + branch + b_down.astype(F32)
        out, norm_back_two = jax.vjp(layer_norm, resid_two, g_ffn, n_ffn)
        layer_out = out.astype(BF16)
        first = lax.axis_index("mp") * rows
        places = first + jnp.arange(rows, dtype=jnp.int32)
        live = (places < 1 + PATCHES + text_lens[0]).astype(F32)
        grad_y = cotangent.astype(F32) * live[:, None]
        d_z2, grad_g_ffn, grad_n_ffn = norm_back_two(grad_y)
        grad_b_down = jnp.sum(d_z2, axis=0)
        d_ffn = d_z2.astype(BF16)
        d_ffn_full = lax.all_gather(d_ffn, "mp", axis=0, tiled=True)
        d_act = jnp.einsum("rd,sfd->srf", d_ffn, wd, preferred_element_type=F32)
        d_pre = gelu_back(d_act)[0].astype(BF16)
        d_normed = d_z2 + jnp.einsum("srf,sdf->rd", d_pre, wu, preferred_element_type=F32)
        d_a1, grad_g_attn, grad_n_attn = norm_back_one(d_normed)
        grad_b_out = jnp.sum(d_a1, axis=0)
        d_attn = d_a1.astype(BF16)
        d_ctx = jnp.einsum("rd,sed->sre", d_attn, wo, preferred_element_type=F32).astype(BF16)
        input_grad, gw, gb, gt, gl = back(n_mp, d_ctx, q, k, v, e, inv, w_qkv, xf, d_a1, bx, by, t_pos.shape[1])

        pre_mine = jnp.dot(normed_full, w_up, preferred_element_type=F32) + b_up.astype(F32)
        act_mine, back_mine = jax.vjp(exact_gelu, pre_mine)
        grad_w_down = jnp.einsum("tf,td->fd", act_mine.astype(BF16), d_ffn_full, preferred_element_type=F32)
        d_act_mine = jnp.einsum("td,fd->tf", d_ffn_full, w_down, preferred_element_type=F32)
        d_pre_mine = back_mine(d_act_mine)[0].astype(BF16)
        grad_w_up = jnp.einsum("td,tf->df", normed_full, d_pre_mine, preferred_element_type=F32)
        grad_b_up = jnp.sum(d_pre_mine.astype(F32), axis=0)
        d_wo = jnp.einsum("sre,rd->sed", ctx, d_attn, preferred_element_type=F32).astype(BF16)
        grad_w_out = lax.psum_scatter(d_wo.reshape(-1, wide), "mp", scatter_dimension=0, tiled=True)

        big = lax.psum((gw.astype(BF16), grad_w_out, grad_w_up.astype(BF16), grad_w_down.astype(BF16)), "dp")
        gw, grad_w_out, grad_w_up, grad_w_down = [g.astype(F32) for g in big]
        grad_w_qkv = jnp.transpose(gw, (0, 2, 1))
        grad_t = gt.reshape(2, HI, heads, LO).transpose(0, 2, 1, 3).reshape(2, heads, HI * LO)
        small = lax.psum((gb[0, 0], gb[2, 0], grad_b_up, gl[:, :, 0], grad_t), "dp")
        grad_b_q, grad_b_v, grad_b_up, grad_t_pos, grad_t = small
        over_rows = lax.psum((grad_b_out, grad_g_attn, grad_n_attn, grad_b_down, grad_g_ffn, grad_n_ffn), ("dp", "mp"))
        grad_b_out, grad_g_attn, grad_n_attn, grad_b_down, grad_g_ffn, grad_n_ffn = over_rows
        return (
            layer_out, input_grad, grad_w_qkv, grad_b_q, grad_b_v, grad_w_out, grad_b_out, grad_g_attn, grad_n_attn,
            grad_w_up, grad_b_up, grad_w_down, grad_b_down, grad_g_ffn, grad_n_ffn, grad_t_pos, grad_t[0], grad_t[1],
        )

    return on_device


def solution(mesh):
    both, split = P(("dp", "mp"), None), P("mp")
    rows_mp, cols_mp, qkv = P("mp", None), P(None, "mp"), P(None, None, "mp")
    doc = P("dp", None, None)
    return jax.shard_map(
        layer(mesh.shape["mp"], mesh.shape["dp"]),
        mesh=mesh,
        in_specs=(
            both, P("dp"), P("dp"), doc, doc, qkv, split, split, rows_mp, P(), P(), P(), cols_mp, split, rows_mp, P(), P(), P(),
            rows_mp, rows_mp, rows_mp, both,
        ),
        out_specs=(
            both, both, qkv, split, split, rows_mp, P(), P(), P(), cols_mp, split, rows_mp, P(), P(), P(), rows_mp, rows_mp, rows_mp,
        ),
        check_vma=False,
    )
```

```python
import functools
import jax
import jax.numpy as jnp
from jax import lax
from jax.experimental import pallas as pl
from jax.experimental.pallas import tpu as pltpu
from jax.sharding import PartitionSpec as P

HEAD_DIM = 64
PATCHES = 196
THRESHOLDS = (12, 16, 23, 32, 46, 64, 91)
TILE = 128
F32, BF16 = jnp.float32, jnp.bfloat16
MESH = pl.DeviceIdType.MESH
VMEM = pl.BlockSpec(memory_space=pltpu.VMEM)
ANY = pl.BlockSpec(memory_space=pl.ANY)
BIG = 58 << 20


def line_bucket(off):
    mag = jnp.abs(off)
    far = jnp.full(off.shape, 8, jnp.int32)
    for border in THRESHOLDS:
        far = far + (mag >= border).astype(jnp.int32)
    return jnp.where(off > 0, 16, 0) + jnp.where(mag < 8, mag, far)


def dot(a, b, ca, cb):
    return lax.dot_general(a, b, (((ca,), (cb,)), ((), ())), preferred_element_type=F32)


def flip(index, bit):
    step = 2**bit
    return index + step * (1 - 2 * ((index // step) % 2))


def gather_plan(dp_size, reverse):
    bits = list(range(1, dp_size.bit_length() - 1))
    return (bits[::-1] if reverse else bits) + [0]


def plan_label(index, plan):
    label = 0
    for place, bit in enumerate(plan):
        label = label + ((index // 2**bit) % 2) * 2**place
    return label


def front_kernel(
    n_mp, n_dp, plans,
    x_ref, w_ref, bq_ref, bv_ref, bx_hbm, by_hbm, tx_ref, ty_ref, tp_ref, len_ref, km_ref, bu_ref, wo_src, wu_src, wd_src,
    xf_ref, q_ref, k_ref, v_ref, e_ref, inv_ref, cr_ref, bf_ref, wo_out, wu_out, wd_out,
    bx_ref, by_ref, bias_ref, line_ref, cs_ref,
    b_sem, x_send, x_recv, c_send, c_recv, u_send, u_recv, z_send, z_recv, p_send, p_recv,
):
    d = lax.axis_index("dp")
    z = lax.axis_index("mp")
    rows = x_ref.shape[0]
    slot = bx_ref.shape[0]
    width = w_ref.shape[1]
    heads = width // HEAD_DIM
    tiles = slot // TILE
    scale = HEAD_DIM**-0.5
    sources = (wo_src, wu_src, wd_src)
    gathered = (wo_out, wu_out, wd_out)
    others = [(z + k) % n_mp for k in range(1, n_mp)]
    depth = len(plans[0])
    labels = [plan_label(d, plan) for plan in plans]

    loads = []
    for c in range(tiles):
        part = pl.ds(c * TILE, TILE)
        pair = (
            pltpu.make_async_copy(bx_hbm.at[part], bx_ref.at[part], b_sem.at[0, c]),
            pltpu.make_async_copy(by_hbm.at[part], by_ref.at[part], b_sem.at[1, c]),
        )
        for copy in pair:
            copy.start()
        loads.append(pair)

    barrier = pltpu.get_barrier_semaphore()
    peers = [(d, to) for to in others] + [(flip(d, bit), z) for bit in plans[0]]
    for peer in peers:
        pl.semaphore_signal(barrier, inc=1, device_id=peer, device_id_type=MESH)
    xf_ref[z] = x_ref[...]
    bf_ref[z] = jnp.broadcast_to(bu_ref[...].astype(F32).reshape(1, -1), bf_ref.shape[1:])
    pl.semaphore_wait(barrier, len(peers))

    def x_hop(block, to, sem):
        return pltpu.make_async_remote_copy(
            xf_ref.at[block], xf_ref.at[block], x_send.at[sem], x_recv.at[block], device_id=(d, to), device_id_type=MESH
        )

    def w_hop(w, block, to, sem, own=False):
        held = sources[w].at[labels[w]] if own else gathered[w].at[block, labels[w]]
        return pltpu.make_async_remote_copy(
            held, gathered[w].at[block, labels[w]], z_send.at[w, sem], z_recv.at[w, block], device_id=(d, to), device_id_type=MESH
        )

    def all_w(block, to, sem, own=False):
        return [w_hop(w, block, to, sem, own) for w in range(3)]

    def start_all(copies):
        for copy in copies:
            copy.start()

    def on_step(step, act):
        for block, ahead in ((z - step, z + 1), (z + step, z - 1)):

            @pl.when(jnp.logical_and(block >= 0, block < n_mp))
            def _():
                act(block, ahead, jnp.logical_and(ahead >= 0, ahead < n_mp))

    def ends(act):
        for ahead, sem in ((z + 1, z), (z - 1, n_mp)):

            @pl.when(jnp.logical_and(ahead >= 0, ahead < n_mp))
            def _():
                act(ahead, sem)

    ends(lambda ahead, sem: x_hop(z, ahead, sem).start())
    ends(lambda ahead, sem: start_all(all_w(z, ahead, sem, True)))

    def u_copy(to, source):
        return pltpu.make_async_remote_copy(
            bf_ref.at[source], bf_ref.at[source], u_send.at[to], u_recv.at[source], device_id=(d, to), device_id_type=MESH
        )

    for to in others:
        u_copy(to, z).start()

    def x_arrived(step):
        def act(block, ahead, more):
            x_hop(block, z, block).wait_recv()

            @pl.when(more)
            def _():
                x_hop(block, ahead, block).start()

        on_step(step, act)

    def plane_copy(w, place, shard, incoming):
        size = 2**place
        base = (labels[w] // size) * size
        if incoming:
            base = flip(base, place)
        part = gathered[w].at[shard, pl.ds(base, size)]
        return pltpu.make_async_remote_copy(
            part, part, p_send.at[w, place, shard], p_recv.at[w, place, shard],
            device_id=(flip(d, plans[w][place]), z), device_id_type=MESH,
        )

    def w_arrived(step):
        def act(block, ahead, more):
            for w in range(3):
                w_hop(w, block, z, block).wait_recv()

            @pl.when(more)
            def _():
                start_all(all_w(block, ahead, block))

            for w in range(3):
                plane_copy(w, 0, block, False).start()

        on_step(step, act)

    def plane_next(step, place):
        def act(block, ahead, more):
            for w in range(3):
                plane_copy(w, place - 1, block, True).wait_recv()
                plane_copy(w, place, block, False).start()

        on_step(step, act)

    def plane_done(step):
        def act(block, ahead, more):
            for w in range(3):
                plane_copy(w, depth - 1, block, True).wait_recv()

        on_step(step, act)

    tab = [
        jnp.broadcast_to(
            jnp.concatenate([tx_ref[h : h + 1, :].astype(F32), ty_ref[h : h + 1, :].astype(F32)], axis=1) * scale, (8, TILE)
        )
        for h in range(heads)
    ]
    bins_x = tx_ref.shape[1]
    pad = jnp.zeros((1, TILE - tp_ref.shape[1]), F32)
    ltab = [
        jnp.broadcast_to(jnp.concatenate([tp_ref[h : h + 1, :].astype(F32) * scale, pad], axis=1), (8, TILE))
        for h in range(heads)
    ]
    ci = lax.broadcasted_iota(jnp.int32, (8, TILE), 1)
    ri = lax.broadcasted_iota(jnp.int32, (8, TILE), 0)

    @pl.loop(0, TILE // 8)
    def _(g):
        at = pl.ds(pl.multiple_of(g * 8, 8), 8)
        for off in range(5):
            idx = line_bucket(ci - ri - g * 8 + (off - 2) * TILE)
            for h in range(heads):
                line_ref[h, off, at, :] = jnp.take_along_axis(ltab[h], idx, axis=1)

    place_ids = lax.broadcasted_iota(jnp.int32, (1, slot), 1)
    live = place_ids < 1 + PATCHES + len_ref[0]
    seen = jnp.where(live & ((km_ref[...].reshape(1, slot) == 1) | (place_ids == 0)), 0.0, -1e30)

    def bias_chunk(c):
        for copy in loads[c]:
            copy.wait()

        @pl.loop(0, TILE // 8)
        def _(g):
            at = pl.ds(pl.multiple_of(c * TILE + g * 8, 8), 8)
            near = pl.ds(pl.multiple_of(g * 8, 8), 8)
            for j in range(tiles):
                cols = slice(j * TILE, (j + 1) * TILE)
                ix = bx_ref[at, cols]
                iy = by_ref[at, cols] + bins_x
                hide = seen[:, cols]
                off = min(max(j - c + 2, 0), 4)
                for h in range(heads):
                    b = jnp.take_along_axis(tab[h], ix, axis=1) + jnp.take_along_axis(tab[h], iy, axis=1)
                    bias_ref[h, at, cols] = (b + line_ref[h, off, near, :]) + hide

    for c in range(tiles):
        if c == tiles // 2:
            x_arrived(1)
        bias_chunk(c)
    w_arrived(1)
    x_arrived(2)
    plane_next(1, 1)
    w_arrived(2)
    for place in range(2, depth):
        plane_next(1, place)
    x_arrived(3)

    lane = lax.broadcasted_iota(jnp.int32, (1, width), 1)
    mine = [(lane >= h * HEAD_DIM) & (lane < (h + 1) * HEAD_DIM) for h in range(heads)]
    b_q = bq_ref[...].astype(F32).reshape(1, width)
    b_v = bv_ref[...].astype(F32).reshape(1, width)
    for b in range(n_mp):
        at = pl.ds(b * rows, rows)
        xb = xf_ref[b]
        q_ref[at, :] = ((dot(xb, w_ref[0], 1, 1) + b_q).astype(BF16).astype(F32) * scale).astype(BF16)
        k_ref[at, :] = dot(xb, w_ref[1], 1, 1).astype(BF16)
        v_ref[at, :] = (dot(xb, w_ref[2], 1, 1) + b_v).astype(BF16)

    def c_copy(turn, to, source):
        return pltpu.make_async_remote_copy(
            cs_ref.at[turn], cr_ref.at[source], c_send.at[turn], c_recv.at[source], device_id=(d, to), device_id_type=MESH
        )

    def attend(turn):
        to = (z + 1 + turn) % n_mp
        at = pl.ds(pl.multiple_of(to * rows, rows), rows)
        q = q_ref[at, :]
        out = jnp.zeros((rows, width), F32)
        for h in range(heads):
            s = dot(jnp.where(mine[h], q, jnp.zeros((), BF16)), k_ref[...], 1, 1) + bias_ref[h, at, :]
            top = jnp.max(s, axis=1, keepdims=True)
            e = jnp.exp(s - top).astype(BF16)
            e_ref[h, at, :] = e
            inv = 1.0 / jnp.sum(e.astype(F32), axis=1, keepdims=True)
            inv_ref[at, h : h + 1] = inv
            out = out + jnp.where(mine[h], dot(e, v_ref[...], 1, 0) * inv, 0.0)
        if turn == n_mp - 1:
            cr_ref[z] = out.astype(BF16)
        else:
            cs_ref[turn] = out.astype(BF16)
            c_copy(turn, to, z).start()

    between = {0: lambda: plane_next(2, 1), 1: lambda: w_arrived(3)}
    for turn in range(n_mp):
        attend(turn)
        if turn in between:
            between[turn]()

    for place in range(2, depth):
        plane_next(2, place)
    for place in range(1, depth):
        plane_next(3, place)
    for step in range(1, n_mp):
        plane_done(step)

    for source in others:
        c_copy(0, z, source).wait_recv()
        u_copy(z, source).wait_recv()
    for turn in range(n_mp - 1):
        c_copy(turn, z, z).wait_send()
    for to in others:
        u_copy(to, z).wait_send()

    def wait_all(copies):
        for copy in copies:
            copy.wait_send()

    def sent(block, ahead, more):
        @pl.when(more)
        def _():
            wait_all([x_hop(block, ahead, block)] + all_w(block, ahead, block))

        for w in range(3):
            for place in range(depth):
                plane_copy(w, place, block, False).wait_send()

    ends(lambda ahead, sem: wait_all([x_hop(z, ahead, sem)] + all_w(z, ahead, sem, True)))
    for step in range(1, n_mp):
        on_step(step, sent)


def front(n_mp, n_dp, x, w_qkv, b_q, b_v, bx, by, t_x, t_y, t_pos, text_lens, key_mask, b_up, w_out, w_up, w_down):
    rows, wide = x.shape
    slot = bx.shape[0]
    width = w_qkv.shape[1]
    heads = width // HEAD_DIM
    plans = [gather_plan(n_dp, False), gather_plan(n_dp, False), gather_plan(n_dp, True)]
    depth = len(plans[0])
    slices = [w.reshape(n_dp, w.shape[0] // n_dp, w.shape[1]) for w in (w_out, w_up, w_down)]
    sds = jax.ShapeDtypeStruct
    dma = pltpu.SemaphoreType.DMA
    return pl.pallas_call(
        functools.partial(front_kernel, n_mp, n_dp, plans),
        out_shape=[
            sds((n_mp, rows, wide), BF16), sds((slot, width), BF16), sds((slot, width), BF16), sds((slot, width), BF16),
            sds((heads, slot, slot), BF16), sds((slot, heads), F32), sds((n_mp, rows, width), BF16),
            sds((n_mp, 8) + b_up.shape, F32),
        ] + [sds((n_mp,) + s.shape, BF16) for s in slices],
        in_specs=[VMEM] * 4 + [ANY, ANY] + [VMEM] * 3 + [pl.BlockSpec(memory_space=pltpu.SMEM), VMEM, VMEM] + [ANY] * 3,
        out_specs=[VMEM] * 8 + [ANY] * 3,
        scratch_shapes=[
            pltpu.VMEM((slot, slot), jnp.int32), pltpu.VMEM((slot, slot), jnp.int32), pltpu.VMEM((heads, slot, slot), F32),
            pltpu.VMEM((heads, 5, TILE, TILE), F32), pltpu.VMEM((n_mp - 1, rows, width), BF16),
            dma((2, slot // TILE)), dma((n_mp + 1,)), dma((n_mp,)), dma((n_mp - 1,)), dma((n_mp,)), dma((n_mp,)), dma((n_mp,)),
            dma((3, n_mp + 1)), dma((3, n_mp)), dma((3, depth, n_mp)), dma((3, depth, n_mp)),
        ],
        compiler_params=pltpu.CompilerParams(collective_id=0, has_side_effects=True, vmem_limit_bytes=BIG),
        name="front",
    )(x, w_qkv, b_q, b_v, bx, by, t_x, t_y, t_pos, text_lens, key_mask, b_up, *slices)

EPS = 1e-05


def mid_kernel(
    n_mp,
    x_ref, ctx_ref, wo_own, wu_own, wd_own, wo_hbm, wu_hbm, wd_hbm, bu_ref, bo_ref, ga_ref, na_ref, bd_ref, gf_ref, nf_ref,
    cot_ref, len_ref,
    lo_ref, nl_ref, df_ref, da_ref, dc_ref, go_ref, gs_ref,
    wo_ref, wu_ref, wd_ref, gp_ref, sem,
):
    z = lax.axis_index("mp")
    rows, wide = x_ref.shape
    others = [(z + k) % n_mp for k in range(1, n_mp)]
    loads = []
    for w, (own, rest, held) in enumerate(((wo_own, wo_hbm, wo_ref), (wu_own, wu_hbm, wu_ref), (wd_own, wd_hbm, wd_ref))):
        copies = [pltpu.make_async_copy(own, held.at[z], sem.at[w, z])]
        copies += [pltpu.make_async_copy(rest.at[s], held.at[s], sem.at[w, s]) for s in others]
        for copy in copies:
            copy.start()
        loads.append(copies)

    def vec(ref):
        return ref[...].astype(F32).reshape(1, wide)

    def norm(values):
        spread = values - jnp.mean(values, axis=1, keepdims=True)
        rate = lax.rsqrt(jnp.mean(spread * spread, axis=1, keepdims=True) + EPS)
        return spread * rate, rate

    def norm_back(up, gain, hat, rate):
        scaled = up * gain
        first = jnp.mean(scaled, axis=1, keepdims=True)
        second = jnp.mean(scaled * hat, axis=1, keepdims=True)
        return rate * (scaled - first - hat * second)

    def total(values):
        return jnp.sum(values, axis=0, keepdims=True)

    for copy in loads[0]:
        copy.wait()
    attn = dot(ctx_ref[0], wo_ref[0], 1, 0)
    for s in range(1, n_mp):
        attn = attn + dot(ctx_ref[s], wo_ref[s], 1, 0)
    hat_one, rate_one = norm(x_ref[...].astype(F32) + attn + vec(bo_ref))
    normed = hat_one * vec(ga_ref) + vec(na_ref)
    low = normed.astype(BF16)
    nl_ref[...] = low

    for copies in loads[1:]:
        for copy in copies:
            copy.wait()
    ffn = jnp.zeros((rows, wide), F32)
    for s in range(n_mp):
        pre = dot(low, wu_ref[s], 1, 0) + bu_ref[s, 0:1, :]
        cdf = 0.5 * (1.0 + lax.erf(pre * (0.5**0.5)))
        gp_ref[s] = cdf + pre * (jnp.exp(-0.5 * pre * pre) * 0.3989422804014327)
        ffn = ffn + dot((pre * cdf).astype(BF16), wd_ref[s], 1, 0)
    hat_two, rate_two = norm(normed + ffn + vec(bd_ref))
    lo_ref[...] = (hat_two * vec(gf_ref) + vec(nf_ref)).astype(BF16)

    place = z * rows + lax.broadcasted_iota(jnp.int32, (rows, 1), 0)
    grad_y = jnp.where(place < 1 + PATCHES + len_ref[0], cot_ref[...].astype(F32), 0.0)
    d_two = norm_back(grad_y, vec(gf_ref), hat_two, rate_two)
    d_ffn = d_two.astype(BF16)
    df_ref[...] = d_ffn
    d_normed = d_two
    for s in range(n_mp):
        d_pre = (dot(d_ffn, wd_ref[s], 1, 1) * gp_ref[s]).astype(BF16)
        d_normed = d_normed + dot(d_pre, wu_ref[s], 1, 1)
    d_one = norm_back(d_normed, vec(ga_ref), hat_one, rate_one)
    da_ref[...] = d_one
    d_attn = d_one.astype(BF16)
    for s in range(n_mp):
        dc_ref[s] = dot(d_attn, wo_ref[s], 1, 1).astype(BF16)
        go_ref[s] = dot(ctx_ref[s].astype(F32).T.astype(BF16), d_attn, 1, 0).astype(BF16)
    gs_ref[...] = jnp.concatenate(
        [
            total(grad_y * hat_two), total(grad_y), total(d_two), total(d_normed * hat_one), total(d_normed), total(d_one),
            jnp.zeros((2, wide), F32),
        ],
        axis=0,
    )


def middle(n_mp, x, ctx, owns, gathered, b_up_all, b_out, g_attn, n_attn, b_down, g_ffn, n_ffn, cotangent, text_lens):
    rows, wide = x.shape
    sds = jax.ShapeDtypeStruct
    width, units = owns[0].shape[0], owns[1].shape[1]
    return pl.pallas_call(
        functools.partial(mid_kernel, n_mp),
        out_shape=[
            sds((rows, wide), BF16), sds((rows, wide), BF16), sds((rows, wide), BF16), sds((rows, wide), F32),
            sds((n_mp, rows, width), BF16), sds((n_mp, width, wide), BF16), sds((8, wide), F32),
        ],
        in_specs=[VMEM] * 2 + [ANY] * 6 + [VMEM] * 8 + [pl.BlockSpec(memory_space=pltpu.SMEM)],
        out_specs=[VMEM] * 7,
        scratch_shapes=[
            pltpu.VMEM((n_mp, width, wide), BF16), pltpu.VMEM((n_mp, wide, units), BF16), pltpu.VMEM((n_mp, units, wide), BF16),
            pltpu.VMEM((n_mp, rows, units), F32), pltpu.SemaphoreType.DMA((3, n_mp)),
        ],
        compiler_params=pltpu.CompilerParams(vmem_limit_bytes=BIG),
        name="middle",
    )(x, ctx, *owns, *gathered, b_up_all, b_out, g_attn, n_attn, b_down, g_ffn, n_ffn, cotangent, text_lens)

HI, LO, GROUP, STEP = 4, 16, 16, 2
PACK = 48


def sums_in_kernel(n_dp, *sizes):
    return all(size % (8 * n_dp) == 0 for size in sizes)


def rear_kernel(
    n_mp, n_dp, plans, summed,
    nl_ref, df_ref, dc_in, go_ref, gs_ref, da_ref, q_ref, k_ref, v_ref, e_ref, inv_ref, w_ref, xf_ref, wu_ref, wd_ref, bu_ref,
    bx_hbm, by_hbm,
    ig_ref, pack_ref, uo_ref, do_ref, qo_ref, oo_ref,
    dc_ref, ds_ref, dt_ref, dn_ref, acc_ref, near_ref, part_ref, got_ref, bx_ref, by_ref, nf_ref, dff_ref, act_ref, gp_ref,
    sp_ref, b_sem, d_send, d_recv, r_send, r_recv, h_send, h_recv,
    *for_sums,
):
    if summed:
        (
            ua_ref, da2_ref, qa_ref, oa_ref, us_ref, ds2_ref, qs_ref, os_ref, ur_ref, dr_ref, qr_ref, or_ref, oz_ref, sr_ref, sz_ref,
            rs_send, rs_recv, ag_send, ag_recv, oz_send, oz_recv, sp_send, sp_recv, sz_send, sz_recv,
        ) = for_sums
    d = lax.axis_index("dp")
    z = lax.axis_index("mp")
    heads, slot, _ = e_ref.shape
    width = k_ref.shape[1]
    rows, wide = da_ref.shape
    tiles = slot // TILE
    scale = HEAD_DIM**-0.5
    others = [(z + k) % n_mp for k in range(1, n_mp)]
    depth = len(plans[0])

    loads = [pltpu.make_async_copy(bx_hbm, bx_ref, b_sem.at[0]), pltpu.make_async_copy(by_hbm, by_ref, b_sem.at[1])]
    for copy in loads:
        copy.start()
    barrier = pltpu.get_barrier_semaphore()
    peers = [(d, to) for to in others] + [(flip(d, bit), z) for bit in plans[0] if summed]
    for peer in peers:
        pl.semaphore_signal(barrier, inc=1, device_id=peer, device_id_type=MESH)
    nf_ref[z] = nl_ref[...]
    dff_ref[z] = df_ref[...]
    dc_ref[z] = dc_in[z]
    pl.semaphore_wait(barrier, len(peers))

    def remote(src, dst, send, recv, to):
        return pltpu.make_async_remote_copy(src, dst, send, recv, device_id=to, device_id_type=MESH)

    def d_copy(to, source):
        return remote(dc_in.at[to], dc_ref.at[source], d_send.at[to], d_recv.at[source], (d, to))

    for to in others:
        d_copy(to, z).start()

    lines = (nf_ref, dff_ref)

    def hop(a, block, to, sem):
        return remote(lines[a].at[block], lines[a].at[block], h_send.at[a, sem], h_recv.at[a, block], (d, to))

    def ends(act):
        for ahead, sem in ((z + 1, z), (z - 1, n_mp)):

            @pl.when(jnp.logical_and(ahead >= 0, ahead < n_mp))
            def _():
                act(ahead, sem)

    def on_step(step, act):
        for block, ahead in ((z - step, z + 1), (z + step, z - 1)):

            @pl.when(jnp.logical_and(block >= 0, block < n_mp))
            def _():
                act(block, ahead, jnp.logical_and(ahead >= 0, ahead < n_mp))

    def arrived(a, step):
        def act(block, ahead, more):
            hop(a, block, z, block).wait_recv()

            @pl.when(more)
            def _():
                hop(a, block, ahead, block).start()

        on_step(step, act)

    for a in range(2):
        ends(lambda ahead, sem: hop(a, z, ahead, sem).start())

    items = ((None, None, None, plans[0]),) if not summed else (
        (ua_ref, us_ref, ur_ref, plans[0]), (da2_ref, ds2_ref, dr_ref, plans[1]), (qa_ref, qs_ref, qr_ref, plans[0]),
        (oa_ref, os_ref, or_ref, plans[1]),
    )
    outs = (uo_ref, do_ref, qo_ref, oo_ref)
    labels = [plan_label(d, item[3]) for item in items]

    def halves(i, place):
        size = 2**place
        base = (labels[i] // size) * size
        return pl.ds(base, size), pl.ds(flip(base, place), size), size

    def rs_copy(i, place):
        _, away, size = halves(i, place)
        _, staged, got, plan = items[i]
        return remote(staged.at[away], got.at[pl.ds(size, size)], rs_send.at[i, place], rs_recv.at[i, place], (flip(d, plan[place]), z))

    def rs_start(i, place):
        if not summed:
            return
        _, away, _ = halves(i, place)
        items[i][1][away] = items[i][0][away].astype(BF16)
        rs_copy(i, place).start()

    def rs_finish(i, place):
        if not summed:
            return
        kept, _, size = halves(i, place)
        rs_copy(i, place).wait_recv()
        total, _, got, _ = items[i]
        total[kept] = total[kept] + got[size : 2 * size].astype(F32)

    def ag_copy(i, place, incoming=False):
        kept, away, _ = halves(i, place)
        part = outs[i].at[away if incoming else kept]
        return remote(part, part, ag_send.at[i, place], ag_recv.at[i, place], (flip(d, items[i][3][place]), z))

    if summed:
        for s in range(n_mp):
            oa_ref[:, s] = go_ref[s].astype(F32).reshape(n_dp, -1, wide)
    else:
        oo_ref[...] = go_ref[...]
    rs_start(3, depth - 1)

    sp_ref[0:8, :] = gs_ref[...]

    def sz_copy(to, source):
        return remote(gs_ref, sz_ref.at[source], sz_send.at[to], sz_recv.at[source], (d, to))

    if summed:
        for to in others:
            sz_copy(to, z).start()

    lane = lax.broadcasted_iota(jnp.int32, (1, width), 1)
    mine = [(lane >= h * HEAD_DIM) & (lane < (h + 1) * HEAD_DIM) for h in range(heads)]
    zero = jnp.zeros((), BF16)
    factor = jnp.zeros((slot, width), F32)
    for h in range(heads):
        factor = jnp.where(mine[h], inv_ref[:, h : h + 1], factor)
    qt = q_ref[...].astype(F32).T.astype(BF16)
    for source in others:
        d_copy(source, source).wait_recv()
    for a in range(2):
        arrived(a, 1)

    dctx = dc_ref[...].reshape(slot, width)
    gt = (dctx.astype(F32) * factor).T.astype(BF16)
    block = 384
    dq = [None] * (slot // block)
    for h in range(heads):
        hs = slice(h * HEAD_DIM, (h + 1) * HEAD_DIM)
        dk = dv = None
        for r in range(slot // block):
            rs = slice(r * block, (r + 1) * block)
            e = e_ref[h, rs, :]
            p = e.astype(F32) * inv_ref[rs, h : h + 1]
            dp = dot(jnp.where(mine[h], dctx[rs, :], zero), v_ref[...], 1, 1)
            ds = (p * (dp - jnp.sum(p * dp, axis=1, keepdims=True))).astype(BF16)
            ds_ref[h, rs, :] = ds
            a = jnp.where(mine[h], dot(ds, k_ref[...], 1, 0), 0.0)
            dq[r] = a if dq[r] is None else dq[r] + a
            b = dot(qt[hs, rs], ds, 1, 0)
            dk = b if dk is None else dk + b
            c = dot(gt[hs, rs], e, 1, 0)
            dv = c if dv is None else dv + c
        dt_ref[1, hs, :] = dk.astype(BF16)
        dt_ref[2, hs, :] = dv.astype(BF16)
    for r in range(slot // block):
        rs = slice(r * block, (r + 1) * block)
        low = (dq[r] * scale).astype(BF16)
        dn_ref[0, rs, :] = low
        dt_ref[0, :, rs] = low.astype(F32).T.astype(BF16)
    for c in (1, 2):
        dn_ref[c] = dt_ref[c].astype(F32).T.astype(BF16)

    for a in range(2):
        arrived(a, 2)
    rs_finish(3, depth - 1)
    rs_start(3, depth - 2)

    def r_copy(turn, to, source):
        return remote(part_ref.at[turn], got_ref.at[source], r_send.at[turn], r_recv.at[source], (d, to))

    def dx_part(to):
        at = pl.ds(pl.multiple_of(to * rows, rows), rows)
        out = dot(dn_ref[0, at, :], w_ref[0], 1, 0)
        for c in (1, 2):
            out = out + dot(dn_ref[c, at, :], w_ref[c], 1, 0)
        return out

    for turn in range(n_mp - 1):
        part_ref[turn] = dx_part(others[turn]).astype(BF16)
        r_copy(turn, others[turn], z).start()
    dx = da_ref[...] + dx_part(z)

    ones = jnp.ones((8, slot), BF16)
    xf = xf_ref[...].reshape(slot, wide)
    def keep(i, values, part=0, parts=1):
        if summed:
            total = items[i][0]
            count_ = total.shape[0] // parts
            total[part * count_ : (part + 1) * count_] = values.reshape(count_, -1, values.shape[1])
        else:
            outs[i][part] = values.astype(BF16)

    for c in range(3):
        gw = dot(dt_ref[c], xf, 1, 0)
        if summed:
            qa_ref[:, c] = gw.reshape(n_dp, -1, wide)
        else:
            qo_ref[c] = gw.astype(BF16)
    sp_ref[9:10, 0:width] = dot(ones, dn_ref[0], 1, 0)[0:1]
    sp_ref[10:11, 0:width] = dot(ones, dn_ref[2], 1, 0)[0:1]
    rs_start(2, depth - 1)

    for copy in loads:
        copy.wait()
    acc_ref[...] = jnp.zeros_like(acc_ref)
    one = jnp.ones((), BF16)

    def count(first, last):
        @pl.loop(first, last)
        def _(i):
            at = [pl.ds(pl.multiple_of(i * GROUP * STEP + g * GROUP, GROUP), GROUP) for g in range(STEP)]
            ds = [[ds_ref[h, at[g], :] for h in range(heads)] for g in range(STEP)]
            for t, b_ref in enumerate((bx_ref, by_ref)):
                tot = None
                for g in range(STEP):
                    b = b_ref[at[g], :]
                    hi = (b >> 4).astype(F32).astype(BF16)
                    lo = (b & 15).astype(F32).astype(BF16)
                    left = []
                    for a in range(HI):
                        m = hi == jnp.asarray(a, BF16)
                        left += [jnp.where(m, ds[g][h], zero) for h in range(heads)]
                    right = [jnp.where(lo == jnp.asarray(c, BF16), one, zero) for c in range(LO)]
                    o = dot(jnp.concatenate(left, 0), jnp.concatenate(right, 0), 1, 1)
                    tot = o if tot is None else tot + o
                acc_ref[t] += tot

    waiting = {2: depth - 1, 3: depth - 2}

    def onward(i):
        if waiting[i] > 0:
            rs_finish(i, waiting[i])
            waiting[i] -= 1
            rs_start(i, waiting[i])

    trips = slot // (GROUP * STEP)
    for part in range(4):
        count(part * trips // 4, (part + 1) * trips // 4)
        onward(2)
        onward(3)
    for i in (2, 3):
        while waiting[i] > 0:
            onward(i)

    m, n = HI * heads * GROUP, LO * GROUP
    same = (lax.broadcasted_iota(jnp.int32, (m, n), 0) & (GROUP - 1)) == (lax.broadcasted_iota(jnp.int32, (m, n), 1) & (GROUP - 1))
    pick = (lax.broadcasted_iota(jnp.int32, (n, LO), 0) // GROUP == lax.broadcasted_iota(jnp.int32, (n, LO), 1)).astype(F32)
    for t in range(2):
        kept = jnp.sum(jnp.where(same, acc_ref[t], 0.0).reshape(m // GROUP, GROUP, n), axis=1)
        found = lax.dot_general(
            kept, pick, (((1,), (0,)), ((), ())), precision=lax.Precision.HIGHEST, preferred_element_type=F32
        )
        sp_ref[16 : 16 + HI * heads, t * TILE : t * TILE + LO] = found * scale

    for h in range(heads):
        for off in range(5):
            tot = jnp.zeros((TILE, TILE), F32)
            for i in range(tiles):
                for j in range(tiles):
                    if min(max(j - i, -2), 2) + 2 == off:
                        tot = tot + ds_ref[h, i * TILE : (i + 1) * TILE, j * TILE : (j + 1) * TILE].astype(F32)
            near_ref[h, off] = tot
    ci = lax.broadcasted_iota(jnp.int32, (TILE, TILE), 1)
    ri = lax.broadcasted_iota(jnp.int32, (TILE, TILE), 0)
    bins = 32
    half = bins // 2
    ids = [line_bucket(ci - ri + (off - 2) * TILE) for off in range(5)]
    for h in range(heads):
        found = []
        for b in range(bins):
            tot = None
            for off in range(5):
                if off in (1, 2, 3) and (off == 2 or (b >= half) == (off == 3)):
                    piece = jnp.where(ids[off] == b, near_ref[h, off], 0.0)
                elif off == 0 and b == half - 1 or off == 4 and b == bins - 1:
                    piece = near_ref[h, off]
                else:
                    continue
                tot = piece if tot is None else tot + piece
            found.append(jnp.sum(tot, axis=0, keepdims=True))
        lines_h = jnp.sum(jnp.concatenate(found, 0), axis=1, keepdims=True) * scale
        sp_ref[16 : 16 + bins, (2 + h) * TILE : (2 + h) * TILE + 1] = lines_h

    for a in range(2):
        arrived(a, 3)
    b_up = bu_ref[...].astype(F32).reshape(1, -1)
    for b in range(n_mp):
        at = slice(b * rows, (b + 1) * rows)
        pre = dot(nf_ref[b], wu_ref[...], 1, 0) + b_up
        cdf = 0.5 * (1.0 + lax.erf(pre * (0.5**0.5)))
        act_ref[at, :] = (pre * cdf).astype(BF16)
        gp_ref[at, :] = cdf + pre * (jnp.exp(-0.5 * pre * pre) * 0.3989422804014327)
    dff = dff_ref[...].reshape(slot, wide)
    keep(1, dot(act_ref[...], dff, 0, 0))
    rs_start(1, depth - 1)
    act_ref[...] = (dot(dff, wd_ref[...], 1, 1) * gp_ref[...]).astype(BF16)
    keep(0, dot(nf_ref[...].reshape(slot, wide), act_ref[...], 0, 0))
    rs_start(0, depth - 1)
    sp_ref[8:9, :] = dot(ones, act_ref[...], 1, 0)[0:1]

    def sp_copy(place):
        return remote(sp_ref, sr_ref.at[place], sp_send.at[place], sp_recv.at[place], (flip(d, plans[0][place]), z))

    def oz_copy(to, source):
        return remote(os_ref.at[labels[3], to], oz_ref.at[source], oz_send.at[to], oz_recv.at[source], (d, to))

    def finish_sums():
        for source in others:
            sz_copy(z, source).wait_recv()
            sp_ref[0:8, :] = sp_ref[0:8, :] + sz_ref[source]

        sp_copy(depth - 1).start()
        rs_finish(2, 0)
        rs_finish(3, 0)
        qo_ref[labels[2]] = qa_ref[labels[2]].astype(BF16)
        ag_copy(2, 0).start()
        os_ref[labels[3]] = oa_ref[labels[3]].astype(BF16)
        for to in others:
            oz_copy(to, z).start()
        for place in range(depth - 1, -1, -1):
            for i in (1, 0):
                rs_finish(i, place)
                if place:
                    rs_start(i, place - 1)
            sp_copy(place).wait_send()
            sp_copy(place).wait_recv()
            sp_ref[...] = sp_ref[...] + sr_ref[place]
            if place:
                sp_copy(place - 1).start()
            if place == depth - 1:
                out = oa_ref[labels[3], z]
                for source in others:
                    oz_copy(z, source).wait_recv()
                    out = out + oz_ref[source].astype(F32)
                oo_ref[labels[3]] = out.astype(BF16)
                ag_copy(3, 0).start()
        for i, ref in ((0, uo_ref), (1, do_ref)):
            ref[labels[i]] = items[i][0][labels[i]].astype(BF16)
            ag_copy(i, 0).start()
        pack_ref[...] = sp_ref[...]
        for place in range(1, depth):
            for i in (2, 3, 0, 1):
                ag_copy(i, place - 1, True).wait_recv()
                ag_copy(i, place).start()

    if summed:
        finish_sums()
    else:
        pack_ref[...] = sp_ref[...]

    for source in others:
        r_copy(0, z, source).wait_recv()
        dx = dx + got_ref[source].astype(F32)
    ig_ref[...] = dx.astype(BF16)

    for turn in range(n_mp - 1):
        r_copy(turn, z, z).wait_send()
    for to in others:
        d_copy(to, z).wait_send()
    if summed:
        for i in range(4):
            ag_copy(i, depth - 1, True).wait_recv()
        for to in others:
            sz_copy(to, z).wait_send()
            oz_copy(to, z).wait_send()
        for i in range(4):
            for place in range(depth):
                rs_copy(i, place).wait_send()
                ag_copy(i, place).wait_send()
    for a in range(2):
        ends(lambda ahead, sem: hop(a, z, ahead, sem).wait_send())

        def sent(block, ahead, more):
            @pl.when(more)
            def _():
                hop(a, block, ahead, block).wait_send()

        for step in range(1, n_mp):
            on_step(step, sent)


def rear(n_mp, n_dp, nl, df, dctx, d_wo, over_rows, d_a1, q, k, v, e, inv, w_t, xf, w_up, w_down, b_up, bx, by):
    heads, slot, _ = e.shape
    width = k.shape[1]
    rows, wide = d_a1.shape
    units = w_up.shape[1]
    plans = [gather_plan(n_dp, False), gather_plan(n_dp, True)]
    depth = len(plans[0])
    summed = sums_in_kernel(n_dp, width, units, wide)
    if summed:
        ru, rd, ro = wide // n_dp, units // n_dp, width // n_dp
        shapes = [(n_dp, ru, units), (n_dp, rd, wide), (n_dp, 3, ro, wide), (n_dp, ro, wide)]
    else:
        shapes = [(1, wide, units), (1, units, wide), (3, width, wide), (n_mp, width, wide)]
    sds = jax.ShapeDtypeStruct
    dma = pltpu.SemaphoreType.DMA
    vm = pltpu.VMEM
    return pl.pallas_call(
        functools.partial(rear_kernel, n_mp, n_dp, plans, summed),
        out_shape=[
            sds((rows, wide), BF16), sds((PACK, wide), F32)] + [sds(shape, BF16) for shape in shapes],
        in_specs=[VMEM] * 16 + [ANY] * 2,
        out_specs=[VMEM] * 6,
        scratch_shapes=[
            vm((n_mp, rows, width), BF16), vm((heads, slot, slot), BF16), vm((3, width, slot), BF16), vm((3, slot, width), BF16),
            vm((2, HI * heads * GROUP, LO * GROUP), F32), vm((heads, 5, TILE, TILE), F32), vm((n_mp - 1, rows, wide), BF16),
            vm((n_mp, rows, wide), BF16), vm((slot, slot), jnp.int32), vm((slot, slot), jnp.int32),
            vm((n_mp, rows, wide), BF16), vm((n_mp, rows, wide), BF16), vm((slot, units), BF16), vm((slot, units), F32),
            vm((PACK, wide), F32), dma((2,)), dma((n_mp,)), dma((n_mp,)), dma((n_mp - 1,)), dma((n_mp,)), dma((2, n_mp + 1)), dma((2, n_mp)),
        ] + ([
            vm((n_dp, ru, units), F32), vm((n_dp, rd, wide), F32), vm((n_dp, 3, ro, wide), F32), vm((n_dp, n_mp, ro, wide), F32),
        ] + 2 * [
            vm((n_dp, ru, units), BF16), vm((n_dp, rd, wide), BF16), vm((n_dp, 3, ro, wide), BF16), vm((n_dp, n_mp, ro, wide), BF16),
        ] + [
            vm((n_mp, ro, wide), BF16), vm((depth, PACK, wide), F32), vm((n_mp, 8, wide), F32),
            dma((4, depth)), dma((4, depth)), dma((4, depth)), dma((4, depth)), dma((n_mp,)), dma((n_mp,)), dma((depth,)), dma((depth,)),
            dma((n_mp,)), dma((n_mp,)),
        ] if summed else []),
        compiler_params=pltpu.CompilerParams(collective_id=1, has_side_effects=True, vmem_limit_bytes=60 << 20),
        name="rear",
    )(nl, df, dctx, d_wo, over_rows, d_a1, q, k, v, e, inv, w_t, xf, w_up, w_down, b_up, bx, by)


def layer(n_mp, n_dp):
    def on_device(
        hidden_in, text_lens, key_mask, bucket_x, bucket_y, w_qkv, b_q, b_v, w_out, b_out, g_attn, n_attn,
        w_up, b_up, w_down, b_down, g_ffn, n_ffn, t_pos, t_x, t_y, cotangent,
    ):
        rows, wide = hidden_in.shape
        slot = bucket_x.shape[1]
        width = w_qkv.shape[2]
        heads = width // HEAD_DIM
        bx, by = bucket_x[0], bucket_y[0]
        w_t = jnp.transpose(w_qkv, (0, 2, 1))
        xf, q, k, v, e, inv, ctx, b_up_all, wo, wu, wd = front(
            n_mp, n_dp, hidden_in, w_t, b_q, b_v, bx, by, t_x, t_y, t_pos, text_lens, key_mask, b_up, w_out, w_up, w_down
        )
        gathered = (wo.reshape((n_mp,) + w_out.shape), wu.reshape((n_mp,) + w_up.shape), wd.reshape((n_mp,) + w_down.shape))
        layer_out, normed_low, d_ffn, d_a1, d_ctx, d_wo, over_rows = middle(
            n_mp, hidden_in, ctx, (w_out, w_up, w_down), gathered, b_up_all, b_out, g_attn, n_attn, b_down, g_ffn, n_ffn,
            cotangent, text_lens,
        )
        input_grad, pack, g_up, g_down, g_qkv, g_out = rear(
            n_mp, n_dp, normed_low, d_ffn, d_ctx, d_wo, over_rows, d_a1, q, k, v, e, inv, w_t, xf, w_up, w_down, b_up, bx, by
        )

        if sums_in_kernel(n_dp, width, w_up.shape[1], wide):
            g_qkv = jnp.transpose(g_qkv, (1, 0, 2, 3))
        else:
            g_out = lax.psum_scatter(g_out.reshape(-1, wide), "mp", scatter_dimension=0, tiled=True)
            g_up, g_down, g_qkv, g_out, pack = lax.psum((g_up, g_down, g_qkv, g_out, pack), "dp")
            pack = jnp.concatenate([lax.psum(pack[:8], "mp"), pack[8:]], axis=0)
        grad_w_up = g_up.reshape(w_up.shape).astype(F32)
        grad_w_down = g_down.reshape(w_down.shape).astype(F32)
        grad_w_out = g_out.reshape(w_out.shape).astype(F32)
        grad_w_qkv = jnp.transpose(g_qkv.reshape(3, width, wide).astype(F32), (0, 2, 1))
        grad_g_ffn, grad_n_ffn, grad_b_down, grad_g_attn, grad_n_attn, grad_b_out, _, _, grad_b_up = [pack[i] for i in range(9)]
        grad_b_q, grad_b_v = pack[9, :width], pack[10, :width]
        tables = [
            pack[16 : 16 + HI * heads, t * TILE : t * TILE + LO].reshape(HI, heads, LO).transpose(1, 0, 2).reshape(heads, HI * LO)
            for t in range(2)
        ]
        grad_t_pos = jnp.stack([pack[16:, (2 + h) * TILE] for h in range(heads)])
        return (
            layer_out, input_grad, grad_w_qkv, grad_b_q, grad_b_v, grad_w_out, grad_b_out, grad_g_attn, grad_n_attn,
            grad_w_up, grad_b_up, grad_w_down, grad_b_down, grad_g_ffn, grad_n_ffn, grad_t_pos, tables[0], tables[1],
        )

    return on_device


def solution(mesh):
    both, split = P(("dp", "mp"), None), P("mp")
    rows_mp, cols_mp, qkv = P("mp", None), P(None, "mp"), P(None, None, "mp")
    doc = P("dp", None, None)
    return jax.shard_map(
        layer(mesh.shape["mp"], mesh.shape["dp"]),
        mesh=mesh,
        in_specs=(
            both, P("dp"), P("dp"), doc, doc, qkv, split, split, rows_mp, P(), P(), P(), cols_mp, split, rows_mp, P(), P(), P(),
            rows_mp, rows_mp, rows_mp, both,
        ),
        out_specs=(
            both, both, qkv, split, split, rows_mp, P(), P(), P(), cols_mp, split, rows_mp, P(), P(), P(), rows_mp, rows_mp, rows_mp,
        ),
        check_vma=False,
    )
```

```python
import functools
import jax
import jax.numpy as jnp
from jax import lax
from jax.experimental import pallas as pl
from jax.experimental.pallas import tpu as pltpu
from jax.sharding import PartitionSpec as P

HEAD_DIM = 64
PATCHES = 196
THRESHOLDS = (12, 16, 23, 32, 46, 64, 91)
TILE = 128
F32, BF16 = jnp.float32, jnp.bfloat16
MESH = pl.DeviceIdType.MESH
VMEM = pl.BlockSpec(memory_space=pltpu.VMEM)
ANY = pl.BlockSpec(memory_space=pl.ANY)
BIG = 58 << 20


def line_bucket(off):
    mag = jnp.abs(off)
    far = jnp.full(off.shape, 8, jnp.int32)
    for border in THRESHOLDS:
        far = far + (mag >= border).astype(jnp.int32)
    return jnp.where(off > 0, 16, 0) + jnp.where(mag < 8, mag, far)


def dot(a, b, ca, cb):
    return lax.dot_general(a, b, (((ca,), (cb,)), ((), ())), preferred_element_type=F32)


def flip(index, bit):
    step = 2**bit
    return index + step * (1 - 2 * ((index // step) % 2))


def gather_plan(dp_size, reverse):
    bits = list(range(1, dp_size.bit_length() - 1))
    return (bits[::-1] if reverse else bits) + [0]


def plan_label(index, plan):
    label = 0
    for place, bit in enumerate(plan):
        label = label + ((index // 2**bit) % 2) * 2**place
    return label


def front_kernel(
    n_mp, n_dp, plans,
    x_ref, w_ref, bq_ref, bv_ref, bx_hbm, by_hbm, tx_ref, ty_ref, tp_ref, len_ref, km_ref, bu_ref, wo_src, wu_src, wd_src,
    xf_ref, q_ref, k_ref, v_ref, e_ref, inv_ref, cr_ref, bf_ref, wo_out, wu_out, wd_out,
    bx_ref, by_ref, bias_ref, line_ref, cs_ref,
    b_sem, x_send, x_recv, c_send, c_recv, u_send, u_recv, z_send, z_recv, p_send, p_recv,
):
    d = lax.axis_index("dp")
    z = lax.axis_index("mp")
    rows = x_ref.shape[0]
    slot = bx_ref.shape[0]
    width = w_ref.shape[1]
    heads = width // HEAD_DIM
    tiles = slot // TILE
    scale = HEAD_DIM**-0.5
    sources = (wo_src, wu_src, wd_src)
    gathered = (wo_out, wu_out, wd_out)
    others = [(z + k) % n_mp for k in range(1, n_mp)]
    depth = len(plans[0])
    labels = [plan_label(d, plan) for plan in plans]

    loads = []
    for c in range(tiles):
        part = pl.ds(c * TILE, TILE)
        pair = (
            pltpu.make_async_copy(bx_hbm.at[part], bx_ref.at[part], b_sem.at[0, c]),
            pltpu.make_async_copy(by_hbm.at[part], by_ref.at[part], b_sem.at[1, c]),
        )
        for copy in pair:
            copy.start()
        loads.append(pair)

    barrier = pltpu.get_barrier_semaphore()
    peers = [(d, to) for to in others] + [(flip(d, bit), z) for bit in plans[0]]
    for peer in peers:
        pl.semaphore_signal(barrier, inc=1, device_id=peer, device_id_type=MESH)
    xf_ref[z] = x_ref[...]
    bf_ref[z] = jnp.broadcast_to(bu_ref[...].astype(F32).reshape(1, -1), bf_ref.shape[1:])
    pl.semaphore_wait(barrier, len(peers))

    def x_hop(block, to, sem):
        return pltpu.make_async_remote_copy(
            xf_ref.at[block], xf_ref.at[block], x_send.at[sem], x_recv.at[block], device_id=(d, to), device_id_type=MESH
        )

    def w_hop(w, block, to, sem, own=False):
        held = sources[w].at[labels[w]] if own else gathered[w].at[block, labels[w]]
        return pltpu.make_async_remote_copy(
            held, gathered[w].at[block, labels[w]], z_send.at[w, sem], z_recv.at[w, block], device_id=(d, to), device_id_type=MESH
        )

    def all_w(block, to, sem, own=False):
        return [w_hop(w, block, to, sem, own) for w in range(3)]

    def start_all(copies):
        for copy in copies:
            copy.start()

    def on_step(step, act):
        for block, ahead in ((z - step, z + 1), (z + step, z - 1)):

            @pl.when(jnp.logical_and(block >= 0, block < n_mp))
            def _():
                act(block, ahead, jnp.logical_and(ahead >= 0, ahead < n_mp))

    def ends(act):
        for ahead, sem in ((z + 1, z), (z - 1, n_mp)):

            @pl.when(jnp.logical_and(ahead >= 0, ahead < n_mp))
            def _():
                act(ahead, sem)

    ends(lambda ahead, sem: x_hop(z, ahead, sem).start())
    ends(lambda ahead, sem: start_all(all_w(z, ahead, sem, True)))

    def u_copy(to, source):
        return pltpu.make_async_remote_copy(
            bf_ref.at[source], bf_ref.at[source], u_send.at[to], u_recv.at[source], device_id=(d, to), device_id_type=MESH
        )

    for to in others:
        u_copy(to, z).start()

    def x_arrived(step):
        def act(block, ahead, more):
            x_hop(block, z, block).wait_recv()

            @pl.when(more)
            def _():
                x_hop(block, ahead, block).start()

        on_step(step, act)

    def plane_copy(w, place, shard, incoming):
        size = 2**place
        base = (labels[w] // size) * size
        if incoming:
            base = flip(base, place)
        part = gathered[w].at[shard, pl.ds(base, size)]
        return pltpu.make_async_remote_copy(
            part, part, p_send.at[w, place, shard], p_recv.at[w, place, shard],
            device_id=(flip(d, plans[w][place]), z), device_id_type=MESH,
        )

    def w_arrived(step):
        def act(block, ahead, more):
            for w in range(3):
                w_hop(w, block, z, block).wait_recv()

            @pl.when(more)
            def _():
                start_all(all_w(block, ahead, block))

            for w in range(3):
                plane_copy(w, 0, block, False).start()

        on_step(step, act)

    def plane_next(step, place):
        def act(block, ahead, more):
            for w in range(3):
                plane_copy(w, place - 1, block, True).wait_recv()
                plane_copy(w, place, block, False).start()

        on_step(step, act)

    def plane_done(step):
        def act(block, ahead, more):
            for w in range(3):
                plane_copy(w, depth - 1, block, True).wait_recv()

        on_step(step, act)

    tab = [
        jnp.broadcast_to(
            jnp.concatenate([tx_ref[h : h + 1, :].astype(F32), ty_ref[h : h + 1, :].astype(F32)], axis=1) * scale, (8, TILE)
        )
        for h in range(heads)
    ]
    bins_x = tx_ref.shape[1]
    pad = jnp.zeros((1, TILE - tp_ref.shape[1]), F32)
    ltab = [
        jnp.broadcast_to(jnp.concatenate([tp_ref[h : h + 1, :].astype(F32) * scale, pad], axis=1), (8, TILE))
        for h in range(heads)
    ]
    ci = lax.broadcasted_iota(jnp.int32, (8, TILE), 1)
    ri = lax.broadcasted_iota(jnp.int32, (8, TILE), 0)

    @pl.loop(0, TILE // 8)
    def _(g):
        at = pl.ds(pl.multiple_of(g * 8, 8), 8)
        for off in range(5):
            idx = line_bucket(ci - ri - g * 8 + (off - 2) * TILE)
            for h in range(heads):
                line_ref[h, off, at, :] = jnp.take_along_axis(ltab[h], idx, axis=1)

    place_ids = lax.broadcasted_iota(jnp.int32, (1, slot), 1)
    live = place_ids < 1 + PATCHES + len_ref[0]
    seen = jnp.where(live & ((km_ref[...].reshape(1, slot) == 1) | (place_ids == 0)), 0.0, -1e30)

    def bias_chunk(c):
        for copy in loads[c]:
            copy.wait()

        @pl.loop(0, TILE // 8)
        def _(g):
            at = pl.ds(pl.multiple_of(c * TILE + g * 8, 8), 8)
            near = pl.ds(pl.multiple_of(g * 8, 8), 8)
            for j in range(tiles):
                cols = slice(j * TILE, (j + 1) * TILE)
                ix = bx_ref[at, cols]
                iy = by_ref[at, cols] + bins_x
                hide = seen[:, cols]
                off = min(max(j - c + 2, 0), 4)
                for h in range(heads):
                    b = jnp.take_along_axis(tab[h], ix, axis=1) + jnp.take_along_axis(tab[h], iy, axis=1)
                    bias_ref[h, at, cols] = (b + line_ref[h, off, near, :]) + hide

    for c in range(tiles):
        if c == tiles // 2:
            x_arrived(1)
        bias_chunk(c)
    w_arrived(1)
    x_arrived(2)
    plane_next(1, 1)
    w_arrived(2)
    for place in range(2, depth):
        plane_next(1, place)
    x_arrived(3)

    lane = lax.broadcasted_iota(jnp.int32, (1, width), 1)
    mine = [(lane >= h * HEAD_DIM) & (lane < (h + 1) * HEAD_DIM) for h in range(heads)]
    b_q = bq_ref[...].astype(F32).reshape(1, width)
    b_v = bv_ref[...].astype(F32).reshape(1, width)
    for b in range(n_mp):
        at = pl.ds(b * rows, rows)
        xb = xf_ref[b]
        q_ref[at, :] = ((dot(xb, w_ref[0], 1, 1) + b_q).astype(BF16).astype(F32) * scale).astype(BF16)
        k_ref[at, :] = dot(xb, w_ref[1], 1, 1).astype(BF16)
        v_ref[at, :] = (dot(xb, w_ref[2], 1, 1) + b_v).astype(BF16)

    def c_copy(turn, to, source):
        return pltpu.make_async_remote_copy(
            cs_ref.at[turn], cr_ref.at[source], c_send.at[turn], c_recv.at[source], device_id=(d, to), device_id_type=MESH
        )

    def attend(turn):
        to = (z + 1 + turn) % n_mp
        at = pl.ds(pl.multiple_of(to * rows, rows), rows)
        q = q_ref[at, :]
        out = jnp.zeros((rows, width), F32)
        for h in range(heads):
            s = dot(jnp.where(mine[h], q, jnp.zeros((), BF16)), k_ref[...], 1, 1) + bias_ref[h, at, :]
            top = jnp.max(s, axis=1, keepdims=True)
            e = jnp.exp(s - top).astype(BF16)
            e_ref[h, at, :] = e
            inv = 1.0 / jnp.sum(e.astype(F32), axis=1, keepdims=True)
            inv_ref[at, h : h + 1] = inv
            out = out + jnp.where(mine[h], dot(e, v_ref[...], 1, 0) * inv, 0.0)
        if turn == n_mp - 1:
            cr_ref[z] = out.astype(BF16)
        else:
            cs_ref[turn] = out.astype(BF16)
            c_copy(turn, to, z).start()

    between = {0: lambda: plane_next(2, 1), 1: lambda: w_arrived(3)}
    for turn in range(n_mp):
        attend(turn)
        if turn in between:
            between[turn]()

    for place in range(2, depth):
        plane_next(2, place)
    for place in range(1, depth):
        plane_next(3, place)
    for step in range(1, n_mp):
        plane_done(step)

    for source in others:
        c_copy(0, z, source).wait_recv()
        u_copy(z, source).wait_recv()
    for turn in range(n_mp - 1):
        c_copy(turn, z, z).wait_send()
    for to in others:
        u_copy(to, z).wait_send()

    def wait_all(copies):
        for copy in copies:
            copy.wait_send()

    def sent(block, ahead, more):
        @pl.when(more)
        def _():
            wait_all([x_hop(block, ahead, block)] + all_w(block, ahead, block))

        for w in range(3):
            for place in range(depth):
                plane_copy(w, place, block, False).wait_send()

    ends(lambda ahead, sem: wait_all([x_hop(z, ahead, sem)] + all_w(z, ahead, sem, True)))
    for step in range(1, n_mp):
        on_step(step, sent)


def front(n_mp, n_dp, x, w_qkv, b_q, b_v, bx, by, t_x, t_y, t_pos, text_lens, key_mask, b_up, w_out, w_up, w_down):
    rows, wide = x.shape
    slot = bx.shape[0]
    width = w_qkv.shape[1]
    heads = width // HEAD_DIM
    plans = [gather_plan(n_dp, False), gather_plan(n_dp, False), gather_plan(n_dp, True)]
    depth = len(plans[0])
    slices = [w.reshape(n_dp, w.shape[0] // n_dp, w.shape[1]) for w in (w_out, w_up, w_down)]
    sds = jax.ShapeDtypeStruct
    dma = pltpu.SemaphoreType.DMA
    return pl.pallas_call(
        functools.partial(front_kernel, n_mp, n_dp, plans),
        out_shape=[
            sds((n_mp, rows, wide), BF16), sds((slot, width), BF16), sds((slot, width), BF16), sds((slot, width), BF16),
            sds((heads, slot, slot), BF16), sds((slot, heads), F32), sds((n_mp, rows, width), BF16),
            sds((n_mp, 8) + b_up.shape, F32),
        ] + [sds((n_mp,) + s.shape, BF16) for s in slices],
        in_specs=[VMEM] * 4 + [ANY, ANY] + [VMEM] * 3 + [pl.BlockSpec(memory_space=pltpu.SMEM), VMEM, VMEM] + [ANY] * 3,
        out_specs=[VMEM] * 8 + [ANY] * 3,
        scratch_shapes=[
            pltpu.VMEM((slot, slot), jnp.int32), pltpu.VMEM((slot, slot), jnp.int32), pltpu.VMEM((heads, slot, slot), F32),
            pltpu.VMEM((heads, 5, TILE, TILE), F32), pltpu.VMEM((n_mp - 1, rows, width), BF16),
            dma((2, slot // TILE)), dma((n_mp + 1,)), dma((n_mp,)), dma((n_mp - 1,)), dma((n_mp,)), dma((n_mp,)), dma((n_mp,)),
            dma((3, n_mp + 1)), dma((3, n_mp)), dma((3, depth, n_mp)), dma((3, depth, n_mp)),
        ],
        compiler_params=pltpu.CompilerParams(collective_id=0, has_side_effects=True, vmem_limit_bytes=BIG),
        name="front",
    )(x, w_qkv, b_q, b_v, bx, by, t_x, t_y, t_pos, text_lens, key_mask, b_up, *slices)

EPS = 1e-05
HI, LO, GROUP, STEP = 4, 16, 16, 2
PACK = 48


def sums_in_kernel(n_dp, *sizes):
    return all(size % (8 * n_dp) == 0 for size in sizes)


def gelu_parts(pre):
    cdf = 0.5 * (1.0 + lax.erf(pre * (0.5**0.5)))
    return (pre * cdf).astype(BF16), cdf + pre * (jnp.exp(-0.5 * pre * pre) * 0.3989422804014327)


def rear_kernel(
    n_mp, n_dp, plans, summed,
    x_ref, ctx_ref, bu_ref, ball_ref, bo_ref, ga_ref, na_ref, bd_ref, gf_ref, nf_gain_ref, cot_ref, len_ref,
    q_ref, k_ref, v_ref, e_ref, inv_ref, w_ref, xf_ref, wu_own, wd_own, wo_own, wo_hbm, wu_hbm, wd_hbm, bx_hbm, by_hbm,
    lo_ref, ig_ref, pack_ref, uo_ref, do_ref, qo_ref, oo_ref,
    wo_ref, wu_ref, wd_ref, gp_ref, wdo_ref, da_ref, gs_ref, dc_in, dc_ref, dt_ref, dn_ref, acc_ref, near_ref, part_ref, got_ref, bx_ref, by_ref,
    nf_ref, dff_ref, sp_ref,
    w_sem, b_sem, d_send, d_recv, r_send, r_recv, h_send, h_recv,
    *for_sums,
):
    if summed:
        (
            ua_ref, da2_ref, qa_ref, oa_ref, us_ref, ds2_ref, qs_ref, os_ref, ur_ref, dr_ref, qr_ref, or_ref, oz_ref, sr_ref, sz_ref,
            rs_send, rs_recv, ag_send, ag_recv, oz_send, oz_recv, sp_send, sp_recv, sz_send, sz_recv,
        ) = for_sums
    d = lax.axis_index("dp")
    z = lax.axis_index("mp")
    heads, slot, _ = e_ref.shape
    width = k_ref.shape[1]
    rows, wide = da_ref.shape
    tiles = slot // TILE
    scale = HEAD_DIM**-0.5
    others = [(z + k) % n_mp for k in range(1, n_mp)]
    depth = len(plans[0])

    weights = []
    for w, (own, rest, held) in enumerate(((wo_own, wo_hbm, wo_ref), (wu_own, wu_hbm, wu_ref), (wd_own, wd_hbm, wd_ref))):
        copies = [pltpu.make_async_copy(own, held.at[z], w_sem.at[w, z])]
        copies += [pltpu.make_async_copy(rest.at[s], held.at[s], w_sem.at[w, s]) for s in others]
        for copy in copies:
            copy.start()
        weights.append(copies)
    again = pltpu.make_async_copy(wd_own, wdo_ref, b_sem.at[2])
    again.start()
    loads = [pltpu.make_async_copy(bx_hbm, bx_ref, b_sem.at[0]), pltpu.make_async_copy(by_hbm, by_ref, b_sem.at[1])]
    for copy in loads:
        copy.start()
    loads.append(again)
    barrier = pltpu.get_barrier_semaphore()
    peers = [(d, to) for to in others] + [(flip(d, bit), z) for bit in plans[0] if summed]
    for peer in peers:
        pl.semaphore_signal(barrier, inc=1, device_id=peer, device_id_type=MESH)

    def remote(src, dst, send, recv, to):
        return pltpu.make_async_remote_copy(src, dst, send, recv, device_id=to, device_id_type=MESH)

    lines = (nf_ref, dff_ref)

    def hop(a, block, to, sem):
        return remote(lines[a].at[block], lines[a].at[block], h_send.at[a, sem], h_recv.at[a, block], (d, to))

    def ends(act):
        for ahead, sem in ((z + 1, z), (z - 1, n_mp)):

            @pl.when(jnp.logical_and(ahead >= 0, ahead < n_mp))
            def _():
                act(ahead, sem)

    def on_step(step, act):
        for block, ahead in ((z - step, z + 1), (z + step, z - 1)):

            @pl.when(jnp.logical_and(block >= 0, block < n_mp))
            def _():
                act(block, ahead, jnp.logical_and(ahead >= 0, ahead < n_mp))

    def arrived(a, step):
        def act(block, ahead, more):
            hop(a, block, z, block).wait_recv()

            @pl.when(more)
            def _():
                hop(a, block, ahead, block).start()

        on_step(step, act)

    def set_off(a):
        ends(lambda ahead, sem: hop(a, z, ahead, sem).start())

    items = ((None, None, None, plans[0]),) if not summed else (
        (ua_ref, us_ref, ur_ref, plans[0]), (da2_ref, ds2_ref, dr_ref, plans[1]), (qa_ref, qs_ref, qr_ref, plans[0]),
        (oa_ref, os_ref, or_ref, plans[1]),
    )
    outs = (uo_ref, do_ref, qo_ref, oo_ref)
    labels = [plan_label(d, item[3]) for item in items]

    def halves(i, place):
        size = 2**place
        base = (labels[i] // size) * size
        return pl.ds(base, size), pl.ds(flip(base, place), size), size

    def rs_copy(i, place):
        _, away, size = halves(i, place)
        _, staged, got, plan = items[i]
        return remote(staged.at[away], got.at[pl.ds(size, size)], rs_send.at[i, place], rs_recv.at[i, place], (flip(d, plan[place]), z))

    def rs_start(i, place):
        _, away, _ = halves(i, place)
        items[i][1][away] = items[i][0][away].astype(BF16)
        rs_copy(i, place).start()

    def ag_copy(i, place, incoming=False):
        kept, away, _ = halves(i, place)
        part = outs[i].at[away if incoming else kept]
        return remote(part, part, ag_send.at[i, place], ag_recv.at[i, place], (flip(d, items[i][3][place]), z))

    def oz_copy(to, source):
        return remote(os_ref.at[labels[3], to], oz_ref.at[source], oz_send.at[to], oz_recv.at[source], (d, to))

    stage = {}

    def begin(i):
        if summed:
            rs_start(i, depth - 1)
            stage[i] = ("halve", depth - 1)

    def onward(i):
        if not summed or stage[i] is None:
            return
        kind, place = stage[i]
        if kind == "halve":
            kept, _, size = halves(i, place)
            rs_copy(i, place).wait_recv()
            total, _, got, _ = items[i]
            total[kept] = total[kept] + got[size : 2 * size].astype(F32)
            if place:
                rs_start(i, place - 1)
                stage[i] = ("halve", place - 1)
            elif i == 3:
                os_ref[labels[3]] = oa_ref[labels[3]].astype(BF16)
                for to in others:
                    oz_copy(to, z).start()
                stage[i] = ("line", 0)
            else:
                outs[i][labels[i]] = total[labels[i]].astype(BF16)
                ag_copy(i, 0).start()
                stage[i] = ("gather", 0)
        elif kind == "line":
            out = oa_ref[labels[3], z]
            for source in others:
                oz_copy(z, source).wait_recv()
                out = out + oz_ref[source].astype(F32)
            oo_ref[labels[3]] = out.astype(BF16)
            ag_copy(3, 0).start()
            stage[i] = ("gather", 0)
        else:
            ag_copy(i, place, True).wait_recv()
            if place < depth - 1:
                ag_copy(i, place + 1).start()
                stage[i] = ("gather", place + 1)
            else:
                stage[i] = None

    def vec(ref):
        return ref[...].astype(F32).reshape(1, wide)

    def norm(values):
        spread = values - jnp.mean(values, axis=1, keepdims=True)
        rate = lax.rsqrt(jnp.mean(spread * spread, axis=1, keepdims=True) + EPS)
        return spread * rate, rate

    def norm_back(up, gain, hat, rate):
        scaled = up * gain
        first = jnp.mean(scaled, axis=1, keepdims=True)
        second = jnp.mean(scaled * hat, axis=1, keepdims=True)
        return rate * (scaled - first - hat * second)

    def total_rows(values):
        return jnp.sum(values, axis=0, keepdims=True)

    for copy in weights[0]:
        copy.wait()
    attn = dot(ctx_ref[0], wo_ref[0], 1, 0)
    for s in range(1, n_mp):
        attn = attn + dot(ctx_ref[s], wo_ref[s], 1, 0)
    hat_one, rate_one = norm(x_ref[...].astype(F32) + attn + vec(bo_ref))
    normed = hat_one * vec(ga_ref) + vec(na_ref)
    low = normed.astype(BF16)
    nf_ref[z] = low
    pl.semaphore_wait(barrier, len(peers))
    set_off(0)

    for copies in weights[1:]:
        for copy in copies:
            copy.wait()
    ffn = jnp.zeros((rows, wide), F32)
    for s in range(n_mp):
        act, slope = gelu_parts(dot(low, wu_ref[s], 1, 0) + ball_ref[s, 0:1, :])
        gp_ref[s] = slope
        ffn = ffn + dot(act, wd_ref[s], 1, 0)
    hat_two, rate_two = norm(normed + ffn + vec(bd_ref))
    lo_ref[...] = (hat_two * vec(gf_ref) + vec(nf_gain_ref)).astype(BF16)

    place_row = z * rows + lax.broadcasted_iota(jnp.int32, (rows, 1), 0)
    grad_y = jnp.where(place_row < 1 + PATCHES + len_ref[0], cot_ref[...].astype(F32), 0.0)
    d_two = norm_back(grad_y, vec(gf_ref), hat_two, rate_two)
    d_ffn = d_two.astype(BF16)
    dff_ref[z] = d_ffn
    set_off(1)
    arrived(0, 1)
    d_normed = d_two
    for s in range(n_mp):
        d_pre = (dot(d_ffn, wd_ref[s], 1, 1) * gp_ref[s]).astype(BF16)
        d_normed = d_normed + dot(d_pre, wu_ref[s], 1, 1)
    d_one = norm_back(d_normed, vec(ga_ref), hat_one, rate_one)
    da_ref[...] = d_one
    d_attn = d_one.astype(BF16)

    def d_copy(to, source):
        return remote(dc_in.at[to], dc_ref.at[source], d_send.at[to], d_recv.at[source], (d, to))

    for s in range(n_mp):
        dc_in[s] = dot(d_attn, wo_ref[s], 1, 1).astype(BF16)
    for to in others:
        d_copy(to, z).start()
    dc_ref[z] = dc_in[z]

    for s in range(n_mp):
        go = dot(ctx_ref[s].astype(F32).T.astype(BF16), d_attn, 1, 0)
        if summed:
            oa_ref[:, s] = go.reshape(n_dp, -1, wide)
        else:
            oo_ref[s] = go.astype(BF16)
    begin(3)
    gs_ref[...] = jnp.concatenate(
        [
            total_rows(grad_y * hat_two), total_rows(grad_y), total_rows(d_two), total_rows(d_normed * hat_one),
            total_rows(d_normed), total_rows(d_one), jnp.zeros((2, wide), F32),
        ],
        axis=0,
    )
    sp_ref[0:8, :] = gs_ref[...]

    def sz_copy(to, source):
        return remote(gs_ref, sz_ref.at[source], sz_send.at[to], sz_recv.at[source], (d, to))

    if summed:
        for to in others:
            sz_copy(to, z).start()

    lane = lax.broadcasted_iota(jnp.int32, (1, width), 1)
    mine = [(lane >= h * HEAD_DIM) & (lane < (h + 1) * HEAD_DIM) for h in range(heads)]
    zero = jnp.zeros((), BF16)
    factor = jnp.zeros((slot, width), F32)
    for h in range(heads):
        factor = jnp.where(mine[h], inv_ref[:, h : h + 1], factor)
    qt = q_ref[...].astype(F32).T.astype(BF16)
    arrived(0, 2)
    arrived(1, 1)
    onward(3)
    for source in others:
        d_copy(source, source).wait_recv()

    ds_ref = wd_ref
    dctx = dc_ref[...].reshape(slot, width)
    gt = (dctx.astype(F32) * factor).T.astype(BF16)
    block = 384
    dq = [None] * (slot // block)
    for h in range(heads):
        hs = slice(h * HEAD_DIM, (h + 1) * HEAD_DIM)
        dk = dv = None
        for r in range(slot // block):
            rs = slice(r * block, (r + 1) * block)
            e = e_ref[h, rs, :]
            p = e.astype(F32) * inv_ref[rs, h : h + 1]
            dp = dot(jnp.where(mine[h], dctx[rs, :], zero), v_ref[...], 1, 1)
            ds = (p * (dp - jnp.sum(p * dp, axis=1, keepdims=True))).astype(BF16)
            ds_ref[h, rs, :] = ds
            a = jnp.where(mine[h], dot(ds, k_ref[...], 1, 0), 0.0)
            dq[r] = a if dq[r] is None else dq[r] + a
            b = dot(qt[hs, rs], ds, 1, 0)
            dk = b if dk is None else dk + b
            c = dot(gt[hs, rs], e, 1, 0)
            dv = c if dv is None else dv + c
        dt_ref[1, hs, :] = dk.astype(BF16)
        dt_ref[2, hs, :] = dv.astype(BF16)
        if h == 0:
            arrived(1, 2)
        elif h == 1:
            arrived(0, 3)
    onward(3)
    for r in range(slot // block):
        rs = slice(r * block, (r + 1) * block)
        low_q = (dq[r] * scale).astype(BF16)
        dn_ref[0, rs, :] = low_q
        dt_ref[0, :, rs] = low_q.astype(F32).T.astype(BF16)
    for c in (1, 2):
        dn_ref[c] = dt_ref[c].astype(F32).T.astype(BF16)

    ones = jnp.ones((8, slot), BF16)
    xf = xf_ref[...].reshape(slot, wide)
    for c in range(3):
        gw = dot(dt_ref[c], xf, 1, 0)
        if summed:
            qa_ref[:, c] = gw.reshape(n_dp, -1, wide)
        else:
            qo_ref[c] = gw.astype(BF16)
    sp_ref[9:10, 0:width] = dot(ones, dn_ref[0], 1, 0)[0:1]
    sp_ref[10:11, 0:width] = dot(ones, dn_ref[2], 1, 0)[0:1]
    begin(2)
    onward(3)

    b_up = bu_ref[...].astype(F32).reshape(1, -1)
    last = heads
    for b in range(n_mp):
        act, slope = gelu_parts(dot(nf_ref[b], wu_ref[z], 1, 0) + b_up)
        wd_ref[last, b * rows : (b + 1) * rows, :] = act
        gp_ref[b] = slope
    onward(2)
    onward(3)
    arrived(1, 3)

    def keep(i, values):
        if summed:
            items[i][0][...] = values.reshape(n_dp, -1, values.shape[1])
        else:
            outs[i][0] = values.astype(BF16)

    for copy in loads:
        copy.wait()
    dff = dff_ref[...].reshape(slot, wide)
    act_ref = wd_ref.at[last]
    keep(1, dot(act_ref[...], dff, 0, 0))
    begin(1)
    act_ref[...] = (dot(dff, wdo_ref[...], 1, 1) * gp_ref[...].reshape(slot, -1)).astype(BF16)
    keep(0, dot(nf_ref[...].reshape(slot, wide), act_ref[...], 0, 0))
    begin(0)
    sp_ref[8:9, :] = dot(ones, act_ref[...], 1, 0)[0:1]

    def r_copy(turn, to, source):
        return remote(part_ref.at[turn], got_ref.at[turn], r_send.at[turn], r_recv.at[turn], (d, to))

    def dx_part(to):
        at = pl.ds(pl.multiple_of(to * rows, rows), rows)
        out = dot(dn_ref[0, at, :], w_ref[0], 1, 0)
        for c in (1, 2):
            out = out + dot(dn_ref[c, at, :], w_ref[c], 1, 0)
        return out

    for turn in range(n_mp - 1):
        part_ref[turn] = dx_part(others[turn]).astype(BF16)
        r_copy(turn, others[turn], z).start()
    da_ref[...] = da_ref[...] + dx_part(z)
    for i in (1, 0, 2, 3):
        onward(i)

    acc_ref[...] = jnp.zeros_like(acc_ref)
    one = jnp.ones((), BF16)

    def count(first, last_):
        @pl.loop(first, last_)
        def _(i):
            at = [pl.ds(pl.multiple_of(i * GROUP * STEP + g * GROUP, GROUP), GROUP) for g in range(STEP)]
            ds = [[ds_ref[h, at[g], :] for h in range(heads)] for g in range(STEP)]
            for t, b_ref in enumerate((bx_ref, by_ref)):
                tot = None
                for g in range(STEP):
                    b = b_ref[at[g], :]
                    hi = (b >> 4).astype(F32).astype(BF16)
                    lo = (b & 15).astype(F32).astype(BF16)
                    left = []
                    for a in range(HI):
                        m = hi == jnp.asarray(a, BF16)
                        left += [jnp.where(m, ds[g][h], zero) for h in range(heads)]
                    right = [jnp.where(lo == jnp.asarray(c, BF16), one, zero) for c in range(LO)]
                    o = dot(jnp.concatenate(left, 0), jnp.concatenate(right, 0), 1, 1)
                    tot = o if tot is None else tot + o
                acc_ref[t] += tot

    trips = slot // (GROUP * STEP)
    parts = 4
    for part in range(parts):
        count(part * trips // parts, (part + 1) * trips // parts)
        for i in (1, 0, 2, 3):
            onward(i)

    m, n = HI * heads * GROUP, LO * GROUP
    same = (lax.broadcasted_iota(jnp.int32, (m, n), 0) & (GROUP - 1)) == (lax.broadcasted_iota(jnp.int32, (m, n), 1) & (GROUP - 1))
    pick = (lax.broadcasted_iota(jnp.int32, (n, LO), 0) // GROUP == lax.broadcasted_iota(jnp.int32, (n, LO), 1)).astype(F32)
    for t in range(2):
        kept = jnp.sum(jnp.where(same, acc_ref[t], 0.0).reshape(m // GROUP, GROUP, n), axis=1)
        found = lax.dot_general(
            kept, pick, (((1,), (0,)), ((), ())), precision=lax.Precision.HIGHEST, preferred_element_type=F32
        )
        sp_ref[16 : 16 + HI * heads, t * TILE : t * TILE + LO] = found * scale

    for h in range(heads):
        for off in range(5):
            tot = jnp.zeros((TILE, TILE), F32)
            for i in range(tiles):
                for j in range(tiles):
                    if min(max(j - i, -2), 2) + 2 == off:
                        tot = tot + ds_ref[h, i * TILE : (i + 1) * TILE, j * TILE : (j + 1) * TILE].astype(F32)
            near_ref[h, off] = tot
    ci = lax.broadcasted_iota(jnp.int32, (TILE, TILE), 1)
    ri = lax.broadcasted_iota(jnp.int32, (TILE, TILE), 0)
    bins = 32
    half = bins // 2
    ids = [line_bucket(ci - ri + (off - 2) * TILE) for off in range(5)]
    for h in range(heads):
        found = []
        for b in range(bins):
            tot = None
            for off in range(5):
                if off in (1, 2, 3) and (off == 2 or (b >= half) == (off == 3)):
                    piece = jnp.where(ids[off] == b, near_ref[h, off], 0.0)
                elif off == 0 and b == half - 1 or off == 4 and b == bins - 1:
                    piece = near_ref[h, off]
                else:
                    continue
                tot = piece if tot is None else tot + piece
            found.append(jnp.sum(tot, axis=0, keepdims=True))
        line_sums = jnp.sum(jnp.concatenate(found, 0), axis=1, keepdims=True) * scale
        sp_ref[16 : 16 + bins, (2 + h) * TILE : (2 + h) * TILE + 1] = line_sums

    def sp_copy(place):
        return remote(sp_ref, sr_ref.at[place], sp_send.at[place], sp_recv.at[place], (flip(d, plans[0][place]), z))

    if summed:
        for source in others:
            sz_copy(z, source).wait_recv()
            sp_ref[0:8, :] = sp_ref[0:8, :] + sz_ref[source]
        for place in range(depth - 1, -1, -1):
            sp_copy(place).start()
            for i in (1, 0, 2, 3):
                onward(i)
            sp_copy(place).wait_send()
            sp_copy(place).wait_recv()
            sp_ref[...] = sp_ref[...] + sr_ref[place]
    pack_ref[...] = sp_ref[...]

    for turn in range(n_mp - 1):
        r_copy(turn, z, z).wait_recv()
        da_ref[...] = da_ref[...] + got_ref[turn].astype(F32)
    ig_ref[...] = da_ref[...].astype(BF16)

    while any(stage.values()):
        for i in (1, 0, 2, 3):
            onward(i)
    for turn in range(n_mp - 1):
        r_copy(turn, z, z).wait_send()
    for to in others:
        d_copy(to, z).wait_send()
    if summed:
        for to in others:
            sz_copy(to, z).wait_send()
            oz_copy(to, z).wait_send()
        for i in range(4):
            for place in range(depth):
                rs_copy(i, place).wait_send()
                ag_copy(i, place).wait_send()
    for a in range(2):
        ends(lambda ahead, sem: hop(a, z, ahead, sem).wait_send())

        def sent(block, ahead, more):
            @pl.when(more)
            def _():
                hop(a, block, ahead, block).wait_send()

        for step in range(1, n_mp):
            on_step(step, sent)


def rear(
    n_mp, n_dp, x, ctx, b_up, b_up_all, b_out, g_attn, n_attn, b_down, g_ffn, n_ffn, cotangent, text_lens,
    q, k, v, e, inv, w_t, xf, w_up, w_down, w_out, gathered, bx, by,
):
    heads, slot, _ = e.shape
    width = k.shape[1]
    rows, wide = x.shape
    units = w_up.shape[1]
    plans = [gather_plan(n_dp, False), gather_plan(n_dp, True)]
    depth = len(plans[0])
    summed = sums_in_kernel(n_dp, width, units, wide)
    if summed:
        ru, rd, ro = wide // n_dp, units // n_dp, width // n_dp
        shapes = [(n_dp, ru, units), (n_dp, rd, wide), (n_dp, 3, ro, wide), (n_dp, ro, wide)]
    else:
        shapes = [(1, wide, units), (1, units, wide), (3, width, wide), (n_mp, width, wide)]
    sds = jax.ShapeDtypeStruct
    dma = pltpu.SemaphoreType.DMA
    vm = pltpu.VMEM
    sums = []
    if summed:
        whole = [(n_dp, ru, units), (n_dp, rd, wide), (n_dp, 3, ro, wide), (n_dp, n_mp, ro, wide)]
        sums = [vm(shape, F32) for shape in whole] + 2 * [vm(shape, BF16) for shape in whole]
        sums += [vm((n_mp, ro, wide), BF16), vm((depth, PACK, wide), F32), vm((n_mp, 8, wide), F32)]
        sums += [dma((4, depth))] * 4 + [dma((n_mp,))] * 2 + [dma((depth,))] * 2 + [dma((n_mp,))] * 2
    return pl.pallas_call(
        functools.partial(rear_kernel, n_mp, n_dp, plans, summed),
        out_shape=[sds((rows, wide), BF16), sds((rows, wide), BF16), sds((PACK, wide), F32)] + [sds(shape, BF16) for shape in shapes],
        in_specs=[VMEM] * 11 + [pl.BlockSpec(memory_space=pltpu.SMEM)] + [VMEM] * 7 + [ANY] * 8,
        out_specs=[VMEM] * 7,
        scratch_shapes=[
            vm((n_mp, width, wide), BF16), vm((n_mp, wide, units), BF16), vm((n_mp, units, wide), BF16), vm((n_mp, rows, units), F32),
            vm((units, wide), BF16), vm((rows, wide), F32), vm((8, wide), F32), vm((n_mp, rows, width), BF16), vm((n_mp, rows, width), BF16),
            vm((3, width, slot), BF16), vm((3, slot, width), BF16),
            vm((2, HI * heads * GROUP, LO * GROUP), F32), vm((heads, 5, TILE, TILE), F32), vm((n_mp - 1, rows, wide), BF16),
            vm((n_mp - 1, rows, wide), BF16), vm((slot, slot), jnp.int32), vm((slot, slot), jnp.int32),
            vm((n_mp, rows, wide), BF16), vm((n_mp, rows, wide), BF16), vm((PACK, wide), F32),
            dma((3, n_mp)), dma((3,)), dma((n_mp,)), dma((n_mp,)), dma((n_mp - 1,)), dma((n_mp - 1,)), dma((2, n_mp + 1)), dma((2, n_mp)),
        ] + sums,
        compiler_params=pltpu.CompilerParams(collective_id=1, has_side_effects=True, vmem_limit_bytes=62 << 20),
        name="rear",
    )(
        x, ctx, b_up, b_up_all, b_out, g_attn, n_attn, b_down, g_ffn, n_ffn, cotangent, text_lens,
        q, k, v, e, inv, w_t, xf, w_up, w_down, w_out, *gathered, bx, by,
    )


def layer(n_mp, n_dp):
    def on_device(
        hidden_in, text_lens, key_mask, bucket_x, bucket_y, w_qkv, b_q, b_v, w_out, b_out, g_attn, n_attn,
        w_up, b_up, w_down, b_down, g_ffn, n_ffn, t_pos, t_x, t_y, cotangent,
    ):
        rows, wide = hidden_in.shape
        slot = bucket_x.shape[1]
        width = w_qkv.shape[2]
        heads = width // HEAD_DIM
        bx, by = bucket_x[0], bucket_y[0]
        w_t = jnp.transpose(w_qkv, (0, 2, 1))
        xf, q, k, v, e, inv, ctx, b_up_all, wo, wu, wd = front(
            n_mp, n_dp, hidden_in, w_t, b_q, b_v, bx, by, t_x, t_y, t_pos, text_lens, key_mask, b_up, w_out, w_up, w_down
        )
        gathered = (wo.reshape((n_mp,) + w_out.shape), wu.reshape((n_mp,) + w_up.shape), wd.reshape((n_mp,) + w_down.shape))
        layer_out, input_grad, pack, g_up, g_down, g_qkv, g_out = rear(
            n_mp, n_dp, hidden_in, ctx, b_up, b_up_all, b_out, g_attn, n_attn, b_down, g_ffn, n_ffn, cotangent, text_lens,
            q, k, v, e, inv, w_t, xf, w_up, w_down, w_out, gathered, bx, by,
        )

        if sums_in_kernel(n_dp, width, w_up.shape[1], wide):
            g_qkv = jnp.transpose(g_qkv, (1, 0, 2, 3))
        else:
            g_out = lax.psum_scatter(g_out.reshape(-1, wide), "mp", scatter_dimension=0, tiled=True)
            g_up, g_down, g_qkv, g_out, pack = lax.psum((g_up, g_down, g_qkv, g_out, pack), "dp")
            pack = jnp.concatenate([lax.psum(pack[:8], "mp"), pack[8:]], axis=0)
        grad_w_up = g_up.reshape(w_up.shape).astype(F32)
        grad_w_down = g_down.reshape(w_down.shape).astype(F32)
        grad_w_out = g_out.reshape(w_out.shape).astype(F32)
        grad_w_qkv = jnp.transpose(g_qkv.reshape(3, width, wide).astype(F32), (0, 2, 1))
        grad_g_ffn, grad_n_ffn, grad_b_down, grad_g_attn, grad_n_attn, grad_b_out, _, _, grad_b_up = [pack[i] for i in range(9)]
        grad_b_q, grad_b_v = pack[9, :width], pack[10, :width]
        tables = [
            pack[16 : 16 + HI * heads, t * TILE : t * TILE + LO].reshape(HI, heads, LO).transpose(1, 0, 2).reshape(heads, HI * LO)
            for t in range(2)
        ]
        grad_t_pos = jnp.stack([pack[16:, (2 + h) * TILE] for h in range(heads)])
        return (
            layer_out, input_grad, grad_w_qkv, grad_b_q, grad_b_v, grad_w_out, grad_b_out, grad_g_attn, grad_n_attn,
            grad_w_up, grad_b_up, grad_w_down, grad_b_down, grad_g_ffn, grad_n_ffn, grad_t_pos, tables[0], tables[1],
        )

    return on_device


def solution(mesh):
    both, split = P(("dp", "mp"), None), P("mp")
    rows_mp, cols_mp, qkv = P("mp", None), P(None, "mp"), P(None, None, "mp")
    doc = P("dp", None, None)
    return jax.shard_map(
        layer(mesh.shape["mp"], mesh.shape["dp"]),
        mesh=mesh,
        in_specs=(
            both, P("dp"), P("dp"), doc, doc, qkv, split, split, rows_mp, P(), P(), P(), cols_mp, split, rows_mp, P(), P(), P(),
            rows_mp, rows_mp, rows_mp, both,
        ),
        out_specs=(
            both, both, qkv, split, split, rows_mp, P(), P(), P(), cols_mp, split, rows_mp, P(), P(), P(), rows_mp, rows_mp, rows_mp,
        ),
        check_vma=False,
    )
```

```python
import functools
import jax
import jax.numpy as jnp
from jax import lax
from jax.experimental import pallas as pl
from jax.experimental.pallas import tpu as pltpu
from jax.sharding import PartitionSpec as P

HEAD_DIM = 64
PATCHES = 196
THRESHOLDS = (12, 16, 23, 32, 46, 64, 91)
TILE = 128
F32, BF16 = jnp.float32, jnp.bfloat16
MESH = pl.DeviceIdType.MESH
VMEM = pl.BlockSpec(memory_space=pltpu.VMEM)
ANY = pl.BlockSpec(memory_space=pl.ANY)
BIG = 58 << 20


def line_bucket(off):
    mag = jnp.abs(off)
    far = jnp.full(off.shape, 8, jnp.int32)
    for border in THRESHOLDS:
        far = far + (mag >= border).astype(jnp.int32)
    return jnp.where(off > 0, 16, 0) + jnp.where(mag < 8, mag, far)


def dot(a, b, ca, cb):
    return lax.dot_general(a, b, (((ca,), (cb,)), ((), ())), preferred_element_type=F32)


def flip(index, bit):
    step = 2**bit
    return index + step * (1 - 2 * ((index // step) % 2))


SLICES = 8
EPS = 1e-05
HI, LO, GROUP, STEP = 4, 16, 16, 2


def plane_bits(dp_size):
    chips = list(range(1, dp_size.bit_length() - 1))
    used = SLICES.bit_length() - 2
    return chips[:used], chips[used:]


def plan_label(index, plan):
    label = 0
    for place, bit in enumerate(plan):
        label = label + ((index // 2**bit) % 2) * 2**place
    return label


def gelu_parts(pre):
    cdf = 0.5 * (1.0 + lax.erf(pre * (0.5**0.5)))
    return (pre * cdf).astype(BF16), cdf + pre * (jnp.exp(-0.5 * pre * pre) * 0.3989422804014327)


def layer_kernel(
    n_mp, plans, extra,
    x_ref, w_ref, bq_ref, bv_ref, tx_ref, ty_ref, tp_ref, km_ref, bu_ref, bo_ref, ga_ref, na_ref, bd_ref, gf_ref, nn_ref, cot_ref,
    len_ref, bx_hbm, by_hbm, wo_src, wu_src, wd_src,
    lo_ref, ig_ref, pack_ref, tab_out, uo_ref, do_ref, qo_ref, oo_ref,
    xf_ref, q_ref, k_ref, v_ref, e_ref, inv_ref, cr_ref, ball_ref, bx_ref, by_ref, bias_ref, line_ref, wo_ref, wu_ref, wd_ref,
    da_ref, ffn_ref, gs_ref, di_ref, dc_ref, qt_ref, gt_ref, dq_ref, dt_ref, dn_ref, acc_ref, got_ref, nf_ref, dff_ref,
    sp_ref, st_ref, sr_ref, sv_ref, sz_ref, qa_ref, oa_ref, qs_ref, ur_ref, dr_ref, qr_ref, or_ref, oy_ref, oz_ref, ux_ref, dx_ref, qx_ref, ox_ref,
    own_sem, b_sem, x_send, x_recv, c_send, c_recv, u_send, u_recv, z_send, z_recv, p_send, p_recv,
    d_send, d_recv, r_send, r_recv, h_send, h_recv, rs_send, rs_recv, ag_send, ag_recv, ex_send, ex_recv, oz_send, oz_recv,
    sp_send, sp_recv, sz_send, sz_recv,
):
    d = lax.axis_index("dp")
    z = lax.axis_index("mp")
    rows, wide = x_ref.shape
    slot = bx_ref.shape[0]
    width = w_ref.shape[1]
    heads = width // HEAD_DIM
    tiles = slot // TILE
    units = wu_ref.shape[3]
    scale = HEAD_DIM**-0.5
    sources = (wo_src, wu_src, wd_src)
    gathered = (wo_ref, wu_ref, wd_ref)
    others = [(z + k) % n_mp for k in range(1, n_mp)]
    depth = len(plans[0])
    labels = [plan_label(d, plan) for plan in plans]
    w_plan = (0, 0, 1)

    def remote(src, dst, send, recv, to):
        return pltpu.make_async_remote_copy(src, dst, send, recv, device_id=to, device_id_type=MESH)

    loads = []
    for c in range(tiles):
        part = pl.ds(c * TILE, TILE)
        pair = (
            pltpu.make_async_copy(bx_hbm.at[part], bx_ref.at[part], b_sem.at[0, c]),
            pltpu.make_async_copy(by_hbm.at[part], by_ref.at[part], b_sem.at[1, c]),
        )
        for copy in pair:
            copy.start()
        loads.append(pair)

    barrier = pltpu.get_barrier_semaphore()
    peers = [(d, to) for to in others] + [(flip(d, bit), z) for bit in plans[0] + extra]
    for peer in peers:
        pl.semaphore_signal(barrier, inc=1, device_id=peer, device_id_type=MESH)
    xf_ref[z] = x_ref[...]
    ball_ref[z] = jnp.broadcast_to(bu_ref[...].astype(F32).reshape(1, -1), ball_ref.shape[1:])
    pl.semaphore_wait(barrier, len(peers))

    def on_step(step, act):
        for block, ahead in ((z - step, z + 1), (z + step, z - 1)):

            @pl.when(jnp.logical_and(block >= 0, block < n_mp))
            def _():
                act(block, ahead, jnp.logical_and(ahead >= 0, ahead < n_mp))

    def ends(act):
        for ahead, sem in ((z + 1, z), (z - 1, n_mp)):

            @pl.when(jnp.logical_and(ahead >= 0, ahead < n_mp))
            def _():
                act(ahead, sem)

    def start_all(copies):
        for copy in copies:
            copy.start()

    def x_hop(block, to, sem):
        return remote(xf_ref.at[block], xf_ref.at[block], x_send.at[sem], x_recv.at[block], (d, to))

    def w_hop(w, block, to, sem, own=False):
        label = labels[w_plan[w]]
        held = sources[w].at[label] if own else gathered[w].at[block, label]
        return remote(held, gathered[w].at[block, label], z_send.at[w, sem], z_recv.at[w, block], (d, to))

    def all_w(block, to, sem, own=False):
        return [w_hop(w, block, to, sem, own) for w in range(3)]

    ends(lambda ahead, sem: x_hop(z, ahead, sem).start())
    ends(lambda ahead, sem: start_all(all_w(z, ahead, sem, True)))

    def u_copy(to, source):
        return remote(ball_ref.at[source], ball_ref.at[source], u_send.at[to], u_recv.at[source], (d, to))

    for to in others:
        u_copy(to, z).start()
    own = [pltpu.make_async_copy(sources[w], gathered[w].at[z], own_sem.at[w]) for w in range(3)]
    start_all(own)

    def x_arrived(step):
        def act(block, ahead, more):
            x_hop(block, z, block).wait_recv()

            @pl.when(more)
            def _():
                x_hop(block, ahead, block).start()

        on_step(step, act)

    def plane_copy(w, place, shard, incoming):
        plan = w_plan[w]
        size = 2**place
        base = (labels[plan] // size) * size
        if incoming:
            base = flip(base, place)
        part = gathered[w].at[shard, pl.ds(base, size)]
        return remote(part, part, p_send.at[w, place, shard], p_recv.at[w, place, shard], (flip(d, plans[plan][place]), z))

    def w_arrived(step):
        def act(block, ahead, more):
            for w in range(3):
                w_hop(w, block, z, block).wait_recv()

            @pl.when(more)
            def _():
                start_all(all_w(block, ahead, block))

            for w in range(3):
                plane_copy(w, 0, block, False).start()

        on_step(step, act)

    def plane_next(step, place, which=(0, 1, 2)):
        def act(block, ahead, more):
            for w in which:
                plane_copy(w, place - 1, block, True).wait_recv()
                plane_copy(w, place, block, False).start()

        on_step(step, act)

    def plane_done(step, which):
        def act(block, ahead, more):
            for w in which:
                plane_copy(w, depth - 1, block, True).wait_recv()

        on_step(step, act)

    tab = [
        jnp.broadcast_to(
            jnp.concatenate([tx_ref[h : h + 1, :].astype(F32), ty_ref[h : h + 1, :].astype(F32)], axis=1) * scale, (8, TILE)
        )
        for h in range(heads)
    ]
    bins_x = tx_ref.shape[1]
    bins = tp_ref.shape[1]
    pad = jnp.zeros((1, TILE - bins), F32)
    ltab = [
        jnp.broadcast_to(jnp.concatenate([tp_ref[h : h + 1, :].astype(F32) * scale, pad], axis=1), (8, TILE))
        for h in range(heads)
    ]
    ci = lax.broadcasted_iota(jnp.int32, (8, TILE), 1)
    ri = lax.broadcasted_iota(jnp.int32, (8, TILE), 0)

    @pl.loop(0, TILE // 8)
    def _(g):
        at = pl.ds(pl.multiple_of(g * 8, 8), 8)
        for off in range(5):
            idx = line_bucket(ci - ri - g * 8 + (off - 2) * TILE)
            for h in range(heads):
                line_ref[h, off, at, :] = jnp.take_along_axis(ltab[h], idx, axis=1)

    place_ids = lax.broadcasted_iota(jnp.int32, (1, slot), 1)
    live = place_ids < 1 + PATCHES + len_ref[0]
    seen = jnp.where(live & ((km_ref[...].reshape(1, slot) == 1) | (place_ids == 0)), 0.0, -1e30)

    def bias_chunk(c):
        for copy in loads[c]:
            copy.wait()

        @pl.loop(0, TILE // 8)
        def _(g):
            at = pl.ds(pl.multiple_of(c * TILE + g * 8, 8), 8)
            near = pl.ds(pl.multiple_of(g * 8, 8), 8)
            for j in range(tiles):
                cols = slice(j * TILE, (j + 1) * TILE)
                ix = bx_ref[at, cols]
                iy = by_ref[at, cols] + bins_x
                hide = seen[:, cols]
                off = min(max(j - c + 2, 0), 4)
                for h in range(heads):
                    b = jnp.take_along_axis(tab[h], ix, axis=1) + jnp.take_along_axis(tab[h], iy, axis=1)
                    bias_ref[h, at, cols] = (b + line_ref[h, off, near, :]) + hide

    for c in range(tiles):
        if c == tiles // 2:
            x_arrived(1)
        bias_chunk(c)
    w_arrived(1)
    x_arrived(2)
    plane_next(1, 1)
    w_arrived(2)
    for place in range(2, depth):
        plane_next(1, place)
    x_arrived(3)

    lane = lax.broadcasted_iota(jnp.int32, (1, width), 1)

    def mine(h):
        return (lane >= h * HEAD_DIM) & (lane < (h + 1) * HEAD_DIM)

    zero = jnp.zeros((), BF16)
    b_q = bq_ref[...].astype(F32).reshape(1, width)
    b_v = bv_ref[...].astype(F32).reshape(1, width)

    @pl.loop(0, n_mp)
    def _(b):
        at = pl.ds(pl.multiple_of(b * rows, rows), rows)
        xb = xf_ref[b]
        q_ref[at, :] = ((dot(xb, w_ref[0], 1, 1) + b_q).astype(BF16).astype(F32) * scale).astype(BF16)
        k_ref[at, :] = dot(xb, w_ref[1], 1, 1).astype(BF16)
        v_ref[at, :] = (dot(xb, w_ref[2], 1, 1) + b_v).astype(BF16)

    def c_copy(turn, to, source):
        return remote(di_ref.at[turn], cr_ref.at[source], c_send.at[turn], c_recv.at[source], (d, to))

    @pl.loop(0, n_mp)
    def _(turn):
        to = (z + 1 + turn) % n_mp
        at = pl.ds(pl.multiple_of(to * rows, rows), rows)
        q = q_ref[at, :]
        out = jnp.zeros((rows, width), F32)
        for h in range(heads):
            s = dot(jnp.where(mine(h), q, zero), k_ref[...], 1, 1) + bias_ref[h, at, :]
            top = jnp.max(s, axis=1, keepdims=True)
            e = jnp.exp(s - top).astype(BF16)
            e_ref[h, at, :] = e
            inv = 1.0 / jnp.sum(e.astype(F32), axis=1, keepdims=True)
            inv_ref[h, at, :] = inv
            out = out + jnp.where(mine(h), dot(e, v_ref[...], 1, 0) * inv, 0.0)
        low = out.astype(BF16)

        @pl.when(turn == n_mp - 1)
        def _():
            cr_ref[z] = low

        @pl.when(turn < n_mp - 1)
        def _():
            di_ref[turn] = low
            c_copy(turn, to, z).start()

        @pl.when(turn == 0)
        def _():
            plane_next(2, 1)

        @pl.when(turn == 1)
        def _():
            w_arrived(3)

    for place in range(2, depth):
        plane_next(2, place)
    for place in range(1, depth):
        plane_next(3, place, (0,))
        if place == 1:
            plane_next(3, 1, (1, 2))
    for step in range(1, n_mp):
        plane_done(step, (0,))
    own[0].wait()
    for source in others:
        c_copy(0, z, source).wait_recv()
    for turn in range(n_mp - 1):
        c_copy(turn, z, z).wait_send()

    lines = (nf_ref, dff_ref)

    def hop(a, block, to, sem):
        return remote(lines[a].at[block], lines[a].at[block], h_send.at[a, sem], h_recv.at[a, block], (d, to))

    def arrived(a, step):
        def act(block, ahead, more):
            hop(a, block, z, block).wait_recv()

            @pl.when(more)
            def _():
                hop(a, block, ahead, block).start()

        on_step(step, act)

    def set_off(a):
        ends(lambda ahead, sem: hop(a, z, ahead, sem).start())

    def vec(ref):
        return ref[...].astype(F32).reshape(1, wide)

    def norm(values):
        spread = values - jnp.mean(values, axis=1, keepdims=True)
        rate = lax.rsqrt(jnp.mean(spread * spread, axis=1, keepdims=True) + EPS)
        return spread * rate, rate

    def norm_back(up, gain, hat, rate):
        scaled = up * gain
        first = jnp.mean(scaled, axis=1, keepdims=True)
        second = jnp.mean(scaled * hat, axis=1, keepdims=True)
        return rate * (scaled - first - hat * second)

    def total_rows(values):
        return jnp.sum(values, axis=0, keepdims=True)

    def slab(ref, s):
        return ref[s].reshape(-1, wide)

    attn = dot(cr_ref[0], slab(wo_ref, 0), 1, 0)
    for s in range(1, n_mp):
        attn = attn + dot(cr_ref[s], slab(wo_ref, s), 1, 0)
    hat_one, rate_one = norm(x_ref[...].astype(F32) + attn + vec(bo_ref))
    normed = hat_one * vec(ga_ref) + vec(na_ref)
    low_own = normed.astype(BF16)
    nf_ref[z] = low_own
    set_off(0)

    for place in range(2, depth):
        plane_next(3, place, (1, 2))
    for step in range(1, n_mp):
        plane_done(step, (1, 2))
    for w in (1, 2):
        own[w].wait()
    for source in others:
        u_copy(z, source).wait_recv()

    slope_at = heads - 1
    ffn_ref[...] = jnp.zeros_like(ffn_ref)

    @pl.loop(0, n_mp)
    def _(s):
        at = pl.ds(pl.multiple_of(s * rows, rows), rows)
        act, slope = gelu_parts(dot(nf_ref[z], slab(wu_ref, s), 1, 0) + ball_ref[s, 0:1, :])
        bias_ref[slope_at, at, :] = slope
        ffn_ref[...] += dot(act, slab(wd_ref, s), 1, 0)

        @pl.when(s == n_mp - 1)
        def _():
            arrived(0, 1)

    hat_two, rate_two = norm(normed + ffn_ref[...] + vec(bd_ref))
    lo_ref[...] = (hat_two * vec(gf_ref) + vec(nn_ref)).astype(BF16)

    place_row = z * rows + lax.broadcasted_iota(jnp.int32, (rows, 1), 0)
    grad_y = jnp.where(place_row < 1 + PATCHES + len_ref[0], cot_ref[...].astype(F32), 0.0)
    d_two = norm_back(grad_y, vec(gf_ref), hat_two, rate_two)
    dff_ref[z] = d_two.astype(BF16)
    set_off(1)
    ffn_ref[...] = d_two

    @pl.loop(0, n_mp)
    def _(s):
        at = pl.ds(pl.multiple_of(s * rows, rows), rows)
        d_pre = (dot(dff_ref[z], slab(wd_ref, s), 1, 1) * bias_ref[slope_at, at, :]).astype(BF16)
        ffn_ref[...] += dot(d_pre, slab(wu_ref, s), 1, 1)

    d_normed = ffn_ref[...]
    d_one = norm_back(d_normed, vec(ga_ref), hat_one, rate_one)
    da_ref[...] = d_one
    d_attn = d_one.astype(BF16)

    def d_copy(to, source):
        return remote(di_ref.at[to], dc_ref.at[source], d_send.at[to], d_recv.at[source], (d, to))

    for s in range(n_mp):
        di_ref[s] = dot(d_attn, slab(wo_ref, s), 1, 1).astype(BF16)
    for to in others:
        d_copy(to, z).start()
    dc_ref[z] = di_ref[z]
    arrived(0, 2)

    def wait_all(copies):
        for copy in copies:
            copy.wait_send()

    def sent(block, ahead, more):
        @pl.when(more)
        def _():
            wait_all([x_hop(block, ahead, block)] + all_w(block, ahead, block))

        for w in range(3):
            for place in range(depth):
                plane_copy(w, place, block, False).wait_send()

    ends(lambda ahead, sem: wait_all([x_hop(z, ahead, sem)] + all_w(z, ahead, sem, True)))
    for step in range(1, n_mp):
        on_step(step, sent)
    for to in others:
        u_copy(to, z).wait_send()

    per_u = wide // SLICES

    def flat(slab_index):
        def at(base, size):
            return bias_ref.at[slab_index, pl.ds(pl.multiple_of(base * per_u, per_u), size * per_u)]

        return at

    def lead(ref):
        return lambda base, size: ref.at[pl.ds(base, size)]

    def inside(ref, s):
        return lambda base, size: ref.at[s, pl.ds(base, size)]

    totals = (flat(0), flat(1), lead(qa_ref), lead(oa_ref))
    staged = (inside(wu_ref, others[0]), inside(wu_ref, others[1]), lead(qs_ref), inside(wu_ref, others[2]))
    taken = (ur_ref, dr_ref, qr_ref, or_ref)
    beyond = (ux_ref, dx_ref, qx_ref, ox_ref)
    outs = (uo_ref, do_ref, qo_ref, oo_ref)
    item_plan = (0, 1, 0, 1)

    def own_label(i):
        return labels[item_plan[i]]

    def halves(i, place):
        size = 2**place
        base = (own_label(i) // size) * size
        return base, flip(base, place), size

    def partner(i, place):
        return (flip(d, plans[item_plan[i]][place]), z)

    def rs_copy(i, place):
        _, away, size = halves(i, place)
        return remote(
            staged[i](away, size), taken[i].at[pl.ds(size, size)], rs_send.at[i, place], rs_recv.at[i, place], partner(i, place)
        )

    def rs_start(i, place):
        _, away, size = halves(i, place)
        target = staged[i](away, size)
        target[...] = totals[i](away, size)[...].astype(BF16).reshape(target.shape)
        rs_copy(i, place).start()

    def ex_copy(i, turn):
        return remote(
            staged[i](own_label(i), 1), beyond[i].at[pl.ds(turn, 1)], ex_send.at[i, turn], ex_recv.at[i, turn],
            (flip(d, extra[turn]), z),
        )

    def ex_start(i, turn):
        target = staged[i](own_label(i), 1)
        target[...] = totals[i](own_label(i), 1)[...].astype(BF16).reshape(target.shape)
        ex_copy(i, turn).start()

    def ag_copy(i, place, incoming=False):
        base, away, size = halves(i, place)
        part = outs[i].at[pl.ds(away if incoming else base, size)]
        return remote(part, part, ag_send.at[i, place], ag_recv.at[i, place], partner(i, place))

    def oz_copy(to, source):
        return remote(oy_ref.at[to], oz_ref.at[source], oz_send.at[to], oz_recv.at[source], (d, to))

    stage = {}

    def begin(i):
        rs_start(i, depth - 1)
        stage[i] = ("halve", depth - 1)

    def spread(i):
        if i == 3:
            per = oy_ref.shape[1]
            for s in range(n_mp):
                oy_ref[s] = oa_ref[own_label(3), s * per : (s + 1) * per, :].astype(BF16)
            for to in others:
                oz_copy(to, z).start()
            stage[i] = ("line", 0)
        else:
            outs[i][own_label(i)] = totals[i](own_label(i), 1)[...].astype(BF16).reshape(outs[i].shape[1:])
            ag_copy(i, 0).start()
            stage[i] = ("gather", 0)

    def onward(*which):
        for i in which:
            if stage[i] is None:
                continue
            kind, place = stage[i]
            if kind == "halve":
                kept, _, size = halves(i, place)
                rs_copy(i, place).wait_recv()
                total = totals[i](kept, size)
                total[...] = total[...] + taken[i][size : 2 * size].astype(F32).reshape(total.shape)
                if place:
                    rs_start(i, place - 1)
                    stage[i] = ("halve", place - 1)
                elif extra:
                    ex_start(i, 0)
                    stage[i] = ("swap", 0)
                else:
                    spread(i)
            elif kind == "swap":
                ex_copy(i, place).wait_send()
                ex_copy(i, place).wait_recv()
                total = totals[i](own_label(i), 1)
                total[...] = total[...] + beyond[i][place : place + 1].astype(F32).reshape(total.shape)
                if place < len(extra) - 1:
                    ex_start(i, place + 1)
                    stage[i] = ("swap", place + 1)
                else:
                    spread(i)
            elif kind == "line":
                per = oz_ref.shape[1]
                out = oa_ref[own_label(3), pl.ds(pl.multiple_of(z * per, per), per), :]
                for source in others:
                    oz_copy(z, source).wait_recv()
                    out = out + oz_ref[source].astype(F32)
                oo_ref[own_label(3)] = out.astype(BF16)
                ag_copy(3, 0).start()
                stage[i] = ("gather", 0)
            else:
                ag_copy(i, place, True).wait_recv()
                if place < depth - 1:
                    ag_copy(i, place + 1).start()
                    stage[i] = ("gather", place + 1)
                else:
                    stage[i] = None

    per_o = width // SLICES
    for s in range(n_mp):
        go = dot(cr_ref[s].astype(F32).T.astype(BF16), d_attn, 1, 0)
        oa_ref[:, s * per_o : (s + 1) * per_o, :] = go.reshape(SLICES, per_o, wide)
    begin(3)
    gs_ref[...] = jnp.concatenate(
        [
            total_rows(grad_y * hat_two), total_rows(grad_y), total_rows(d_two), total_rows(d_normed * hat_one),
            total_rows(d_normed), total_rows(d_one), jnp.zeros((2, wide), F32),
        ],
        axis=0,
    )
    sp_ref[0:8, :] = gs_ref[...]

    def sz_copy(to, source):
        return remote(gs_ref, sz_ref.at[source], sz_send.at[to], sz_recv.at[source], (d, to))

    for to in others:
        sz_copy(to, z).start()

    factor = jnp.zeros((slot, width), F32)
    for h in range(heads):
        factor = jnp.where(mine(h), inv_ref[h], factor)
    qt_ref[...] = q_ref[...].astype(F32).T.astype(BF16)
    arrived(1, 1)
    onward(3)
    for source in others:
        d_copy(source, source).wait_recv()

    gt_ref[...] = (dc_ref[...].reshape(slot, width).astype(F32) * factor).T.astype(BF16)
    dq_ref[...] = jnp.zeros_like(dq_ref)
    block = slot // 2
    groups = block // rows

    def score_slab(h):
        return (z + 1 + h) % n_mp

    @pl.loop(0, heads)
    def _(h):
        hs = pl.ds(pl.multiple_of(h * HEAD_DIM, HEAD_DIM), HEAD_DIM)
        dk = dv = None
        for r in range(slot // block):
            rs = slice(r * block, (r + 1) * block)
            e = e_ref[h, rs, :]
            p = e.astype(F32) * inv_ref[h, rs, :]
            up = dc_ref[r * groups : (r + 1) * groups].reshape(block, width)
            dp = dot(jnp.where(mine(h), up, zero), v_ref[...], 1, 1)
            ds = (p * (dp - jnp.sum(p * dp, axis=1, keepdims=True))).astype(BF16)
            cut = block // per_u
            wd_ref[score_slab(h), r * cut : (r + 1) * cut] = ds.reshape(cut, per_u, slot)
            dq_ref[rs, :] += jnp.where(mine(h), dot(ds, k_ref[...], 1, 0), 0.0)
            b = dot(qt_ref[hs, rs], ds, 1, 0)
            dk = b if dk is None else dk + b
            c = dot(gt_ref[hs, rs], e, 1, 0)
            dv = c if dv is None else dv + c
        dt_ref[1, hs, :] = dk.astype(BF16)
        dt_ref[2, hs, :] = dv.astype(BF16)

        @pl.when(h == 0)
        def _():
            arrived(0, 3)

        @pl.when(h == 1)
        def _():
            arrived(1, 2)

    onward(3)
    low_q = (dq_ref[...] * scale).astype(BF16)
    dn_ref[0] = low_q
    dt_ref[0] = low_q.astype(F32).T.astype(BF16)
    for c in (1, 2):
        dn_ref[c] = dt_ref[c].astype(F32).T.astype(BF16)

    ones = jnp.ones((8, slot), BF16)
    xf = xf_ref[...].reshape(slot, wide)
    for c in range(3):
        qa_ref[:, c * per_o : (c + 1) * per_o, :] = dot(dt_ref[c], xf, 1, 0).reshape(SLICES, per_o, wide)
    sp_ref[8:16, :] = jnp.zeros((8, wide), F32)
    sp_ref[9:10, 0:width] = dot(ones, dn_ref[0], 1, 0)[0:1]
    sp_ref[10:11, 0:width] = dot(ones, dn_ref[2], 1, 0)[0:1]
    begin(2)
    onward(3)

    b_up = bu_ref[...].astype(F32).reshape(1, -1)

    @pl.loop(0, n_mp)
    def _(b):
        at = pl.ds(pl.multiple_of(b * rows, rows), rows)
        act, slope = gelu_parts(dot(nf_ref[b], slab(wu_ref, z), 1, 0) + b_up)
        e_ref[0, at, :] = act
        bias_ref[slope_at, at, :] = slope

    onward(2, 3)
    arrived(1, 3)

    dff = dff_ref[...].reshape(slot, wide)
    bias_ref[1] = dot(e_ref[0], dff, 0, 0)
    begin(1)
    e_ref[1] = (dot(dff, slab(wd_ref, z), 1, 1) * bias_ref[slope_at]).astype(BF16)
    bias_ref[0] = dot(nf_ref[...].reshape(slot, wide), e_ref[1], 0, 0)
    begin(0)
    sp_ref[8:9, :] = dot(ones, e_ref[1], 1, 0)[0:1]

    def r_copy(turn, to):
        return remote(wo_ref.at[turn], got_ref.at[turn], r_send.at[turn], r_recv.at[turn], (d, to))

    def dx_part(to):
        at = pl.ds(pl.multiple_of(to * rows, rows), rows)
        out = dot(dn_ref[0, at, :], w_ref[0], 1, 0)
        for c in (1, 2):
            out = out + dot(dn_ref[c, at, :], w_ref[c], 1, 0)
        return out

    @pl.loop(0, n_mp)
    def _(turn):
        to = (z + 1 + turn) % n_mp
        out = dx_part(to)

        @pl.when(turn < n_mp - 1)
        def _():
            wo_ref[turn] = out.astype(BF16).reshape(wo_ref.shape[1:])
            r_copy(turn, to).start()

        @pl.when(turn == n_mp - 1)
        def _():
            da_ref[...] += out

    onward(1, 0, 2, 3)

    acc_ref[...] = jnp.zeros_like(acc_ref)
    one = jnp.ones((), BF16)
    trips = slot // (GROUP * STEP)
    per_slice = per_u // (GROUP * STEP)
    polls = {trips // 5: (1, 0, 2), 2 * trips // 5: (1, 0, 2), 3 * trips // 5: (1, 0, 2, 3), 4 * trips // 5: (1, 0, 2, 3)}

    @pl.loop(0, trips)
    def _(i):
        first = pl.multiple_of((i % per_slice) * GROUP * STEP, GROUP * STEP)
        flat_at = pl.multiple_of(i * GROUP * STEP, GROUP * STEP)
        ds = [
            [wd_ref[score_slab(h), i // per_slice, pl.ds(first + g * GROUP, GROUP), :] for h in range(heads)] for g in range(STEP)
        ]
        for t, b_ref in enumerate((bx_ref, by_ref)):
            tot = None
            for g in range(STEP):
                b = b_ref[pl.ds(flat_at + g * GROUP, GROUP), :]
                hi = (b >> 4).astype(F32).astype(BF16)
                lo = (b & 15).astype(F32).astype(BF16)
                left = []
                for a in range(HI):
                    m = hi == jnp.asarray(a, BF16)
                    left += [jnp.where(m, ds[g][h], zero) for h in range(heads)]
                right = [jnp.where(lo == jnp.asarray(c, BF16), one, zero) for c in range(LO)]
                o = dot(jnp.concatenate(left, 0), jnp.concatenate(right, 0), 1, 1)
                tot = o if tot is None else tot + o
            acc_ref[t] += tot
        for trip, which in polls.items():

            @pl.when(i == trip)
            def _():
                onward(*which)

    m, n = HI * heads * GROUP, LO * GROUP
    same = (lax.broadcasted_iota(jnp.int32, (m, n), 0) & (GROUP - 1)) == (lax.broadcasted_iota(jnp.int32, (m, n), 1) & (GROUP - 1))
    pick = (lax.broadcasted_iota(jnp.int32, (n, LO), 0) // GROUP == lax.broadcasted_iota(jnp.int32, (n, LO), 1)).astype(F32)
    st_ref[...] = jnp.zeros_like(st_ref)
    for t in range(2):
        kept = jnp.sum(jnp.where(same, acc_ref[t], 0.0).reshape(m // GROUP, GROUP, n), axis=1)
        found = lax.dot_general(
            kept, pick, (((1,), (0,)), ((), ())), precision=lax.Precision.HIGHEST, preferred_element_type=F32
        )
        st_ref[0 : HI * heads, t * LO : (t + 1) * LO] = found * scale

    cw = lax.broadcasted_iota(jnp.int32, (TILE, TILE), 1)
    rw = lax.broadcasted_iota(jnp.int32, (TILE, TILE), 0)
    half = bins // 2

    for h in range(heads):
        tots = [jnp.zeros((TILE, TILE), F32) for _ in range(5)]
        for i in range(tiles):
            pieces = []
            at = i * TILE
            while at < (i + 1) * TILE:
                inner = at % per_u
                take = min(per_u - inner, (i + 1) * TILE - at)
                pieces.append(wd_ref[score_slab(h), at // per_u, inner : inner + take, :])
                at += take
            strip = (jnp.concatenate(pieces, 0) if len(pieces) > 1 else pieces[0]).astype(F32)
            for j in range(tiles):
                off = min(max(j - i, -2), 2) + 2
                tots[off] = tots[off] + strip[:, j * TILE : (j + 1) * TILE]
        for off in range(5):
            line_ref[h, off] = tots[off]
    ids = [line_bucket(cw - rw + (off - 2) * TILE) for off in range(5)]
    for h in range(heads):
        found = []
        for b in range(bins):
            tot = None
            for off in range(5):
                if off in (1, 2, 3) and (off == 2 or (b >= half) == (off == 3)):
                    piece = jnp.where(ids[off] == b, line_ref[h, off], 0.0)
                elif off == 0 and b == half - 1 or off == 4 and b == bins - 1:
                    piece = line_ref[h, off]
                else:
                    continue
                tot = piece if tot is None else tot + piece
            found.append(jnp.sum(tot, axis=0, keepdims=True))
        st_ref[0:bins, 2 * LO + h : 2 * LO + h + 1] = jnp.sum(jnp.concatenate(found, 0), axis=1, keepdims=True) * scale

    bits = plans[0] + extra

    def small(turn):
        to = (flip(d, bits[turn]), z)
        return (
            remote(sp_ref, sr_ref.at[turn], sp_send.at[0, turn], sp_recv.at[0, turn], to),
            remote(st_ref, sv_ref.at[turn], sp_send.at[1, turn], sp_recv.at[1, turn], to),
        )

    for source in others:
        sz_copy(z, source).wait_recv()
        sp_ref[0:8, :] = sp_ref[0:8, :] + sz_ref[source]
    for turn in range(len(bits)):
        start_all(small(turn))
        onward(1, 0, 2, 3)
        for copy in small(turn):
            copy.wait_send()
            copy.wait_recv()
        sp_ref[...] = sp_ref[...] + sr_ref[turn]
        st_ref[...] = st_ref[...] + sv_ref[turn]
    pack_ref[...] = sp_ref[...]
    tab_out[...] = st_ref[...]

    for turn in range(n_mp - 1):
        r_copy(turn, z).wait_recv()
        da_ref[...] = da_ref[...] + got_ref[turn].astype(F32).reshape(rows, wide)
    ig_ref[...] = da_ref[...].astype(BF16)

    while any(stage.values()):
        onward(1, 0, 2, 3)
    for turn in range(n_mp - 1):
        r_copy(turn, z).wait_send()
    for to in others:
        d_copy(to, z).wait_send()
        sz_copy(to, z).wait_send()
        oz_copy(to, z).wait_send()
    for i in range(4):
        for place in range(depth):
            rs_copy(i, place).wait_send()
            ag_copy(i, place).wait_send()
    for a in range(2):
        ends(lambda ahead, sem: hop(a, z, ahead, sem).wait_send())

        def gone(block, ahead, more):
            @pl.when(more)
            def _():
                hop(a, block, ahead, block).wait_send()

        for step in range(1, n_mp):
            on_step(step, gone)


def finish_kernel(
    lo_hbm, ig_hbm, sp_hbm, st_hbm, u_hbm, d_hbm, q_hbm, o_hbm,
    lo_ref, ig_ref, gq_ref, bq_ref, bv_ref, go_ref, bo_ref, ga_ref, na_ref, gu_ref, bu_ref, gd_ref, bd_ref, gf_ref, nf_ref,
    tp_ref, tx_ref, ty_ref,
    u32, d32, q32, sp_ref, st_ref, u_ref, d_ref, q_ref, o_ref, sem, in_sem,
):
    pairs = ((u_hbm, u_ref), (d_hbm, d_ref), (q_hbm, q_ref), (o_hbm, o_ref), (sp_hbm, sp_ref), (st_hbm, st_ref), (lo_hbm, lo_ref), (ig_hbm, ig_ref))
    loads = [pltpu.make_async_copy(src, dst, in_sem.at[i]) for i, (src, dst) in enumerate(pairs)]
    for copy in loads:
        copy.start()
    loads[0].wait()
    wide = sp_ref.shape[1]
    width = bq_ref.shape[0]
    heads = width // HEAD_DIM
    per = width // SLICES
    u32[...] = u_ref[...].astype(F32)
    cu = pltpu.make_async_copy(u32, gu_ref, sem.at[0])
    cu.start()
    loads[1].wait()
    d32[...] = d_ref[...].astype(F32)
    cd = pltpu.make_async_copy(d32, gd_ref, sem.at[1])
    cd.start()
    loads[2].wait()
    for c in range(3):
        q32[c] = q_ref[:, c * per : (c + 1) * per, :].astype(F32).reshape(width, wide)
    cq = pltpu.make_async_copy(q32, gq_ref, sem.at[2])
    cq.start()
    for copy in loads[3:]:
        copy.wait()
    go_ref[...] = o_ref[...].astype(F32).reshape(width, wide)
    for row, ref in enumerate((gf_ref, nf_ref, bd_ref, ga_ref, na_ref, bo_ref)):
        ref[...] = sp_ref[row : row + 1, :].reshape(wide)
    bu_ref[...] = sp_ref[8:9, :].reshape(wide)
    bq_ref[...] = sp_ref[9:10, 0:width].reshape(width)
    bv_ref[...] = sp_ref[10:11, 0:width].reshape(width)
    table = st_ref[...]
    turned = table.T
    bins = tp_ref.shape[1]
    tp_ref[...] = turned[2 * LO : 2 * LO + heads, 0:bins]
    for t, ref in enumerate((tx_ref, ty_ref)):
        for h in range(heads):
            ref[h : h + 1, :] = jnp.concatenate(
                [table[a * heads + h : a * heads + h + 1, t * LO : (t + 1) * LO] for a in range(HI)], axis=1
            )
    for copy in (cu, cd, cq):
        copy.wait()


def layer(n_mp, n_dp):
    chips, extra = plane_bits(n_dp)
    plans = [chips + [0], chips[::-1] + [0]]
    depth = len(plans[0])

    def on_device(
        hidden_in, text_lens, key_mask, bucket_x, bucket_y, w_qkv, b_q, b_v, w_out, b_out, g_attn, n_attn,
        w_up, b_up, w_down, b_down, g_ffn, n_ffn, t_pos, t_x, t_y, cotangent,
    ):
        rows, wide = hidden_in.shape
        slot = bucket_x.shape[1]
        width = w_qkv.shape[2]
        heads = width // HEAD_DIM
        units = w_up.shape[1]
        per_u, per_o = wide // SLICES, width // SLICES
        bins = t_pos.shape[1]
        sds = jax.ShapeDtypeStruct
        dma = pltpu.SemaphoreType.DMA
        vm = pltpu.VMEM
        more = max(1, len(extra))
        n_bits = depth + len(extra)
        slices = [w.reshape(SLICES, w.shape[0] // SLICES, w.shape[1]) for w in (w_out, w_up, w_down)]
        whole = [(SLICES, per_u, units), (SLICES, units // SLICES, wide), (SLICES, 3 * per_o, wide), (SLICES, per_o, wide)]
        got = whole[:3] + [(SLICES, n_mp * per_o, wide)]
        outs = pl.pallas_call(
            functools.partial(layer_kernel, n_mp, plans, extra),
            out_shape=[sds((rows, wide), BF16), sds((rows, wide), BF16), sds((16, wide), F32), sds((bins, TILE), F32)]
            + [sds(shape, BF16) for shape in whole],
            in_specs=[VMEM] * 16 + [pl.BlockSpec(memory_space=pltpu.SMEM)] + [ANY] * 5,
            out_specs=[VMEM] * 8,
            scratch_shapes=[
                vm((n_mp, rows, wide), BF16), vm((slot, width), BF16), vm((slot, width), BF16), vm((slot, width), BF16),
                vm((heads, slot, slot), BF16), vm((heads, slot, 1), F32), vm((n_mp, rows, width), BF16),
                vm((n_mp, 8, units), F32), vm((slot, slot), jnp.int32), vm((slot, slot), jnp.int32), vm((heads, slot, slot), F32),
                vm((heads, 5, TILE, TILE), F32),
            ] + [vm((n_mp,) + s.shape, BF16) for s in slices] + [
                vm((rows, wide), F32), vm((rows, wide), F32), vm((8, wide), F32), vm((n_mp, rows, width), BF16), vm((n_mp, rows, width), BF16),
                vm((width, slot), BF16), vm((width, slot), BF16), vm((slot, width), F32), vm((3, width, slot), BF16), vm((3, slot, width), BF16),
                vm((2, HI * heads * GROUP, LO * GROUP), F32), vm((n_mp - 1,) + slices[0].shape, BF16), vm((n_mp, rows, wide), BF16), vm((n_mp, rows, wide), BF16),
                vm((16, wide), F32), vm((bins, TILE), F32), vm((n_bits, 16, wide), F32), vm((n_bits, bins, TILE), F32), vm((n_mp, 8, wide), F32),
                vm((SLICES, 3 * per_o, wide), F32), vm((SLICES, n_mp * per_o, wide), F32), vm((SLICES, 3 * per_o, wide), BF16),
            ] + [vm(shape, BF16) for shape in got] + [vm((n_mp, per_o, wide), BF16)] * 2 + [vm((more,) + shape[1:], BF16) for shape in got] + [
                dma((3,)), dma((2, slot // TILE)), dma((n_mp + 1,)), dma((n_mp,)), dma((n_mp - 1,)), dma((n_mp,)), dma((n_mp,)), dma((n_mp,)),
                dma((3, n_mp + 1)), dma((3, n_mp)), dma((3, depth, n_mp)), dma((3, depth, n_mp)),
                dma((n_mp,)), dma((n_mp,)), dma((n_mp - 1,)), dma((n_mp - 1,)), dma((2, n_mp + 1)), dma((2, n_mp)),
                dma((4, depth)), dma((4, depth)), dma((4, depth)), dma((4, depth)), dma((4, more)), dma((4, more)), dma((n_mp,)), dma((n_mp,)),
                dma((2, n_bits)), dma((2, n_bits)), dma((n_mp,)), dma((n_mp,)),
            ],
            compiler_params=pltpu.CompilerParams(collective_id=0, has_side_effects=True, vmem_limit_bytes=62 << 20),
            name="layer",
        )(
            hidden_in, jnp.transpose(w_qkv, (0, 2, 1)), b_q, b_v, t_x, t_y, t_pos, key_mask, b_up, b_out, g_attn, n_attn, b_down, g_ffn,
            n_ffn, cotangent, text_lens, bucket_x[0], bucket_y[0], *slices,
        )
        vec = lambda like: sds(like.shape, F32)
        final = pl.pallas_call(
            finish_kernel,
            out_shape=[
                sds((rows, wide), BF16), sds((rows, wide), BF16), sds((3, width, wide), F32), vec(b_q), vec(b_v), vec(w_out), vec(b_out),
                vec(g_attn), vec(n_attn), sds((SLICES, per_u, units), F32), vec(b_up), sds((SLICES, units // SLICES, wide), F32), vec(b_down),
                vec(g_ffn), vec(n_ffn), vec(t_pos), vec(t_x), vec(t_y),
            ],
            in_specs=[ANY] * 8,
            out_specs=[VMEM] * 2 + [ANY] + [VMEM] * 6 + [ANY] + [VMEM] + [ANY] + [VMEM] * 6,
            scratch_shapes=[
                vm((SLICES, per_u, units), F32), vm((SLICES, units // SLICES, wide), F32), vm((3, width, wide), F32),
                vm((16, wide), F32), vm((bins, TILE), F32),
            ] + [vm(shape, BF16) for shape in whole] + [dma((3,)), dma((8,))],
            compiler_params=pltpu.CompilerParams(vmem_limit_bytes=62 << 20),
            name="finish",
        )(*outs)
        final = list(final)
        final[2] = jnp.transpose(final[2], (0, 2, 1))
        final[9] = final[9].reshape(w_up.shape)
        final[11] = final[11].reshape(w_down.shape)
        return tuple(final)

    return on_device


def solution(mesh):
    both, split = P(("dp", "mp"), None), P("mp")
    rows_mp, cols_mp, qkv = P("mp", None), P(None, "mp"), P(None, None, "mp")
    doc = P("dp", None, None)
    return jax.shard_map(
        layer(mesh.shape["mp"], mesh.shape["dp"]),
        mesh=mesh,
        in_specs=(
            both, P("dp"), P("dp"), doc, doc, qkv, split, split, rows_mp, P(), P(), P(), cols_mp, split, rows_mp, P(), P(), P(),
            rows_mp, rows_mp, rows_mp, both,
        ),
        out_specs=(
            both, both, qkv, split, split, rows_mp, P(), P(), P(), cols_mp, split, rows_mp, P(), P(), P(), rows_mp, rows_mp, rows_mp,
        ),
        check_vma=False,
    )
```

```python
import functools
import jax
import jax.numpy as jnp
from jax import lax
from jax.experimental import pallas as pl
from jax.experimental.pallas import tpu as pltpu
from jax.sharding import PartitionSpec as P

HEAD_DIM = 64
PATCHES = 196
THRESHOLDS = (12, 16, 23, 32, 46, 64, 91)
TILE = 128
F32, BF16 = jnp.float32, jnp.bfloat16
MESH = pl.DeviceIdType.MESH
VMEM = pl.BlockSpec(memory_space=pltpu.VMEM)
ANY = pl.BlockSpec(memory_space=pl.ANY)
BIG = 58 << 20


def line_bucket(off):
    mag = jnp.abs(off)
    far = jnp.full(off.shape, 8, jnp.int32)
    for border in THRESHOLDS:
        far = far + (mag >= border).astype(jnp.int32)
    return jnp.where(off > 0, 16, 0) + jnp.where(mag < 8, mag, far)


def dot(a, b, ca, cb):
    return lax.dot_general(a, b, (((ca,), (cb,)), ((), ())), preferred_element_type=F32)


def flip(index, bit):
    step = 2**bit
    return index + step * (1 - 2 * ((index // step) % 2))


SLICES = 8
EPS = 1e-05
HI, LO, GROUP, STEP = 4, 16, 16, 2


def plane_bits(dp_size):
    chips = list(range(1, dp_size.bit_length() - 1))
    used = SLICES.bit_length() - 2
    return chips[:used], chips[used:]


def plan_label(index, plan):
    label = 0
    for place, bit in enumerate(plan):
        label = label + ((index // 2**bit) % 2) * 2**place
    return label


def gelu_parts(pre):
    cdf = 0.5 * (1.0 + lax.erf(pre * (0.5**0.5)))
    return (pre * cdf).astype(BF16), cdf + pre * (jnp.exp(-0.5 * pre * pre) * 0.3989422804014327)


def layer_kernel(
    n_mp, plans, extra,
    x_ref, w_ref, bq_ref, bv_ref, tx_ref, ty_ref, tp_ref, km_ref, bu_ref, bo_ref, ga_ref, na_ref, bd_ref, gf_ref, nn_ref, cot_ref,
    len_ref, bx_hbm, by_hbm, wo_src, wu_src, wd_src,
    lo_ref, ig_ref, pack_ref, tab_out, uo_ref, do_ref, qo_ref, oo_ref,
    xf_ref, q_ref, k_ref, v_ref, e_ref, inv_ref, cr_ref, ball_ref, bx_ref, by_ref, bias_ref, line_ref, wo_ref, wu_ref, wd_ref,
    da_ref, ffn_ref, gs_ref, di_ref, dc_ref, qt_ref, gt_ref, dq_ref, dt_ref, dn_ref, acc_ref, got_ref, nf_ref, dff_ref,
    sp_ref, st_ref, sr_ref, sv_ref, sz_ref, qa_ref, oa_ref, qs_ref, ur_ref, dr_ref, qr_ref, or_ref, oy_ref, oz_ref, ux_ref, dx_ref, qx_ref, ox_ref,
    own_sem, b_sem, x_send, x_recv, c_send, c_recv, u_send, u_recv, z_send, z_recv, p_send, p_recv,
    d_send, d_recv, r_send, r_recv, h_send, h_recv, rs_send, rs_recv, ag_send, ag_recv, ex_send, ex_recv, oz_send, oz_recv,
    sp_send, sp_recv, sz_send, sz_recv,
):
    d = lax.axis_index("dp")
    z = lax.axis_index("mp")
    rows, wide = x_ref.shape
    slot = bx_ref.shape[0]
    width = w_ref.shape[1]
    heads = width // HEAD_DIM
    tiles = slot // TILE
    units = wu_ref.shape[3]
    scale = HEAD_DIM**-0.5
    mirrored = z // 2
    toward = 1 - 2 * mirrored
    inner = z + mirrored * (n_mp - 1 - 2 * z)

    def in_line(k):
        if isinstance(k, int):
            found = k if k > 1 else (inner if k == 0 else 1 - inner)
        else:
            found = jnp.where(k < 2, jnp.where(k == 0, inner, 1 - inner), k)
        return found + mirrored * (n_mp - 1 - 2 * found)

    sources = (wo_src, wu_src, wd_src)
    gathered = (wo_ref, wu_ref, wd_ref)
    others = [in_line(k) for k in range(n_mp - 1, 0, -1)]
    depth = len(plans[0])
    labels = [plan_label(d, plan) for plan in plans]
    w_plan = (0, 0, 1)

    def remote(src, dst, send, recv, to):
        return pltpu.make_async_remote_copy(src, dst, send, recv, device_id=to, device_id_type=MESH)

    loads = []
    for c in range(tiles):
        part = pl.ds(c * TILE, TILE)
        pair = (
            pltpu.make_async_copy(bx_hbm.at[part], bx_ref.at[part], b_sem.at[0, c]),
            pltpu.make_async_copy(by_hbm.at[part], by_ref.at[part], b_sem.at[1, c]),
        )
        for copy in pair:
            copy.start()
        loads.append(pair)

    barrier = pltpu.get_barrier_semaphore()
    peers = [(d, to) for to in others] + [(flip(d, bit), z) for bit in plans[0] + extra]
    for peer in peers:
        pl.semaphore_signal(barrier, inc=1, device_id=peer, device_id_type=MESH)
    xf_ref[z] = x_ref[...]
    ball_ref[z] = jnp.broadcast_to(bu_ref[...].astype(F32).reshape(1, -1), ball_ref.shape[1:])
    pl.semaphore_wait(barrier, len(peers))

    def on_step(step, act):
        for block, ahead in ((z + toward * step, z - toward), (z - toward * step, z + toward)):

            @pl.when(jnp.logical_and(block >= 0, block < n_mp))
            def _():
                act(block, ahead, jnp.logical_and(ahead >= 0, ahead < n_mp))

    def ends(act):
        for ahead, sem in ((z + 1, z), (z - 1, n_mp)):

            @pl.when(jnp.logical_and(ahead >= 0, ahead < n_mp))
            def _():
                act(ahead, sem)

    def start_all(copies):
        for copy in copies:
            copy.start()

    def x_hop(block, to, sem):
        return remote(xf_ref.at[block], xf_ref.at[block], x_send.at[sem], x_recv.at[block], (d, to))

    def w_hop(w, block, to, sem, own=False):
        label = labels[w_plan[w]]
        held = sources[w].at[label] if own else gathered[w].at[block, label]
        return remote(held, gathered[w].at[block, label], z_send.at[w, sem], z_recv.at[w, block], (d, to))

    def some_w(which, block, to, sem, own=False):
        return [w_hop(w, block, to, sem, own) for w in which]

    every, narrow, broad = (0, 1, 2), (0,), (1, 2)
    ends(lambda ahead, sem: x_hop(z, ahead, sem).start())
    ends(lambda ahead, sem: start_all(some_w(every, z, ahead, sem, True)))

    def u_copy(to, source):
        return remote(ball_ref.at[source], ball_ref.at[source], u_send.at[to], u_recv.at[source], (d, to))

    for to in others:
        u_copy(to, z).start()
    own = [pltpu.make_async_copy(sources[w], gathered[w].at[z], own_sem.at[w]) for w in range(3)]
    start_all(own)

    def x_arrived(step):
        def act(block, ahead, more):
            x_hop(block, z, block).wait_recv()

            @pl.when(more)
            def _():
                x_hop(block, ahead, block).start()

        on_step(step, act)

    def plane_copy(w, place, shard, incoming):
        plan = w_plan[w]
        size = 2**place
        base = (labels[plan] // size) * size
        if incoming:
            base = flip(base, place)
        part = gathered[w].at[shard, pl.ds(base, size)]
        return remote(part, part, p_send.at[w, place, shard], p_recv.at[w, place, shard], (flip(d, plans[plan][place]), z))

    def w_arrived(step, which):
        def act(block, ahead, more):
            for w in which:
                w_hop(w, block, z, block).wait_recv()

            @pl.when(more)
            def _():
                start_all(some_w(which, block, ahead, block))

            for w in which:
                plane_copy(w, 0, block, False).start()

        on_step(step, act)

    def plane_next(step, place, which):
        def act(block, ahead, more):
            for w in which:
                plane_copy(w, place - 1, block, True).wait_recv()
                plane_copy(w, place, block, False).start()

        on_step(step, act)

    def plane_done(step, which):
        def act(block, ahead, more):
            for w in which:
                plane_copy(w, depth - 1, block, True).wait_recv()

        on_step(step, act)

    tab = [
        jnp.broadcast_to(
            jnp.concatenate([tx_ref[h : h + 1, :].astype(F32), ty_ref[h : h + 1, :].astype(F32)], axis=1) * scale, (8, TILE)
        )
        for h in range(heads)
    ]
    bins_x = tx_ref.shape[1]
    bins = tp_ref.shape[1]
    pad = jnp.zeros((1, TILE - bins), F32)
    ltab = [
        jnp.broadcast_to(jnp.concatenate([tp_ref[h : h + 1, :].astype(F32) * scale, pad], axis=1), (8, TILE))
        for h in range(heads)
    ]
    ci = lax.broadcasted_iota(jnp.int32, (8, TILE), 1)
    ri = lax.broadcasted_iota(jnp.int32, (8, TILE), 0)

    @pl.loop(0, TILE // 8)
    def _(g):
        at = pl.ds(pl.multiple_of(g * 8, 8), 8)
        for off in range(5):
            idx = line_bucket(ci - ri - g * 8 + (off - 2) * TILE)
            for h in range(heads):
                line_ref[h, off, at, :] = jnp.take_along_axis(ltab[h], idx, axis=1)

    place_ids = lax.broadcasted_iota(jnp.int32, (1, slot), 1)
    live = place_ids < 1 + PATCHES + len_ref[0]
    seen = jnp.where(live & ((km_ref[...].reshape(1, slot) == 1) | (place_ids == 0)), 0.0, -1e30)

    def bias_chunk(c):
        for copy in loads[c]:
            copy.wait()

        @pl.loop(0, TILE // 8)
        def _(g):
            at = pl.ds(pl.multiple_of(c * TILE + g * 8, 8), 8)
            near = pl.ds(pl.multiple_of(g * 8, 8), 8)
            for j in range(tiles):
                cols = slice(j * TILE, (j + 1) * TILE)
                ix = bx_ref[at, cols]
                iy = by_ref[at, cols] + bins_x
                hide = seen[:, cols]
                off = min(max(j - c + 2, 0), 4)
                for h in range(heads):
                    b = jnp.take_along_axis(tab[h], ix, axis=1) + jnp.take_along_axis(tab[h], iy, axis=1)
                    bias_ref[h, at, cols] = (b + line_ref[h, off, near, :]) + hide

    for c in range(tiles):
        if c == tiles // 2:
            x_arrived(1)
            w_arrived(1, narrow)
        bias_chunk(c)
    w_arrived(1, broad)
    x_arrived(2)
    w_arrived(2, narrow)
    plane_next(1, 1, every)
    w_arrived(2, broad)
    plane_next(1, 2, every)
    plane_next(2, 1, narrow)
    x_arrived(3)
    w_arrived(3, narrow)

    lane = lax.broadcasted_iota(jnp.int32, (1, width), 1)

    def mine(h):
        return (lane >= h * HEAD_DIM) & (lane < (h + 1) * HEAD_DIM)

    zero = jnp.zeros((), BF16)
    b_q = bq_ref[...].astype(F32).reshape(1, width)
    b_v = bv_ref[...].astype(F32).reshape(1, width)

    @pl.loop(0, n_mp)
    def _(b):
        at = pl.ds(pl.multiple_of(b * rows, rows), rows)
        xb = xf_ref[b]
        q_ref[at, :] = ((dot(xb, w_ref[0], 1, 1) + b_q).astype(BF16).astype(F32) * scale).astype(BF16)
        k_ref[at, :] = dot(xb, w_ref[1], 1, 1).astype(BF16)
        v_ref[at, :] = (dot(xb, w_ref[2], 1, 1) + b_v).astype(BF16)

    def c_copy(turn, to, source):
        return remote(di_ref.at[turn], cr_ref.at[source], c_send.at[turn], c_recv.at[source], (d, to))

    @pl.loop(0, n_mp)
    def _(turn):
        to = in_line(n_mp - 1 - turn)
        at = pl.ds(pl.multiple_of(to * rows, rows), rows)
        q = q_ref[at, :]
        out = jnp.zeros((rows, width), F32)
        for h in range(heads):
            s = dot(jnp.where(mine(h), q, zero), k_ref[...], 1, 1) + bias_ref[h, at, :]
            top = jnp.max(s, axis=1, keepdims=True)
            e = jnp.exp(s - top).astype(BF16)
            e_ref[h, at, :] = e
            inv = 1.0 / jnp.sum(e.astype(F32), axis=1, keepdims=True)
            inv_ref[h, at, :] = inv
            out = out + jnp.where(mine(h), dot(e, v_ref[...], 1, 0) * inv, 0.0)
        low = out.astype(BF16)

        @pl.when(turn == n_mp - 1)
        def _():
            cr_ref[z] = low

        @pl.when(turn < n_mp - 1)
        def _():
            di_ref[turn] = low
            c_copy(turn, to, z).start()

        @pl.when(turn == 0)
        def _():
            plane_next(2, 1, broad)
            plane_next(2, 2, narrow)
            plane_next(3, 1, narrow)

        @pl.when(turn == 1)
        def _():
            w_arrived(3, broad)

        @pl.when(turn == 2)
        def _():
            plane_next(2, 2, broad)
            plane_next(3, 2, narrow)

    plane_next(3, 1, broad)
    for step in range(1, n_mp):
        plane_done(step, narrow)
    own[0].wait()
    for source in others:
        c_copy(0, z, source).wait_recv()
    for turn in range(n_mp - 1):
        c_copy(turn, z, z).wait_send()

    lines = (nf_ref, dff_ref)

    def hop(a, block, to, sem):
        return remote(lines[a].at[block], lines[a].at[block], h_send.at[a, sem], h_recv.at[a, block], (d, to))

    def arrived(a, step):
        def act(block, ahead, more):
            hop(a, block, z, block).wait_recv()

            @pl.when(more)
            def _():
                hop(a, block, ahead, block).start()

        on_step(step, act)

    def set_off(a):
        ends(lambda ahead, sem: hop(a, z, ahead, sem).start())

    def g_copy(to, source):
        return remote(dff_ref.at[source], dff_ref.at[source], h_send.at[1, to], h_recv.at[1, source], (d, to))

    def vec(ref):
        return ref[...].astype(F32).reshape(1, wide)

    def norm(values):
        spread = values - jnp.mean(values, axis=1, keepdims=True)
        rate = lax.rsqrt(jnp.mean(spread * spread, axis=1, keepdims=True) + EPS)
        return spread * rate, rate

    def norm_back(up, gain, hat, rate):
        scaled = up * gain
        first = jnp.mean(scaled, axis=1, keepdims=True)
        second = jnp.mean(scaled * hat, axis=1, keepdims=True)
        return rate * (scaled - first - hat * second)

    def total_rows(values):
        return jnp.sum(values, axis=0, keepdims=True)

    def slab(ref, s):
        return ref[s].reshape(-1, wide)

    attn = dot(cr_ref[0], slab(wo_ref, 0), 1, 0)
    for s in range(1, n_mp):
        attn = attn + dot(cr_ref[s], slab(wo_ref, s), 1, 0)
    hat_one, rate_one = norm(x_ref[...].astype(F32) + attn + vec(bo_ref))
    normed = hat_one * vec(ga_ref) + vec(na_ref)
    low_own = normed.astype(BF16)
    nf_ref[z] = low_own
    set_off(0)

    slope_at = heads - 1
    ffn_ref[...] = jnp.zeros_like(ffn_ref)
    plane_done(1, broad)
    plane_done(2, broad)
    for w in broad:
        own[w].wait()
    for source in others:
        u_copy(z, source).wait_recv()

    @pl.loop(0, n_mp)
    def _(k):
        @pl.when(k == n_mp - 1)
        def _():
            arrived(0, 1)
            plane_next(3, 2, broad)
            plane_done(3, broad)

        s = in_line(k)
        at = pl.ds(pl.multiple_of(s * rows, rows), rows)
        act, slope = gelu_parts(dot(nf_ref[z], slab(wu_ref, s), 1, 0) + ball_ref[s, 0:1, :])
        bias_ref[slope_at, at, :] = slope
        ffn_ref[...] += dot(act, slab(wd_ref, s), 1, 0)

    hat_two, rate_two = norm(normed + ffn_ref[...] + vec(bd_ref))
    lo_ref[...] = (hat_two * vec(gf_ref) + vec(nn_ref)).astype(BF16)

    place_row = z * rows + lax.broadcasted_iota(jnp.int32, (rows, 1), 0)
    grad_y = jnp.where(place_row < 1 + PATCHES + len_ref[0], cot_ref[...].astype(F32), 0.0)
    d_two = norm_back(grad_y, vec(gf_ref), hat_two, rate_two)
    dff_ref[z] = d_two.astype(BF16)
    set_off(1)
    ffn_ref[...] = d_two

    @pl.loop(0, n_mp)
    def _(s):
        at = pl.ds(pl.multiple_of(s * rows, rows), rows)
        d_pre = (dot(dff_ref[z], slab(wd_ref, s), 1, 1) * bias_ref[slope_at, at, :]).astype(BF16)
        ffn_ref[...] += dot(d_pre, slab(wu_ref, s), 1, 1)

        @pl.when(s == 0)
        def _():
            arrived(0, 2)

    d_normed = ffn_ref[...]
    d_one = norm_back(d_normed, vec(ga_ref), hat_one, rate_one)
    da_ref[...] = d_one
    d_attn = d_one.astype(BF16)

    def d_copy(to, source):
        return remote(di_ref.at[to], dc_ref.at[source], d_send.at[to], d_recv.at[source], (d, to))

    for s in range(n_mp):
        di_ref[s] = dot(d_attn, slab(wo_ref, s), 1, 1).astype(BF16)
    for to in others:
        d_copy(to, z).start()
    dc_ref[z] = di_ref[z]

    def wait_all(copies):
        for copy in copies:
            copy.wait_send()

    def sent(block, ahead, more):
        @pl.when(more)
        def _():
            wait_all([x_hop(block, ahead, block)] + some_w(every, block, ahead, block))

        for w in range(3):
            for place in range(depth):
                plane_copy(w, place, block, False).wait_send()

    ends(lambda ahead, sem: wait_all([x_hop(z, ahead, sem)] + some_w(every, z, ahead, sem, True)))
    for step in range(1, n_mp):
        on_step(step, sent)
    for to in others:
        u_copy(to, z).wait_send()

    per_u = wide // SLICES

    def flat(slab_index):
        def at(base, size):
            return bias_ref.at[slab_index, pl.ds(pl.multiple_of(base * per_u, per_u), size * per_u)]

        return at

    def lead(ref):
        return lambda base, size: ref.at[pl.ds(base, size)]

    def inside(ref, s):
        return lambda base, size: ref.at[s, pl.ds(base, size)]

    totals = (flat(0), flat(1), lead(qa_ref), lead(oa_ref))
    staged = (inside(wu_ref, others[0]), inside(wu_ref, others[1]), lead(qs_ref), inside(wu_ref, others[2]))
    taken = (ur_ref, dr_ref, qr_ref, or_ref)
    beyond = (ux_ref, dx_ref, qx_ref, ox_ref)
    outs = (uo_ref, do_ref, qo_ref, oo_ref)
    item_plan = (0, 1, 0, 1)

    def own_label(i):
        return labels[item_plan[i]]

    def halves(i, place):
        size = 2**place
        base = (own_label(i) // size) * size
        return base, flip(base, place), size

    def partner(i, place):
        return (flip(d, plans[item_plan[i]][place]), z)

    def rs_copy(i, place):
        _, away, size = halves(i, place)
        return remote(
            staged[i](away, size), taken[i].at[pl.ds(size, size)], rs_send.at[i, place], rs_recv.at[i, place], partner(i, place)
        )

    def rs_start(i, place):
        _, away, size = halves(i, place)
        target = staged[i](away, size)
        target[...] = totals[i](away, size)[...].astype(BF16).reshape(target.shape)
        rs_copy(i, place).start()

    def ex_copy(i, turn):
        return remote(
            staged[i](own_label(i), 1), beyond[i].at[pl.ds(turn, 1)], ex_send.at[i, turn], ex_recv.at[i, turn],
            (flip(d, extra[turn]), z),
        )

    def ex_start(i, turn):
        target = staged[i](own_label(i), 1)
        target[...] = totals[i](own_label(i), 1)[...].astype(BF16).reshape(target.shape)
        ex_copy(i, turn).start()

    def ag_copy(i, place, incoming=False):
        base, away, size = halves(i, place)
        part = outs[i].at[pl.ds(away if incoming else base, size)]
        return remote(part, part, ag_send.at[i, place], ag_recv.at[i, place], partner(i, place))

    def oz_copy(to, source):
        return remote(oy_ref.at[to], oz_ref.at[source], oz_send.at[to], oz_recv.at[source], (d, to))

    stage = {}

    def begin(i):
        rs_start(i, depth - 1)
        stage[i] = ("halve", depth - 1)

    def spread(i):
        if i == 3:
            per = oy_ref.shape[1]
            for s in range(n_mp):
                oy_ref[s] = oa_ref[own_label(3), s * per : (s + 1) * per, :].astype(BF16)
            for to in others:
                oz_copy(to, z).start()
            stage[i] = ("line", 0)
        else:
            outs[i][own_label(i)] = totals[i](own_label(i), 1)[...].astype(BF16).reshape(outs[i].shape[1:])
            ag_copy(i, 0).start()
            stage[i] = ("gather", 0)

    def onward(*which):
        for i in which:
            if stage[i] is None:
                continue
            kind, place = stage[i]
            if kind == "halve":
                kept, _, size = halves(i, place)
                rs_copy(i, place).wait_recv()
                total = totals[i](kept, size)
                total[...] = total[...] + taken[i][size : 2 * size].astype(F32).reshape(total.shape)
                if place:
                    rs_start(i, place - 1)
                    stage[i] = ("halve", place - 1)
                elif extra:
                    ex_start(i, 0)
                    stage[i] = ("swap", 0)
                else:
                    spread(i)
            elif kind == "swap":
                ex_copy(i, place).wait_send()
                ex_copy(i, place).wait_recv()
                total = totals[i](own_label(i), 1)
                total[...] = total[...] + beyond[i][place : place + 1].astype(F32).reshape(total.shape)
                if place < len(extra) - 1:
                    ex_start(i, place + 1)
                    stage[i] = ("swap", place + 1)
                else:
                    spread(i)
            elif kind == "line":
                per = oz_ref.shape[1]
                out = oa_ref[own_label(3), pl.ds(pl.multiple_of(z * per, per), per), :]
                for source in others:
                    oz_copy(z, source).wait_recv()
                    out = out + oz_ref[source].astype(F32)
                oo_ref[own_label(3)] = out.astype(BF16)
                ag_copy(3, 0).start()
                stage[i] = ("gather", 0)
            else:
                ag_copy(i, place, True).wait_recv()
                if place < depth - 1:
                    ag_copy(i, place + 1).start()
                    stage[i] = ("gather", place + 1)
                else:
                    stage[i] = None

    per_o = width // SLICES
    for s in range(n_mp):
        go = dot(cr_ref[s].astype(F32).T.astype(BF16), d_attn, 1, 0)
        oa_ref[:, s * per_o : (s + 1) * per_o, :] = go.reshape(SLICES, per_o, wide)
    begin(3)
    gs_ref[...] = jnp.concatenate(
        [
            total_rows(grad_y * hat_two), total_rows(grad_y), total_rows(d_two), total_rows(d_normed * hat_one),
            total_rows(d_normed), total_rows(d_one), jnp.zeros((2, wide), F32),
        ],
        axis=0,
    )
    sp_ref[0:8, :] = gs_ref[...]

    def sz_copy(to, source):
        return remote(gs_ref, sz_ref.at[source], sz_send.at[to], sz_recv.at[source], (d, to))

    for to in others:
        sz_copy(to, z).start()

    factor = jnp.zeros((slot, width), F32)
    for h in range(heads):
        factor = jnp.where(mine(h), inv_ref[h], factor)
    qt_ref[...] = q_ref[...].astype(F32).T.astype(BF16)
    arrived(0, 3)

    b_up = bu_ref[...].astype(F32).reshape(1, -1)
    cut_r = rows // per_u

    @pl.loop(0, n_mp)
    def _(b):
        at = pl.ds(pl.multiple_of(b * rows, rows), rows)
        act, slope = gelu_parts(dot(nf_ref[b], slab(wu_ref, z), 1, 0) + b_up)
        uo_ref[pl.ds(b * cut_r, cut_r)] = act.reshape(cut_r, per_u, units)
        bias_ref[slope_at, at, :] = slope

    arrived(1, 1)
    onward(3)
    for source in others:
        d_copy(source, source).wait_recv()

    gt_ref[...] = (dc_ref[...].reshape(slot, width).astype(F32) * factor).T.astype(BF16)
    dq_ref[...] = jnp.zeros_like(dq_ref)
    block = slot // 2
    groups = block // rows

    def score_slab(h):
        return (z + 1 + h) % n_mp

    @pl.loop(0, heads)
    def _(h):
        hs = pl.ds(pl.multiple_of(h * HEAD_DIM, HEAD_DIM), HEAD_DIM)
        dk = dv = None
        for r in range(slot // block):
            rs = slice(r * block, (r + 1) * block)
            e = e_ref[h, rs, :]
            p = e.astype(F32) * inv_ref[h, rs, :]
            up = dc_ref[r * groups : (r + 1) * groups].reshape(block, width)
            dp = dot(jnp.where(mine(h), up, zero), v_ref[...], 1, 1)
            ds = (p * (dp - jnp.sum(p * dp, axis=1, keepdims=True))).astype(BF16)
            cut = block // per_u
            wd_ref[score_slab(h), r * cut : (r + 1) * cut] = ds.reshape(cut, per_u, slot)
            dq_ref[rs, :] += jnp.where(mine(h), dot(ds, k_ref[...], 1, 0), 0.0)
            b = dot(qt_ref[hs, rs], ds, 1, 0)
            dk = b if dk is None else dk + b
            c = dot(gt_ref[hs, rs], e, 1, 0)
            dv = c if dv is None else dv + c
        dt_ref[1, hs, :] = dk.astype(BF16)
        dt_ref[2, hs, :] = dv.astype(BF16)

        @pl.when(h == 1)
        def _():
            arrived(1, 2)

    onward(3)
    low_q = (dq_ref[...] * scale).astype(BF16)
    dn_ref[0] = low_q
    dt_ref[0] = low_q.astype(F32).T.astype(BF16)
    for c in (1, 2):
        dn_ref[c] = dt_ref[c].astype(F32).T.astype(BF16)

    ones = jnp.ones((8, slot), BF16)
    xf = xf_ref[...].reshape(slot, wide)
    for c in range(3):
        qa_ref[:, c * per_o : (c + 1) * per_o, :] = dot(dt_ref[c], xf, 1, 0).reshape(SLICES, per_o, wide)
    sp_ref[8:16, :] = jnp.zeros((8, wide), F32)
    sp_ref[9:10, 0:width] = dot(ones, dn_ref[0], 1, 0)[0:1]
    sp_ref[10:11, 0:width] = dot(ones, dn_ref[2], 1, 0)[0:1]
    begin(2)
    onward(3)

    onward(2, 3)
    arrived(1, 3)
    dff = dff_ref[...].reshape(slot, wide)
    bias_ref[1] = dot(uo_ref[...].reshape(slot, units), dff, 0, 0)
    begin(1)
    e_ref[1] = (dot(dff, slab(wd_ref, z), 1, 1) * bias_ref[slope_at]).astype(BF16)
    bias_ref[0] = dot(nf_ref[...].reshape(slot, wide), e_ref[1], 0, 0)
    begin(0)
    sp_ref[8:9, :] = dot(ones, e_ref[1], 1, 0)[0:1]

    def r_copy(turn, to, place):
        return remote(wo_ref.at[turn], got_ref.at[place], r_send.at[turn], r_recv.at[place], (d, to))

    def dx_part(to):
        at = pl.ds(pl.multiple_of(to * rows, rows), rows)
        out = dot(dn_ref[0, at, :], w_ref[0], 1, 0)
        for c in (1, 2):
            out = out + dot(dn_ref[c, at, :], w_ref[c], 1, 0)
        return out

    @pl.loop(0, n_mp)
    def _(turn):
        to = in_line(n_mp - 1 - turn)
        out = dx_part(to)

        @pl.when(turn < n_mp - 1)
        def _():
            wo_ref[turn] = out.astype(BF16).reshape(wo_ref.shape[1:])
            r_copy(turn, to, (to - z + n_mp - 1) % n_mp).start()

        @pl.when(turn == n_mp - 1)
        def _():
            da_ref[...] += out

    onward(1, 0, 2, 3)

    acc_ref[...] = jnp.zeros_like(acc_ref)
    one = jnp.ones((), BF16)
    trips = slot // (GROUP * STEP)
    per_slice = per_u // (GROUP * STEP)
    polls = {trips // 5: (1, 0, 2), 2 * trips // 5: (1, 0, 2), 3 * trips // 5: (1, 0, 2, 3), 4 * trips // 5: (1, 0, 2, 3)}

    @pl.loop(0, trips)
    def _(i):
        first = pl.multiple_of((i % per_slice) * GROUP * STEP, GROUP * STEP)
        flat_at = pl.multiple_of(i * GROUP * STEP, GROUP * STEP)
        ds = [
            [wd_ref[score_slab(h), i // per_slice, pl.ds(first + g * GROUP, GROUP), :] for h in range(heads)] for g in range(STEP)
        ]
        for t, b_ref in enumerate((bx_ref, by_ref)):
            tot = None
            for g in range(STEP):
                b = b_ref[pl.ds(flat_at + g * GROUP, GROUP), :]
                hi = (b >> 4).astype(F32).astype(BF16)
                lo = (b & 15).astype(F32).astype(BF16)
                left = []
                for a in range(HI):
                    m = hi == jnp.asarray(a, BF16)
                    left += [jnp.where(m, ds[g][h], zero) for h in range(heads)]
                right = [jnp.where(lo == jnp.asarray(c, BF16), one, zero) for c in range(LO)]
                o = dot(jnp.concatenate(left, 0), jnp.concatenate(right, 0), 1, 1)
                tot = o if tot is None else tot + o
            acc_ref[t] += tot
        for trip, which in polls.items():

            @pl.when(i == trip)
            def _():
                onward(*which)

    m, n = HI * heads * GROUP, LO * GROUP
    same = (lax.broadcasted_iota(jnp.int32, (m, n), 0) & (GROUP - 1)) == (lax.broadcasted_iota(jnp.int32, (m, n), 1) & (GROUP - 1))
    pick = (lax.broadcasted_iota(jnp.int32, (n, LO), 0) // GROUP == lax.broadcasted_iota(jnp.int32, (n, LO), 1)).astype(F32)
    st_ref[...] = jnp.zeros_like(st_ref)
    for t in range(2):
        kept = jnp.sum(jnp.where(same, acc_ref[t], 0.0).reshape(m // GROUP, GROUP, n), axis=1)
        found = lax.dot_general(
            kept, pick, (((1,), (0,)), ((), ())), precision=lax.Precision.HIGHEST, preferred_element_type=F32
        )
        st_ref[0 : HI * heads, t * LO : (t + 1) * LO] = found * scale

    cw = lax.broadcasted_iota(jnp.int32, (TILE, TILE), 1)
    rw = lax.broadcasted_iota(jnp.int32, (TILE, TILE), 0)
    half = bins // 2

    for h in range(heads):
        tots = [jnp.zeros((TILE, TILE), F32) for _ in range(5)]
        for i in range(tiles):
            pieces = []
            at = i * TILE
            while at < (i + 1) * TILE:
                inner = at % per_u
                take = min(per_u - inner, (i + 1) * TILE - at)
                pieces.append(wd_ref[score_slab(h), at // per_u, inner : inner + take, :])
                at += take
            strip = (jnp.concatenate(pieces, 0) if len(pieces) > 1 else pieces[0]).astype(F32)
            for j in range(tiles):
                off = min(max(j - i, -2), 2) + 2
                tots[off] = tots[off] + strip[:, j * TILE : (j + 1) * TILE]
        for off in range(5):
            line_ref[h, off] = tots[off]
    ids = [line_bucket(cw - rw + (off - 2) * TILE) for off in range(5)]
    for h in range(heads):
        found = []
        for b in range(bins):
            tot = None
            for off in range(5):
                if off in (1, 2, 3) and (off == 2 or (b >= half) == (off == 3)):
                    piece = jnp.where(ids[off] == b, line_ref[h, off], 0.0)
                elif off == 0 and b == half - 1 or off == 4 and b == bins - 1:
                    piece = line_ref[h, off]
                else:
                    continue
                tot = piece if tot is None else tot + piece
            found.append(jnp.sum(tot, axis=0, keepdims=True))
        st_ref[0:bins, 2 * LO + h : 2 * LO + h + 1] = jnp.sum(jnp.concatenate(found, 0), axis=1, keepdims=True) * scale

    bits = plans[0] + extra

    def small(turn):
        to = (flip(d, bits[turn]), z)
        return (
            remote(sp_ref, sr_ref.at[turn], sp_send.at[0, turn], sp_recv.at[0, turn], to),
            remote(st_ref, sv_ref.at[turn], sp_send.at[1, turn], sp_recv.at[1, turn], to),
        )

    for source in others:
        sz_copy(z, source).wait_recv()
        sp_ref[0:8, :] = sp_ref[0:8, :] + sz_ref[source]
    for turn in range(len(bits)):
        start_all(small(turn))
        onward(1, 0, 2, 3)
        for copy in small(turn):
            copy.wait_send()
            copy.wait_recv()
        sp_ref[...] = sp_ref[...] + sr_ref[turn]
        st_ref[...] = st_ref[...] + sv_ref[turn]
    pack_ref[...] = sp_ref[...]
    tab_out[...] = st_ref[...]

    for turn in range(n_mp - 1):
        r_copy(turn, z, turn).wait_recv()
        da_ref[...] = da_ref[...] + got_ref[turn].astype(F32).reshape(rows, wide)
    ig_ref[...] = da_ref[...].astype(BF16)

    while any(stage.values()):
        onward(1, 0, 2, 3)
    for turn in range(n_mp - 1):
        r_copy(turn, z, turn).wait_send()
    for to in others:
        d_copy(to, z).wait_send()
        sz_copy(to, z).wait_send()
        oz_copy(to, z).wait_send()
    for i in range(4):
        for place in range(depth):
            rs_copy(i, place).wait_send()
            ag_copy(i, place).wait_send()
    for a in range(2):
        ends(lambda ahead, sem: hop(a, z, ahead, sem).wait_send())

        def gone(block, ahead, more):
            @pl.when(more)
            def _():
                hop(a, block, ahead, block).wait_send()

        for step in range(1, n_mp):
            on_step(step, gone)


def finish_kernel(
    lo_hbm, ig_hbm, sp_hbm, st_hbm, u_hbm, d_hbm, q_hbm, o_hbm,
    lo_ref, ig_ref, gq_ref, bq_ref, bv_ref, go_ref, bo_ref, ga_ref, na_ref, gu_ref, bu_ref, gd_ref, bd_ref, gf_ref, nf_ref,
    tp_ref, tx_ref, ty_ref,
    u32, d32, q32, sp_ref, st_ref, u_ref, d_ref, q_ref, o_ref, sem, in_sem,
):
    pairs = ((u_hbm, u_ref), (d_hbm, d_ref), (q_hbm, q_ref), (o_hbm, o_ref), (sp_hbm, sp_ref), (st_hbm, st_ref), (lo_hbm, lo_ref), (ig_hbm, ig_ref))
    loads = [pltpu.make_async_copy(src, dst, in_sem.at[i]) for i, (src, dst) in enumerate(pairs)]
    for copy in loads:
        copy.start()
    loads[0].wait()
    wide = sp_ref.shape[1]
    width = bq_ref.shape[0]
    heads = width // HEAD_DIM
    per = width // SLICES
    u32[...] = u_ref[...].astype(F32)
    cu = pltpu.make_async_copy(u32, gu_ref, sem.at[0])
    cu.start()
    loads[1].wait()
    d32[...] = d_ref[...].astype(F32)
    cd = pltpu.make_async_copy(d32, gd_ref, sem.at[1])
    cd.start()
    loads[2].wait()
    for c in range(3):
        q32[c] = q_ref[:, c * per : (c + 1) * per, :].astype(F32).reshape(width, wide)
    cq = pltpu.make_async_copy(q32, gq_ref, sem.at[2])
    cq.start()
    for copy in loads[3:]:
        copy.wait()
    go_ref[...] = o_ref[...].astype(F32).reshape(width, wide)
    for row, ref in enumerate((gf_ref, nf_ref, bd_ref, ga_ref, na_ref, bo_ref)):
        ref[...] = sp_ref[row : row + 1, :].reshape(wide)
    bu_ref[...] = sp_ref[8:9, :].reshape(wide)
    bq_ref[...] = sp_ref[9:10, 0:width].reshape(width)
    bv_ref[...] = sp_ref[10:11, 0:width].reshape(width)
    table = st_ref[...]
    turned = table.T
    bins = tp_ref.shape[1]
    tp_ref[...] = turned[2 * LO : 2 * LO + heads, 0:bins]
    for t, ref in enumerate((tx_ref, ty_ref)):
        for h in range(heads):
            ref[h : h + 1, :] = jnp.concatenate(
                [table[a * heads + h : a * heads + h + 1, t * LO : (t + 1) * LO] for a in range(HI)], axis=1
            )
    for copy in (cu, cd, cq):
        copy.wait()


def layer(n_mp, n_dp):
    chips, extra = plane_bits(n_dp)
    plans = [chips + [0], chips[::-1] + [0]]
    depth = len(plans[0])

    def on_device(
        hidden_in, text_lens, key_mask, bucket_x, bucket_y, w_qkv, b_q, b_v, w_out, b_out, g_attn, n_attn,
        w_up, b_up, w_down, b_down, g_ffn, n_ffn, t_pos, t_x, t_y, cotangent,
    ):
        rows, wide = hidden_in.shape
        slot = bucket_x.shape[1]
        width = w_qkv.shape[2]
        heads = width // HEAD_DIM
        units = w_up.shape[1]
        per_u, per_o = wide // SLICES, width // SLICES
        bins = t_pos.shape[1]
        sds = jax.ShapeDtypeStruct
        dma = pltpu.SemaphoreType.DMA
        vm = pltpu.VMEM
        more = max(1, len(extra))
        n_bits = depth + len(extra)
        slices = [w.reshape(SLICES, w.shape[0] // SLICES, w.shape[1]) for w in (w_out, w_up, w_down)]
        whole = [(SLICES, per_u, units), (SLICES, units // SLICES, wide), (SLICES, 3 * per_o, wide), (SLICES, per_o, wide)]
        got = whole[:3] + [(SLICES, n_mp * per_o, wide)]
        outs = pl.pallas_call(
            functools.partial(layer_kernel, n_mp, plans, extra),
            out_shape=[sds((rows, wide), BF16), sds((rows, wide), BF16), sds((16, wide), F32), sds((bins, TILE), F32)]
            + [sds(shape, BF16) for shape in whole],
            in_specs=[VMEM] * 16 + [pl.BlockSpec(memory_space=pltpu.SMEM)] + [ANY] * 5,
            out_specs=[VMEM] * 8,
            scratch_shapes=[
                vm((n_mp, rows, wide), BF16), vm((slot, width), BF16), vm((slot, width), BF16), vm((slot, width), BF16),
                vm((heads, slot, slot), BF16), vm((heads, slot, 1), F32), vm((n_mp, rows, width), BF16),
                vm((n_mp, 8, units), F32), vm((slot, slot), jnp.int32), vm((slot, slot), jnp.int32), vm((heads, slot, slot), F32),
                vm((heads, 5, TILE, TILE), F32),
            ] + [vm((n_mp,) + s.shape, BF16) for s in slices] + [
                vm((rows, wide), F32), vm((rows, wide), F32), vm((8, wide), F32), vm((n_mp, rows, width), BF16), vm((n_mp, rows, width), BF16),
                vm((width, slot), BF16), vm((width, slot), BF16), vm((slot, width), F32), vm((3, width, slot), BF16), vm((3, slot, width), BF16),
                vm((2, HI * heads * GROUP, LO * GROUP), F32), vm((n_mp - 1,) + slices[0].shape, BF16), vm((n_mp, rows, wide), BF16), vm((n_mp, rows, wide), BF16),
                vm((16, wide), F32), vm((bins, TILE), F32), vm((n_bits, 16, wide), F32), vm((n_bits, bins, TILE), F32), vm((n_mp, 8, wide), F32),
                vm((SLICES, 3 * per_o, wide), F32), vm((SLICES, n_mp * per_o, wide), F32), vm((SLICES, 3 * per_o, wide), BF16),
            ] + [vm(shape, BF16) for shape in got] + [vm((n_mp, per_o, wide), BF16)] * 2 + [vm((more,) + shape[1:], BF16) for shape in got] + [
                dma((3,)), dma((2, slot // TILE)), dma((n_mp + 1,)), dma((n_mp,)), dma((n_mp - 1,)), dma((n_mp,)), dma((n_mp,)), dma((n_mp,)),
                dma((3, n_mp + 1)), dma((3, n_mp)), dma((3, depth, n_mp)), dma((3, depth, n_mp)),
                dma((n_mp,)), dma((n_mp,)), dma((n_mp - 1,)), dma((n_mp - 1,)), dma((2, n_mp + 1)), dma((2, n_mp)),
                dma((4, depth)), dma((4, depth)), dma((4, depth)), dma((4, depth)), dma((4, more)), dma((4, more)), dma((n_mp,)), dma((n_mp,)),
                dma((2, n_bits)), dma((2, n_bits)), dma((n_mp,)), dma((n_mp,)),
            ],
            compiler_params=pltpu.CompilerParams(collective_id=0, has_side_effects=True, vmem_limit_bytes=62 << 20),
            name="layer",
        )(
            hidden_in, jnp.transpose(w_qkv, (0, 2, 1)), b_q, b_v, t_x, t_y, t_pos, key_mask, b_up, b_out, g_attn, n_attn, b_down, g_ffn,
            n_ffn, cotangent, text_lens, bucket_x[0], bucket_y[0], *slices,
        )
        vec = lambda like: sds(like.shape, F32)
        final = pl.pallas_call(
            finish_kernel,
            out_shape=[
                sds((rows, wide), BF16), sds((rows, wide), BF16), sds((3, width, wide), F32), vec(b_q), vec(b_v), vec(w_out), vec(b_out),
                vec(g_attn), vec(n_attn), sds((SLICES, per_u, units), F32), vec(b_up), sds((SLICES, units // SLICES, wide), F32), vec(b_down),
                vec(g_ffn), vec(n_ffn), vec(t_pos), vec(t_x), vec(t_y),
            ],
            in_specs=[ANY] * 8,
            out_specs=[VMEM] * 2 + [ANY] + [VMEM] * 6 + [ANY] + [VMEM] + [ANY] + [VMEM] * 6,
            scratch_shapes=[
                vm((SLICES, per_u, units), F32), vm((SLICES, units // SLICES, wide), F32), vm((3, width, wide), F32),
                vm((16, wide), F32), vm((bins, TILE), F32),
            ] + [vm(shape, BF16) for shape in whole] + [dma((3,)), dma((8,))],
            compiler_params=pltpu.CompilerParams(vmem_limit_bytes=62 << 20),
            name="finish",
        )(*outs)
        final = list(final)
        final[2] = jnp.transpose(final[2], (0, 2, 1))
        final[9] = final[9].reshape(w_up.shape)
        final[11] = final[11].reshape(w_down.shape)
        return tuple(final)

    return on_device


def solution(mesh):
    both, split = P(("dp", "mp"), None), P("mp")
    rows_mp, cols_mp, qkv = P("mp", None), P(None, "mp"), P(None, None, "mp")
    doc = P("dp", None, None)
    return jax.shard_map(
        layer(mesh.shape["mp"], mesh.shape["dp"]),
        mesh=mesh,
        in_specs=(
            both, P("dp"), P("dp"), doc, doc, qkv, split, split, rows_mp, P(), P(), P(), cols_mp, split, rows_mp, P(), P(), P(),
            rows_mp, rows_mp, rows_mp, both,
        ),
        out_specs=(
            both, both, qkv, split, split, rows_mp, P(), P(), P(), cols_mp, split, rows_mp, P(), P(), P(), rows_mp, rows_mp, rows_mp,
        ),
        check_vma=False,
    )
```

```python
import functools
import jax
import jax.numpy as jnp
from jax import lax
from jax.experimental import pallas as pl
from jax.experimental.pallas import tpu as pltpu
from jax.sharding import PartitionSpec as P

HEAD_DIM = 64
PATCHES = 196
THRESHOLDS = (12, 16, 23, 32, 46, 64, 91)
TILE = 128
F32, BF16 = jnp.float32, jnp.bfloat16
MESH = pl.DeviceIdType.MESH
VMEM = pl.BlockSpec(memory_space=pltpu.VMEM)
ANY = pl.BlockSpec(memory_space=pl.ANY)
BIG = 58 << 20


def line_bucket(off):
    mag = jnp.abs(off)
    far = jnp.full(off.shape, 8, jnp.int32)
    for border in THRESHOLDS:
        far = far + (mag >= border).astype(jnp.int32)
    return jnp.where(off > 0, 16, 0) + jnp.where(mag < 8, mag, far)


def dot(a, b, ca, cb):
    return lax.dot_general(a, b, (((ca,), (cb,)), ((), ())), preferred_element_type=F32)


def flip(index, bit):
    step = 2**bit
    return index + step * (1 - 2 * ((index // step) % 2))


SLICES = 8
EPS = 1e-05
HI, LO, GROUP, STEP = 4, 16, 16, 3


def plane_bits(dp_size):
    chips = list(range(1, dp_size.bit_length() - 1))
    used = SLICES.bit_length() - 2
    return chips[:used], chips[used:]


def plan_label(index, plan):
    label = 0
    for place, bit in enumerate(plan):
        label = label + ((index // 2**bit) % 2) * 2**place
    return label


def gelu_parts(pre):
    cdf = 0.5 * (1.0 + lax.erf(pre * (0.5**0.5)))
    return (pre * cdf).astype(BF16), cdf + pre * (jnp.exp(-0.5 * pre * pre) * 0.3989422804014327)


def layer_kernel(
    n_mp, plans, extra,
    x_ref, w_ref, bq_ref, bv_ref, tx_ref, ty_ref, tp_ref, km_ref, bu_ref, bo_ref, ga_ref, na_ref, bd_ref, gf_ref, nn_ref, cot_ref,
    len_ref, bx_hbm, by_hbm, wo_src, wu_src, wd_src,
    lo_ref, ig_ref, pack_ref, tab_out, uo_ref, do_ref, qo_ref, oo_ref,
    xf_ref, q_ref, k_ref, v_ref, e_ref, inv_ref, cr_ref, ball_ref, bx_ref, by_ref, bias_ref, line_ref, wo_ref, wu_ref, wd_ref,
    da_ref, ffn_ref, gs_ref, di_ref, dc_ref, qt_ref, gt_ref, dq_ref, dt_ref, dn_ref, acc_ref, got_ref, nf_ref, dff_ref,
    sp_ref, st_ref, sr_ref, sv_ref, sz_ref, qa_ref, oa_ref, qs_ref, ur_ref, dr_ref, qr_ref, or_ref, oy_ref, oz_ref, ux_ref, dx_ref, qx_ref, ox_ref,
    own_sem, b_sem, x_send, x_recv, c_send, c_recv, u_send, u_recv, z_send, z_recv, p_send, p_recv,
    d_send, d_recv, r_send, r_recv, h_send, h_recv, rs_send, rs_recv, ag_send, ag_recv, ex_send, ex_recv, oz_send, oz_recv,
    sp_send, sp_recv, sz_send, sz_recv,
):
    d = lax.axis_index("dp")
    z = lax.axis_index("mp")
    rows, wide = x_ref.shape
    slot = bx_ref.shape[0]
    width = w_ref.shape[1]
    heads = width // HEAD_DIM
    tiles = slot // TILE
    units = wu_ref.shape[3]
    scale = HEAD_DIM**-0.5
    mirrored = z // 2
    toward = 1 - 2 * mirrored
    inner = z + mirrored * (n_mp - 1 - 2 * z)

    def in_line(k):
        if isinstance(k, int):
            found = k if k > 1 else (inner if k == 0 else 1 - inner)
        else:
            found = jnp.where(k < 2, jnp.where(k == 0, inner, 1 - inner), k)
        return found + mirrored * (n_mp - 1 - 2 * found)

    sources = (wo_src, wu_src, wd_src)
    gathered = (wo_ref, wu_ref, wd_ref)
    others = [in_line(k) for k in range(n_mp - 1, 0, -1)]
    depth = len(plans[0])
    labels = [plan_label(d, plan) for plan in plans]
    w_plan = (0, 0, 1)

    def remote(src, dst, send, recv, to):
        return pltpu.make_async_remote_copy(src, dst, send, recv, device_id=to, device_id_type=MESH)

    loads = []
    for c in range(tiles):
        part = pl.ds(c * TILE, TILE)
        pair = (
            pltpu.make_async_copy(bx_hbm.at[part], bx_ref.at[part], b_sem.at[0, c]),
            pltpu.make_async_copy(by_hbm.at[part], by_ref.at[part], b_sem.at[1, c]),
        )
        for copy in pair:
            copy.start()
        loads.append(pair)

    barrier = pltpu.get_barrier_semaphore()
    peers = [(d, to) for to in others] + [(flip(d, bit), z) for bit in plans[0] + extra]
    for peer in peers:
        pl.semaphore_signal(barrier, inc=1, device_id=peer, device_id_type=MESH)
    xf_ref[z] = x_ref[...]
    ball_ref[z] = jnp.broadcast_to(bu_ref[...].astype(F32).reshape(1, -1), ball_ref.shape[1:])
    pl.semaphore_wait(barrier, len(peers))

    def on_step(step, act):
        for block, ahead in ((z + toward * step, z - toward), (z - toward * step, z + toward)):

            @pl.when(jnp.logical_and(block >= 0, block < n_mp))
            def _():
                act(block, ahead, jnp.logical_and(ahead >= 0, ahead < n_mp))

    def ends(act):
        for ahead, sem in ((z + 1, z), (z - 1, n_mp)):

            @pl.when(jnp.logical_and(ahead >= 0, ahead < n_mp))
            def _():
                act(ahead, sem)

    def start_all(copies):
        for copy in copies:
            copy.start()

    def x_hop(block, to, sem):
        return remote(xf_ref.at[block], xf_ref.at[block], x_send.at[sem], x_recv.at[block], (d, to))

    def w_hop(w, block, to, sem, own=False):
        label = labels[w_plan[w]]
        held = sources[w].at[label] if own else gathered[w].at[block, label]
        return remote(held, gathered[w].at[block, label], z_send.at[w, sem], z_recv.at[w, block], (d, to))

    def some_w(which, block, to, sem, own=False):
        return [w_hop(w, block, to, sem, own) for w in which]

    every, narrow, broad = (0, 1, 2), (0,), (1, 2)
    ends(lambda ahead, sem: x_hop(z, ahead, sem).start())
    ends(lambda ahead, sem: start_all(some_w(every, z, ahead, sem, True)))

    def u_copy(to, source):
        return remote(ball_ref.at[source], ball_ref.at[source], u_send.at[to], u_recv.at[source], (d, to))

    for to in others:
        u_copy(to, z).start()
    own = [pltpu.make_async_copy(sources[w], gathered[w].at[z], own_sem.at[w]) for w in range(3)]
    start_all(own)

    def x_arrived(step):
        def act(block, ahead, more):
            x_hop(block, z, block).wait_recv()

            @pl.when(more)
            def _():
                x_hop(block, ahead, block).start()

        on_step(step, act)

    def plane_copy(w, place, shard, incoming):
        plan = w_plan[w]
        size = 2**place
        base = (labels[plan] // size) * size
        if incoming:
            base = flip(base, place)
        part = gathered[w].at[shard, pl.ds(base, size)]
        return remote(part, part, p_send.at[w, place, shard], p_recv.at[w, place, shard], (flip(d, plans[plan][place]), z))

    def w_arrived(step, which):
        def act(block, ahead, more):
            for w in which:
                w_hop(w, block, z, block).wait_recv()

            @pl.when(more)
            def _():
                start_all(some_w(which, block, ahead, block))

            for w in which:
                plane_copy(w, 0, block, False).start()

        on_step(step, act)

    def plane_next(step, place, which):
        def act(block, ahead, more):
            for w in which:
                plane_copy(w, place - 1, block, True).wait_recv()
                plane_copy(w, place, block, False).start()

        on_step(step, act)

    def plane_done(step, which):
        def act(block, ahead, more):
            for w in which:
                plane_copy(w, depth - 1, block, True).wait_recv()

        on_step(step, act)

    tab = [
        jnp.broadcast_to(
            jnp.concatenate([tx_ref[h : h + 1, :].astype(F32), ty_ref[h : h + 1, :].astype(F32)], axis=1) * scale, (8, TILE)
        )
        for h in range(heads)
    ]
    bins_x = tx_ref.shape[1]
    bins = tp_ref.shape[1]
    pad = jnp.zeros((1, TILE - bins), F32)
    ltab = [
        jnp.broadcast_to(jnp.concatenate([tp_ref[h : h + 1, :].astype(F32) * scale, pad], axis=1), (8, TILE))
        for h in range(heads)
    ]
    ci = lax.broadcasted_iota(jnp.int32, (8, TILE), 1)
    ri = lax.broadcasted_iota(jnp.int32, (8, TILE), 0)

    @pl.loop(0, TILE // 8)
    def _(g):
        at = pl.ds(pl.multiple_of(g * 8, 8), 8)
        for off in range(5):
            idx = line_bucket(ci - ri - g * 8 + (off - 2) * TILE)
            for h in range(heads):
                line_ref[h, off, at, :] = jnp.take_along_axis(ltab[h], idx, axis=1)

    place_ids = lax.broadcasted_iota(jnp.int32, (1, slot), 1)
    live = place_ids < 1 + PATCHES + len_ref[0]
    seen = jnp.where(live & ((km_ref[...].reshape(1, slot) == 1) | (place_ids == 0)), 0.0, -1e30)

    def bias_chunk(c):
        for copy in loads[c]:
            copy.wait()

        @pl.loop(0, TILE // 8)
        def _(g):
            at = pl.ds(pl.multiple_of(c * TILE + g * 8, 8), 8)
            near = pl.ds(pl.multiple_of(g * 8, 8), 8)
            for j in range(tiles):
                cols = slice(j * TILE, (j + 1) * TILE)
                ix = bx_ref[at, cols]
                iy = by_ref[at, cols] + bins_x
                hide = seen[:, cols]
                off = min(max(j - c + 2, 0), 4)
                for h in range(heads):
                    b = jnp.take_along_axis(tab[h], ix, axis=1) + jnp.take_along_axis(tab[h], iy, axis=1)
                    bias_ref[h, at, cols] = (b + line_ref[h, off, near, :]) + hide

    for c in range(tiles):
        if c == tiles // 2:
            x_arrived(1)
            w_arrived(1, narrow)
        bias_chunk(c)
    w_arrived(1, broad)
    x_arrived(2)
    w_arrived(2, narrow)
    plane_next(1, 1, every)
    w_arrived(2, broad)
    plane_next(1, 2, every)
    plane_next(2, 1, narrow)
    x_arrived(3)
    w_arrived(3, narrow)

    lane = lax.broadcasted_iota(jnp.int32, (1, width), 1)

    def mine(h):
        return (lane >= h * HEAD_DIM) & (lane < (h + 1) * HEAD_DIM)

    zero = jnp.zeros((), BF16)
    b_q = bq_ref[...].astype(F32).reshape(1, width)
    b_v = bv_ref[...].astype(F32).reshape(1, width)

    @pl.loop(0, n_mp)
    def _(b):
        at = pl.ds(pl.multiple_of(b * rows, rows), rows)
        xb = xf_ref[b]
        q_ref[at, :] = ((dot(xb, w_ref[0], 1, 1) + b_q).astype(BF16).astype(F32) * scale).astype(BF16)
        k_ref[at, :] = dot(xb, w_ref[1], 1, 1).astype(BF16)
        v_ref[at, :] = (dot(xb, w_ref[2], 1, 1) + b_v).astype(BF16)

    def c_copy(turn, to, source):
        return remote(di_ref.at[turn], cr_ref.at[source], c_send.at[turn], c_recv.at[source], (d, to))

    @pl.loop(0, n_mp)
    def _(turn):
        to = in_line(n_mp - 1 - turn)
        at = pl.ds(pl.multiple_of(to * rows, rows), rows)
        q = q_ref[at, :]
        out = jnp.zeros((rows, width), F32)
        for h in range(heads):
            s = dot(jnp.where(mine(h), q, zero), k_ref[...], 1, 1) + bias_ref[h, at, :]
            top = jnp.max(s, axis=1, keepdims=True)
            e = jnp.exp(s - top).astype(BF16)
            e_ref[h, at, :] = e
            inv = 1.0 / jnp.sum(e.astype(F32), axis=1, keepdims=True)
            inv_ref[h, at, :] = inv
            out = out + jnp.where(mine(h), dot(e, v_ref[...], 1, 0) * inv, 0.0)
        low = out.astype(BF16)

        @pl.when(turn == n_mp - 1)
        def _():
            cr_ref[z] = low

        @pl.when(turn < n_mp - 1)
        def _():
            di_ref[turn] = low
            c_copy(turn, to, z).start()

        @pl.when(turn == 0)
        def _():
            plane_next(2, 1, broad)
            plane_next(2, 2, narrow)
            plane_next(3, 1, narrow)

        @pl.when(turn == 1)
        def _():
            w_arrived(3, broad)

        @pl.when(turn == 2)
        def _():
            plane_next(2, 2, broad)
            plane_next(3, 2, narrow)

    plane_next(3, 1, broad)
    for step in range(1, n_mp):
        plane_done(step, narrow)
    own[0].wait()
    for source in others:
        c_copy(0, z, source).wait_recv()
    for turn in range(n_mp - 1):
        c_copy(turn, z, z).wait_send()

    lines = (nf_ref, dff_ref)

    def hop(a, block, to, sem):
        return remote(lines[a].at[block], lines[a].at[block], h_send.at[a, sem], h_recv.at[a, block], (d, to))

    def arrived(a, step):
        def act(block, ahead, more):
            hop(a, block, z, block).wait_recv()

            @pl.when(more)
            def _():
                hop(a, block, ahead, block).start()

        on_step(step, act)

    def set_off(a):
        ends(lambda ahead, sem: hop(a, z, ahead, sem).start())

    def g_copy(to, source):
        return remote(dff_ref.at[source], dff_ref.at[source], h_send.at[1, to], h_recv.at[1, source], (d, to))

    def vec(ref):
        return ref[...].astype(F32).reshape(1, wide)

    def norm(values):
        spread = values - jnp.mean(values, axis=1, keepdims=True)
        rate = lax.rsqrt(jnp.mean(spread * spread, axis=1, keepdims=True) + EPS)
        return spread * rate, rate

    def norm_back(up, gain, hat, rate):
        scaled = up * gain
        first = jnp.mean(scaled, axis=1, keepdims=True)
        second = jnp.mean(scaled * hat, axis=1, keepdims=True)
        return rate * (scaled - first - hat * second)

    def total_rows(values):
        return jnp.sum(values, axis=0, keepdims=True)

    def slab(ref, s):
        return ref[s].reshape(-1, wide)

    attn = dot(cr_ref[0], slab(wo_ref, 0), 1, 0)
    for s in range(1, n_mp):
        attn = attn + dot(cr_ref[s], slab(wo_ref, s), 1, 0)
    hat_one, rate_one = norm(x_ref[...].astype(F32) + attn + vec(bo_ref))
    normed = hat_one * vec(ga_ref) + vec(na_ref)
    low_own = normed.astype(BF16)
    nf_ref[z] = low_own
    set_off(0)

    slope_at = heads - 1
    ffn_ref[...] = jnp.zeros_like(ffn_ref)
    plane_done(1, broad)
    plane_done(2, broad)
    for w in broad:
        own[w].wait()
    for source in others:
        u_copy(z, source).wait_recv()

    @pl.loop(0, n_mp)
    def _(k):
        @pl.when(k == n_mp - 1)
        def _():
            arrived(0, 1)
            plane_next(3, 2, broad)
            plane_done(3, broad)

        s = in_line(k)
        at = pl.ds(pl.multiple_of(s * rows, rows), rows)
        act, slope = gelu_parts(dot(nf_ref[z], slab(wu_ref, s), 1, 0) + ball_ref[s, 0:1, :])
        bias_ref[slope_at, at, :] = slope
        ffn_ref[...] += dot(act, slab(wd_ref, s), 1, 0)

    hat_two, rate_two = norm(normed + ffn_ref[...] + vec(bd_ref))
    lo_ref[...] = (hat_two * vec(gf_ref) + vec(nn_ref)).astype(BF16)

    place_row = z * rows + lax.broadcasted_iota(jnp.int32, (rows, 1), 0)
    grad_y = jnp.where(place_row < 1 + PATCHES + len_ref[0], cot_ref[...].astype(F32), 0.0)
    d_two = norm_back(grad_y, vec(gf_ref), hat_two, rate_two)
    dff_ref[z] = d_two.astype(BF16)
    set_off(1)
    ffn_ref[...] = d_two

    @pl.loop(0, n_mp)
    def _(s):
        at = pl.ds(pl.multiple_of(s * rows, rows), rows)
        d_pre = (dot(dff_ref[z], slab(wd_ref, s), 1, 1) * bias_ref[slope_at, at, :]).astype(BF16)
        ffn_ref[...] += dot(d_pre, slab(wu_ref, s), 1, 1)

        @pl.when(s == 0)
        def _():
            arrived(0, 2)

    d_normed = ffn_ref[...]
    d_one = norm_back(d_normed, vec(ga_ref), hat_one, rate_one)
    da_ref[...] = d_one
    d_attn = d_one.astype(BF16)

    def d_copy(to, source):
        return remote(di_ref.at[to], dc_ref.at[source], d_send.at[to], d_recv.at[source], (d, to))

    for s in range(n_mp):
        di_ref[s] = dot(d_attn, slab(wo_ref, s), 1, 1).astype(BF16)
    for to in others:
        d_copy(to, z).start()
    dc_ref[z] = di_ref[z]

    def wait_all(copies):
        for copy in copies:
            copy.wait_send()

    def sent(block, ahead, more):
        @pl.when(more)
        def _():
            wait_all([x_hop(block, ahead, block)] + some_w(every, block, ahead, block))

        for w in range(3):
            for place in range(depth):
                plane_copy(w, place, block, False).wait_send()

    ends(lambda ahead, sem: wait_all([x_hop(z, ahead, sem)] + some_w(every, z, ahead, sem, True)))
    for step in range(1, n_mp):
        on_step(step, sent)
    for to in others:
        u_copy(to, z).wait_send()

    per_u = wide // SLICES

    def flat(slab_index):
        def at(base, size):
            return bias_ref.at[slab_index, pl.ds(pl.multiple_of(base * per_u, per_u), size * per_u)]

        return at

    def lead(ref):
        return lambda base, size: ref.at[pl.ds(base, size)]

    def inside(ref, s):
        return lambda base, size: ref.at[s, pl.ds(base, size)]

    totals = (flat(0), flat(1), lead(qa_ref), lead(oa_ref))
    staged = (inside(wu_ref, others[0]), inside(wu_ref, others[1]), lead(qs_ref), inside(wu_ref, others[2]))
    taken = (ur_ref, dr_ref, qr_ref, or_ref)
    beyond = (ux_ref, dx_ref, qx_ref, ox_ref)
    outs = (uo_ref, do_ref, qo_ref, oo_ref)
    item_plan = (0, 1, 0, 1)

    def own_label(i):
        return labels[item_plan[i]]

    def halves(i, place):
        size = 2**place
        base = (own_label(i) // size) * size
        return base, flip(base, place), size

    def partner(i, place):
        return (flip(d, plans[item_plan[i]][place]), z)

    def rs_copy(i, place):
        _, away, size = halves(i, place)
        return remote(
            staged[i](away, size), taken[i].at[pl.ds(size, size)], rs_send.at[i, place], rs_recv.at[i, place], partner(i, place)
        )

    def rs_start(i, place):
        _, away, size = halves(i, place)
        target = staged[i](away, size)
        target[...] = totals[i](away, size)[...].astype(BF16).reshape(target.shape)
        rs_copy(i, place).start()

    def ex_copy(i, turn):
        return remote(
            staged[i](own_label(i), 1), beyond[i].at[pl.ds(turn, 1)], ex_send.at[i, turn], ex_recv.at[i, turn],
            (flip(d, extra[turn]), z),
        )

    def ex_start(i, turn):
        target = staged[i](own_label(i), 1)
        target[...] = totals[i](own_label(i), 1)[...].astype(BF16).reshape(target.shape)
        ex_copy(i, turn).start()

    def ag_copy(i, place, incoming=False):
        base, away, size = halves(i, place)
        part = outs[i].at[pl.ds(away if incoming else base, size)]
        return remote(part, part, ag_send.at[i, place], ag_recv.at[i, place], partner(i, place))

    def oz_copy(to, source):
        return remote(oy_ref.at[to], oz_ref.at[source], oz_send.at[to], oz_recv.at[source], (d, to))

    stage = {}

    def begin(i):
        rs_start(i, depth - 1)
        stage[i] = ("halve", depth - 1)

    def spread(i):
        if i == 3:
            per = oy_ref.shape[1]
            for s in range(n_mp):
                oy_ref[s] = oa_ref[own_label(3), s * per : (s + 1) * per, :].astype(BF16)
            for to in others:
                oz_copy(to, z).start()
            stage[i] = ("line", 0)
        else:
            outs[i][own_label(i)] = totals[i](own_label(i), 1)[...].astype(BF16).reshape(outs[i].shape[1:])
            ag_copy(i, 0).start()
            stage[i] = ("gather", 0)

    def onward(*which):
        for i in which:
            if stage[i] is None:
                continue
            kind, place = stage[i]
            if kind == "halve":
                kept, _, size = halves(i, place)
                rs_copy(i, place).wait_recv()
                total = totals[i](kept, size)
                total[...] = total[...] + taken[i][size : 2 * size].astype(F32).reshape(total.shape)
                if place:
                    rs_start(i, place - 1)
                    stage[i] = ("halve", place - 1)
                elif extra:
                    ex_start(i, 0)
                    stage[i] = ("swap", 0)
                else:
                    spread(i)
            elif kind == "swap":
                ex_copy(i, place).wait_send()
                ex_copy(i, place).wait_recv()
                total = totals[i](own_label(i), 1)
                total[...] = total[...] + beyond[i][place : place + 1].astype(F32).reshape(total.shape)
                if place < len(extra) - 1:
                    ex_start(i, place + 1)
                    stage[i] = ("swap", place + 1)
                else:
                    spread(i)
            elif kind == "line":
                per = oz_ref.shape[1]
                out = oa_ref[own_label(3), pl.ds(pl.multiple_of(z * per, per), per), :]
                for source in others:
                    oz_copy(z, source).wait_recv()
                    out = out + oz_ref[source].astype(F32)
                oo_ref[own_label(3)] = out.astype(BF16)
                ag_copy(3, 0).start()
                stage[i] = ("gather", 0)
            else:
                ag_copy(i, place, True).wait_recv()
                if place < depth - 1:
                    ag_copy(i, place + 1).start()
                    stage[i] = ("gather", place + 1)
                else:
                    stage[i] = None

    per_o = width // SLICES
    for s in range(n_mp):
        go = dot(cr_ref[s].astype(F32).T.astype(BF16), d_attn, 1, 0)
        oa_ref[:, s * per_o : (s + 1) * per_o, :] = go.reshape(SLICES, per_o, wide)
    begin(3)
    gs_ref[...] = jnp.concatenate(
        [
            total_rows(grad_y * hat_two), total_rows(grad_y), total_rows(d_two), total_rows(d_normed * hat_one),
            total_rows(d_normed), total_rows(d_one), jnp.zeros((2, wide), F32),
        ],
        axis=0,
    )
    sp_ref[0:8, :] = gs_ref[...]

    def sz_copy(to, source):
        return remote(gs_ref, sz_ref.at[source], sz_send.at[to], sz_recv.at[source], (d, to))

    for to in others:
        sz_copy(to, z).start()

    factor = jnp.zeros((slot, width), F32)
    for h in range(heads):
        factor = jnp.where(mine(h), inv_ref[h], factor)
    qt_ref[...] = q_ref[...].astype(F32).T.astype(BF16)
    arrived(0, 3)

    b_up = bu_ref[...].astype(F32).reshape(1, -1)
    cut_r = rows // per_u

    @pl.loop(0, n_mp)
    def _(b):
        at = pl.ds(pl.multiple_of(b * rows, rows), rows)
        act, slope = gelu_parts(dot(nf_ref[b], slab(wu_ref, z), 1, 0) + b_up)
        uo_ref[pl.ds(b * cut_r, cut_r)] = act.reshape(cut_r, per_u, units)
        bias_ref[slope_at, at, :] = slope

    arrived(1, 1)
    onward(3)
    for source in others:
        d_copy(source, source).wait_recv()

    gt_ref[...] = (dc_ref[...].reshape(slot, width).astype(F32) * factor).T.astype(BF16)
    dq_ref[...] = jnp.zeros_like(dq_ref)
    block = slot // 2
    groups = block // rows

    def score_slab(h):
        return (z + 1 + h) % n_mp

    @pl.loop(0, heads)
    def _(h):
        hs = pl.ds(pl.multiple_of(h * HEAD_DIM, HEAD_DIM), HEAD_DIM)
        dk = dv = None
        for r in range(slot // block):
            rs = slice(r * block, (r + 1) * block)
            e = e_ref[h, rs, :]
            p = e.astype(F32) * inv_ref[h, rs, :]
            up = dc_ref[r * groups : (r + 1) * groups].reshape(block, width)
            dp = dot(jnp.where(mine(h), up, zero), v_ref[...], 1, 1)
            ds = (p * (dp - jnp.sum(p * dp, axis=1, keepdims=True))).astype(BF16)
            cut = block // per_u
            wd_ref[score_slab(h), r * cut : (r + 1) * cut] = ds.reshape(cut, per_u, slot)
            dq_ref[rs, :] += jnp.where(mine(h), dot(ds, k_ref[...], 1, 0), 0.0)
            b = dot(qt_ref[hs, rs], ds, 1, 0)
            dk = b if dk is None else dk + b
            c = dot(gt_ref[hs, rs], e, 1, 0)
            dv = c if dv is None else dv + c
        dt_ref[1, hs, :] = dk.astype(BF16)
        dt_ref[2, hs, :] = dv.astype(BF16)

        @pl.when(h == 1)
        def _():
            arrived(1, 2)

    onward(3)
    low_q = (dq_ref[...] * scale).astype(BF16)
    dn_ref[0] = low_q
    dt_ref[0] = low_q.astype(F32).T.astype(BF16)
    for c in (1, 2):
        dn_ref[c] = dt_ref[c].astype(F32).T.astype(BF16)

    ones = jnp.ones((8, slot), BF16)
    xf = xf_ref[...].reshape(slot, wide)
    for c in range(3):
        qa_ref[:, c * per_o : (c + 1) * per_o, :] = dot(dt_ref[c], xf, 1, 0).reshape(SLICES, per_o, wide)
    sp_ref[8:16, :] = jnp.zeros((8, wide), F32)
    sp_ref[9:10, 0:width] = dot(ones, dn_ref[0], 1, 0)[0:1]
    sp_ref[10:11, 0:width] = dot(ones, dn_ref[2], 1, 0)[0:1]
    begin(2)
    onward(3)

    onward(2, 3)
    arrived(1, 3)
    dff = dff_ref[...].reshape(slot, wide)
    bias_ref[1] = dot(uo_ref[...].reshape(slot, units), dff, 0, 0)
    begin(1)
    e_ref[1] = (dot(dff, slab(wd_ref, z), 1, 1) * bias_ref[slope_at]).astype(BF16)
    bias_ref[0] = dot(nf_ref[...].reshape(slot, wide), e_ref[1], 0, 0)
    begin(0)
    sp_ref[8:9, :] = dot(ones, e_ref[1], 1, 0)[0:1]

    def r_copy(turn, to, place):
        return remote(wo_ref.at[turn], got_ref.at[place], r_send.at[turn], r_recv.at[place], (d, to))

    def dx_part(to):
        at = pl.ds(pl.multiple_of(to * rows, rows), rows)
        out = dot(dn_ref[0, at, :], w_ref[0], 1, 0)
        for c in (1, 2):
            out = out + dot(dn_ref[c, at, :], w_ref[c], 1, 0)
        return out

    @pl.loop(0, n_mp)
    def _(turn):
        to = in_line(n_mp - 1 - turn)
        out = dx_part(to)

        @pl.when(turn < n_mp - 1)
        def _():
            wo_ref[turn] = out.astype(BF16).reshape(wo_ref.shape[1:])
            r_copy(turn, to, (to - z + n_mp - 1) % n_mp).start()

        @pl.when(turn == n_mp - 1)
        def _():
            da_ref[...] += out

    onward(1, 0, 2, 3)

    acc_ref[...] = jnp.zeros_like(acc_ref)
    one = jnp.ones((), BF16)
    trips = slot // (GROUP * STEP)
    per_slice = per_u // (GROUP * STEP)
    polls = {trips // 3: (1, 0, 2), 2 * trips // 3: (1, 0, 2)}

    @pl.loop(0, trips)
    def _(i):
        first = pl.multiple_of((i % per_slice) * GROUP * STEP, GROUP * STEP)
        flat_at = pl.multiple_of(i * GROUP * STEP, GROUP * STEP)
        ds = [
            [wd_ref[score_slab(h), i // per_slice, pl.ds(first + g * GROUP, GROUP), :] for h in range(heads)] for g in range(STEP)
        ]
        for t, b_ref in enumerate((bx_ref, by_ref)):
            tot = None
            for g in range(STEP):
                b = b_ref[pl.ds(flat_at + g * GROUP, GROUP), :]
                hi = (b >> 4).astype(F32).astype(BF16)
                lo = (b & 15).astype(F32).astype(BF16)
                left = []
                for a in range(HI):
                    m = hi == jnp.asarray(a, BF16)
                    left += [jnp.where(m, ds[g][h], zero) for h in range(heads)]
                right = [jnp.where(lo == jnp.asarray(c, BF16), one, zero) for c in range(LO)]
                o = dot(jnp.concatenate(left, 0), jnp.concatenate(right, 0), 1, 1)
                tot = o if tot is None else tot + o
            acc_ref[t] += tot
        for trip, which in polls.items():

            @pl.when(i == trip)
            def _():
                onward(*which)

    m, n = HI * heads * GROUP, LO * GROUP
    same = (lax.broadcasted_iota(jnp.int32, (m, n), 0) & (GROUP - 1)) == (lax.broadcasted_iota(jnp.int32, (m, n), 1) & (GROUP - 1))
    pick = (lax.broadcasted_iota(jnp.int32, (n, LO), 0) // GROUP == lax.broadcasted_iota(jnp.int32, (n, LO), 1)).astype(F32)
    st_ref[...] = jnp.zeros_like(st_ref)
    for t in range(2):
        kept = jnp.sum(jnp.where(same, acc_ref[t], 0.0).reshape(m // GROUP, GROUP, n), axis=1)
        found = lax.dot_general(
            kept, pick, (((1,), (0,)), ((), ())), precision=lax.Precision.HIGHEST, preferred_element_type=F32
        )
        st_ref[0 : HI * heads, t * LO : (t + 1) * LO] = found * scale

    cw = lax.broadcasted_iota(jnp.int32, (TILE, TILE), 1)
    rw = lax.broadcasted_iota(jnp.int32, (TILE, TILE), 0)
    half = bins // 2

    for h in range(heads):
        tots = [jnp.zeros((TILE, TILE), F32) for _ in range(5)]
        for i in range(tiles):
            pieces = []
            at = i * TILE
            while at < (i + 1) * TILE:
                inner = at % per_u
                take = min(per_u - inner, (i + 1) * TILE - at)
                pieces.append(wd_ref[score_slab(h), at // per_u, inner : inner + take, :])
                at += take
            strip = (jnp.concatenate(pieces, 0) if len(pieces) > 1 else pieces[0]).astype(F32)
            for j in range(tiles):
                off = min(max(j - i, -2), 2) + 2
                tots[off] = tots[off] + strip[:, j * TILE : (j + 1) * TILE]
        for off in range(5):
            line_ref[h, off] = tots[off]
    ids = [line_bucket(cw - rw + (off - 2) * TILE) for off in range(5)]
    for h in range(heads):
        found = []
        for b in range(bins):
            tot = None
            for off in range(5):
                if off in (1, 2, 3) and (off == 2 or (b >= half) == (off == 3)):
                    piece = jnp.where(ids[off] == b, line_ref[h, off], 0.0)
                elif off == 0 and b == half - 1 or off == 4 and b == bins - 1:
                    piece = line_ref[h, off]
                else:
                    continue
                tot = piece if tot is None else tot + piece
            found.append(jnp.sum(tot, axis=0, keepdims=True))
        st_ref[0:bins, 2 * LO + h : 2 * LO + h + 1] = jnp.sum(jnp.concatenate(found, 0), axis=1, keepdims=True) * scale

    bits = plans[0] + extra

    def small(turn):
        to = (flip(d, bits[turn]), z)
        return (
            remote(sp_ref, sr_ref.at[turn], sp_send.at[0, turn], sp_recv.at[0, turn], to),
            remote(st_ref, sv_ref.at[turn], sp_send.at[1, turn], sp_recv.at[1, turn], to),
        )

    for source in others:
        sz_copy(z, source).wait_recv()
        sp_ref[0:8, :] = sp_ref[0:8, :] + sz_ref[source]
    for turn in range(len(bits)):
        start_all(small(turn))
        onward(1, 0, 2, 3)
        for copy in small(turn):
            copy.wait_send()
            copy.wait_recv()
        sp_ref[...] = sp_ref[...] + sr_ref[turn]
        st_ref[...] = st_ref[...] + sv_ref[turn]
    pack_ref[...] = sp_ref[...]
    tab_out[...] = st_ref[...]

    for turn in range(n_mp - 1):
        r_copy(turn, z, turn).wait_recv()
        da_ref[...] = da_ref[...] + got_ref[turn].astype(F32).reshape(rows, wide)
    ig_ref[...] = da_ref[...].astype(BF16)

    while any(stage.values()):
        onward(1, 0, 2, 3)
    for turn in range(n_mp - 1):
        r_copy(turn, z, turn).wait_send()
    for to in others:
        d_copy(to, z).wait_send()
        sz_copy(to, z).wait_send()
        oz_copy(to, z).wait_send()
    for i in range(4):
        for place in range(depth):
            rs_copy(i, place).wait_send()
            ag_copy(i, place).wait_send()
    for a in range(2):
        ends(lambda ahead, sem: hop(a, z, ahead, sem).wait_send())

        def gone(block, ahead, more):
            @pl.when(more)
            def _():
                hop(a, block, ahead, block).wait_send()

        for step in range(1, n_mp):
            on_step(step, gone)


def finish_kernel(
    lo_hbm, ig_hbm, sp_hbm, st_hbm, u_hbm, d_hbm, q_hbm, o_hbm,
    lo_ref, ig_ref, gq_ref, bq_ref, bv_ref, go_ref, bo_ref, ga_ref, na_ref, gu_ref, bu_ref, gd_ref, bd_ref, gf_ref, nf_ref,
    tp_ref, tx_ref, ty_ref,
    u32, d32, q32, sp_ref, st_ref, u_ref, d_ref, q_ref, o_ref, sem, in_sem,
):
    pairs = ((u_hbm, u_ref), (d_hbm, d_ref), (q_hbm, q_ref), (o_hbm, o_ref), (sp_hbm, sp_ref), (st_hbm, st_ref), (lo_hbm, lo_ref), (ig_hbm, ig_ref))
    loads = [pltpu.make_async_copy(src, dst, in_sem.at[i]) for i, (src, dst) in enumerate(pairs)]
    for copy in loads:
        copy.start()
    loads[0].wait()
    wide = sp_ref.shape[1]
    width = bq_ref.shape[0]
    heads = width // HEAD_DIM
    per = width // SLICES
    u32[...] = u_ref[...].astype(F32)
    cu = pltpu.make_async_copy(u32, gu_ref, sem.at[0])
    cu.start()
    loads[1].wait()
    d32[...] = d_ref[...].astype(F32)
    cd = pltpu.make_async_copy(d32, gd_ref, sem.at[1])
    cd.start()
    loads[2].wait()
    for c in range(3):
        q32[c] = q_ref[:, c * per : (c + 1) * per, :].astype(F32).reshape(width, wide)
    cq = pltpu.make_async_copy(q32, gq_ref, sem.at[2])
    cq.start()
    for copy in loads[3:]:
        copy.wait()
    go_ref[...] = o_ref[...].astype(F32).reshape(width, wide)
    for row, ref in enumerate((gf_ref, nf_ref, bd_ref, ga_ref, na_ref, bo_ref)):
        ref[...] = sp_ref[row : row + 1, :].reshape(wide)
    bu_ref[...] = sp_ref[8:9, :].reshape(wide)
    bq_ref[...] = sp_ref[9:10, 0:width].reshape(width)
    bv_ref[...] = sp_ref[10:11, 0:width].reshape(width)
    table = st_ref[...]
    turned = table.T
    bins = tp_ref.shape[1]
    tp_ref[...] = turned[2 * LO : 2 * LO + heads, 0:bins]
    for t, ref in enumerate((tx_ref, ty_ref)):
        for h in range(heads):
            ref[h : h + 1, :] = jnp.concatenate(
                [table[a * heads + h : a * heads + h + 1, t * LO : (t + 1) * LO] for a in range(HI)], axis=1
            )
    for copy in (cu, cd, cq):
        copy.wait()


def layer(n_mp, n_dp):
    chips, extra = plane_bits(n_dp)
    plans = [chips + [0], chips[::-1] + [0]]
    depth = len(plans[0])

    def on_device(
        hidden_in, text_lens, key_mask, bucket_x, bucket_y, w_qkv, b_q, b_v, w_out, b_out, g_attn, n_attn,
        w_up, b_up, w_down, b_down, g_ffn, n_ffn, t_pos, t_x, t_y, cotangent,
    ):
        rows, wide = hidden_in.shape
        slot = bucket_x.shape[1]
        width = w_qkv.shape[2]
        heads = width // HEAD_DIM
        units = w_up.shape[1]
        per_u, per_o = wide // SLICES, width // SLICES
        bins = t_pos.shape[1]
        sds = jax.ShapeDtypeStruct
        dma = pltpu.SemaphoreType.DMA
        vm = pltpu.VMEM
        more = max(1, len(extra))
        n_bits = depth + len(extra)
        slices = [w.reshape(SLICES, w.shape[0] // SLICES, w.shape[1]) for w in (w_out, w_up, w_down)]
        whole = [(SLICES, per_u, units), (SLICES, units // SLICES, wide), (SLICES, 3 * per_o, wide), (SLICES, per_o, wide)]
        got = whole[:3] + [(SLICES, n_mp * per_o, wide)]
        outs = pl.pallas_call(
            functools.partial(layer_kernel, n_mp, plans, extra),
            out_shape=[sds((rows, wide), BF16), sds((rows, wide), BF16), sds((16, wide), F32), sds((bins, TILE), F32)]
            + [sds(shape, BF16) for shape in whole],
            in_specs=[VMEM] * 16 + [pl.BlockSpec(memory_space=pltpu.SMEM)] + [ANY] * 5,
            out_specs=[VMEM] * 8,
            scratch_shapes=[
                vm((n_mp, rows, wide), BF16), vm((slot, width), BF16), vm((slot, width), BF16), vm((slot, width), BF16),
                vm((heads, slot, slot), BF16), vm((heads, slot, 1), F32), vm((n_mp, rows, width), BF16),
                vm((n_mp, 8, units), F32), vm((slot, slot), jnp.int32), vm((slot, slot), jnp.int32), vm((heads, slot, slot), F32),
                vm((heads, 5, TILE, TILE), F32),
            ] + [vm((n_mp,) + s.shape, BF16) for s in slices] + [
                vm((rows, wide), F32), vm((rows, wide), F32), vm((8, wide), F32), vm((n_mp, rows, width), BF16), vm((n_mp, rows, width), BF16),
                vm((width, slot), BF16), vm((width, slot), BF16), vm((slot, width), F32), vm((3, width, slot), BF16), vm((3, slot, width), BF16),
                vm((2, HI * heads * GROUP, LO * GROUP), F32), vm((n_mp - 1,) + slices[0].shape, BF16), vm((n_mp, rows, wide), BF16), vm((n_mp, rows, wide), BF16),
                vm((16, wide), F32), vm((bins, TILE), F32), vm((n_bits, 16, wide), F32), vm((n_bits, bins, TILE), F32), vm((n_mp, 8, wide), F32),
                vm((SLICES, 3 * per_o, wide), F32), vm((SLICES, n_mp * per_o, wide), F32), vm((SLICES, 3 * per_o, wide), BF16),
            ] + [vm(shape, BF16) for shape in got] + [vm((n_mp, per_o, wide), BF16)] * 2 + [vm((more,) + shape[1:], BF16) for shape in got] + [
                dma((3,)), dma((2, slot // TILE)), dma((n_mp + 1,)), dma((n_mp,)), dma((n_mp - 1,)), dma((n_mp,)), dma((n_mp,)), dma((n_mp,)),
                dma((3, n_mp + 1)), dma((3, n_mp)), dma((3, depth, n_mp)), dma((3, depth, n_mp)),
                dma((n_mp,)), dma((n_mp,)), dma((n_mp - 1,)), dma((n_mp - 1,)), dma((2, n_mp + 1)), dma((2, n_mp)),
                dma((4, depth)), dma((4, depth)), dma((4, depth)), dma((4, depth)), dma((4, more)), dma((4, more)), dma((n_mp,)), dma((n_mp,)),
                dma((2, n_bits)), dma((2, n_bits)), dma((n_mp,)), dma((n_mp,)),
            ],
            compiler_params=pltpu.CompilerParams(collective_id=0, has_side_effects=True, vmem_limit_bytes=62 << 20),
            name="layer",
        )(
            hidden_in, jnp.transpose(w_qkv, (0, 2, 1)), b_q, b_v, t_x, t_y, t_pos, key_mask, b_up, b_out, g_attn, n_attn, b_down, g_ffn,
            n_ffn, cotangent, text_lens, bucket_x[0], bucket_y[0], *slices,
        )
        vec = lambda like: sds(like.shape, F32)
        final = pl.pallas_call(
            finish_kernel,
            out_shape=[
                sds((rows, wide), BF16), sds((rows, wide), BF16), sds((3, width, wide), F32), vec(b_q), vec(b_v), vec(w_out), vec(b_out),
                vec(g_attn), vec(n_attn), sds((SLICES, per_u, units), F32), vec(b_up), sds((SLICES, units // SLICES, wide), F32), vec(b_down),
                vec(g_ffn), vec(n_ffn), vec(t_pos), vec(t_x), vec(t_y),
            ],
            in_specs=[ANY] * 8,
            out_specs=[VMEM] * 2 + [ANY] + [VMEM] * 6 + [ANY] + [VMEM] + [ANY] + [VMEM] * 6,
            scratch_shapes=[
                vm((SLICES, per_u, units), F32), vm((SLICES, units // SLICES, wide), F32), vm((3, width, wide), F32),
                vm((16, wide), F32), vm((bins, TILE), F32),
            ] + [vm(shape, BF16) for shape in whole] + [dma((3,)), dma((8,))],
            compiler_params=pltpu.CompilerParams(vmem_limit_bytes=62 << 20),
            name="finish",
        )(*outs)
        final = list(final)
        final[2] = jnp.transpose(final[2], (0, 2, 1))
        final[9] = final[9].reshape(w_up.shape)
        final[11] = final[11].reshape(w_down.shape)
        return tuple(final)

    return on_device


def solution(mesh):
    both, split = P(("dp", "mp"), None), P("mp")
    rows_mp, cols_mp, qkv = P("mp", None), P(None, "mp"), P(None, None, "mp")
    doc = P("dp", None, None)
    return jax.shard_map(
        layer(mesh.shape["mp"], mesh.shape["dp"]),
        mesh=mesh,
        in_specs=(
            both, P("dp"), P("dp"), doc, doc, qkv, split, split, rows_mp, P(), P(), P(), cols_mp, split, rows_mp, P(), P(), P(),
            rows_mp, rows_mp, rows_mp, both,
        ),
        out_specs=(
            both, both, qkv, split, split, rows_mp, P(), P(), P(), cols_mp, split, rows_mp, P(), P(), P(), rows_mp, rows_mp, rows_mp,
        ),
        check_vma=False,
    )
```
